128 devices in a mesh: gx: 32 (over x, z_lo, y), gy: 4 (over z_hi, core).
Axes of the slice: x: 4, y: 4, z: 4 (z_hi: 2, z_lo: 2; z = z_hi * 2 + z_lo), core: 2. Of those that a mesh axis runs over, the one named last changes fastest.
Arguments:
- particles: bfloat16 [65536, 128], P(('gx', 'gy')), may hold values from -6 to 6
- send_counts: int32 [128, 128], P(('gx', 'gy')), may hold values from 0 to 8, as said below
- cell_lists: int32 [128, 1024], P(('gx', 'gy')), may hold values from 0 to 4095
- base_field: bfloat16 [64, 32, 64, 256], P(None, 'gx', 'gy'), may hold values from -6 to 6
- proj_weight: bfloat16 [128, 64], replicated, may hold values from -0.5 to 0.5
- conv_weight: bfloat16 [27, 64, 64], replicated, may hold values from -0.15625 to 0.15625
- cotangent: bfloat16 [64, 32, 64, 256], P(None, 'gx', 'gy'), may hold values from -6 to 6
Outputs:
- out_field: bfloat16 [64, 32, 64, 256], P(None, 'gx', 'gy')
- row_grads: float32 [65536, 128], P(('gx', 'gy'))
- conv_grad: float32 [27, 64, 64], replicated
- proj_grad: float32 [128, 64], replicated
The draws below stay inside these ranges and needn't reach their ends.
Inputs may be any that keep to these rules, and one draw needn't show every extreme that they name: `send_counts`: row s holds how many of source s's 512 rows go to each owner; each row sums to 512; source s's particle rows are listed grouped by owner in increasing order; at most 8 from one source to one owner, and some owner receives 8 from every source. `cell_lists`: entry s * 8 + r of owner d's row is the local cell of the r-th row that source s sends to d; entries of unused slots are ignored.
All inputs are finite; a program needn't handle non-finite values.
Results may differ from the reference program's by a relative error of at most 0.0041.
Values may be sent and summed in bfloat16 or wider, within the bound.
A program may use at most 64 MiB of HBM per device.

```python
import jax
import jax.numpy as jnp
from jax import lax

C = 64
F = 128
CX = 1
CY = 16
NZ = 256
CAP = 8
NDEV = 128
P_SIZE = 512
CELLS = 4096
NX = 32
NY = 64
N_GY = 4


def draw_send_counts(key, part):
    half = CAP // 2
    key_perm, key_shift = jax.random.split(key)
    order = jax.random.permutation(key_perm, NDEV).astype(jnp.int32)
    shifts = jax.random.randint(key_shift, (NDEV, NDEV // 2), 0, half + 1).astype(jnp.int32)
    shifts = shifts.at[:, 0].set(half)
    counts = jnp.zeros((NDEV, NDEV), jnp.int32)
    counts = counts.at[:, order[0::2]].set(half + shifts)
    counts = counts.at[:, order[1::2]].set(half - shifts)
    return counts


def set_ends(array, own_key, least, largest):
    longest = array.shape.index(max(array.shape))
    spots = []
    for shift in (0, 1):
        where = [jax.random.randint(jax.random.fold_in(own_key, axis), (), 0, length) for axis, length in enumerate(array.shape)]
        where[longest] = (where[longest] + shift) % array.shape[longest]
        spots.append(tuple(where))
    return array.at[spots[0]].set(least).at[spots[1]].set(largest)


def steps_of(key, shape, pieces, smallest, high):
    factor_of = 1.0
    for dim, blocks in pieces:
        heights = jax.random.uniform(jax.random.fold_in(jax.random.fold_in(key, 6), dim), (blocks,), jnp.float32, smallest / len(pieces), high / len(pieces))
        factor_of = factor_of * jnp.repeat(jnp.exp(heights), shape[dim] // blocks).reshape((-1,) + (1,) * (len(shape) - 1 - dim))
    return factor_of


def gaussian(rng, extent, spread, bound, shards=(), held_as=jnp.bfloat16):
    array = spread * jax.random.normal(rng, extent, jnp.float32)
    if shards:
        array = array * steps_of(rng, extent, shards, -0.22, 0.18)
    return jnp.clip(array, -bound, bound).astype(held_as)


def setup_inputs(seed: int = 0) -> dict:
    key_list = jax.random.split(jax.random.key(seed), 8)
    particles = gaussian(key_list[0], (NDEV * P_SIZE, F), 1.0, 6.0, ((0, 128),))
    send_counts = draw_send_counts(jax.random.fold_in(key_list[7], 71), 0)
    cell_lists = set_ends(jax.random.randint(key_list[2], (NDEV, NDEV * CAP), 0, CELLS), jax.random.fold_in(key_list[2], 1), 0, CELLS - 1).astype(jnp.int32)
    base_field = gaussian(key_list[3], (C, NX, NY, NZ), 1.0, 6.0, ((1, 32), (2, 4)))
    proj_weight = gaussian(key_list[4], (F, C), F ** -0.5, 0.5)
    conv_weight = gaussian(key_list[5], (27, C, C), (27 * C) ** -0.5, 0.15625)
    cotangent = gaussian(key_list[6], (C, NX, NY, NZ), 1.0, 6.0, ((1, 32), (2, 4)))
    return dict(particles=particles, send_counts=send_counts, cell_lists=cell_lists, base_field=base_field, proj_weight=proj_weight, conv_weight=conv_weight, cotangent=cotangent)


def pack(rows, counts):
    offsets = jnp.cumsum(counts).astype(jnp.int32) - counts
    slots = jnp.arange(CAP, dtype=jnp.int32)
    index = offsets[:, None] + slots[None, :]
    valid = slots[None, :] < counts[:, None]
    picked = jnp.take(rows, jnp.clip(index, 0, P_SIZE - 1).reshape(-1), axis=0)
    outgoing = jnp.where(valid.reshape(-1, 1), picked, jnp.zeros_like(picked))
    places = jnp.arange(P_SIZE, dtype=jnp.int32)
    ends = offsets + counts
    owner = lax.optimization_barrier(jnp.sum((ends[None, :] <= places[:, None]).astype(jnp.int32), axis=1)).astype(jnp.int32)
    slot_of = owner * CAP + places - jnp.take(offsets, owner)
    return (outgoing, slot_of.astype(jnp.int32))

def taps():
    return [(dx, dy, dz) for dx in (-1, 0, 1) for dy in (-1, 0, 1) for dz in (-1, 0, 1)]

def reference(particles, send_counts, cell_lists, base_field, proj_weight, conv_weight, cotangent):
    parts = particles.reshape(NDEV, P_SIZE, F)
    outgoing, slot_of = jax.vmap(pack)(parts, send_counts)
    recv = outgoing.reshape(NDEV, NDEV, CAP, F).transpose(1, 0, 2, 3).reshape(NDEV * NDEV * CAP, F)
    projected = jnp.dot(recv, proj_weight, preferred_element_type=jnp.float32).astype(jnp.bfloat16)
    owner = jnp.arange(NDEV, dtype=jnp.int32)
    gxi = (owner // N_GY)[:, None]
    gyi = (owner % N_GY)[:, None]
    cxl = cell_lists // (CY * NZ)
    cyl = cell_lists // NZ % CY
    czl = cell_lists % NZ
    gidx = (((gxi * CX + cxl) * NY + gyi * CY + cyl) * NZ + czl).astype(jnp.int32).reshape(-1)
    painted = jnp.zeros((NX * NY * NZ, C), jnp.float32).at[gidx].add(projected.astype(jnp.float32))
    painted = painted.T.reshape(C, NX, NY, NZ)
    field = (base_field.astype(jnp.float32) + painted).astype(jnp.bfloat16)
    pre = jnp.zeros((C, NX * NY * NZ), jnp.float32)
    for k, (dx, dy, dz) in enumerate(taps()):
        moved = jnp.roll(field, (-dx, -dy, -dz), axis=(1, 2, 3)).reshape(C, -1)
        pre = pre + jnp.dot(conv_weight[k], moved, preferred_element_type=jnp.float32)
    pre = pre.reshape(C, NX, NY, NZ)
    sig = jax.nn.sigmoid(pre)
    out_field = (field.astype(jnp.float32) + pre * sig).astype(jnp.bfloat16)
    pre_grad = (cotangent.astype(jnp.float32) * sig * (1.0 + pre * (1.0 - sig))).astype(jnp.bfloat16)
    field_grad = cotangent.astype(jnp.float32).reshape(C, -1)
    flat_grad = pre_grad.reshape(C, -1)
    tap_grads = []
    for k, (dx, dy, dz) in enumerate(taps()):
        back = jnp.roll(pre_grad, (dx, dy, dz), axis=(1, 2, 3)).reshape(C, -1)
        field_grad = field_grad + jnp.dot(conv_weight[k].T, back, preferred_element_type=jnp.float32)
        moved = jnp.roll(field, (-dx, -dy, -dz), axis=(1, 2, 3)).reshape(C, -1)
        tap_grads.append(lax.dot_general(flat_grad, moved, (((1,), (1,)), ((), ())), preferred_element_type=jnp.float32))
    conv_grad = jnp.stack(tap_grads) / jnp.sqrt(jnp.float32(NX * NY * NZ))
    slot_grad = jnp.take(field_grad, gidx, axis=1).T.astype(jnp.bfloat16)
    grad_slots = jnp.dot(slot_grad, proj_weight.T, preferred_element_type=jnp.float32)
    grad_slots = grad_slots.reshape(NDEV, NDEV, CAP, F).transpose(1, 0, 2, 3).reshape(NDEV, NDEV * CAP, F)
    proj_grad = jnp.dot(recv.T, slot_grad, preferred_element_type=jnp.float32)
    proj_grad = proj_grad / jnp.sqrt(jnp.float32(NDEV * P_SIZE))
    row_grads = jax.vmap(lambda grads, slot: jnp.take(grads, slot, axis=0))(grad_slots, slot_of).reshape(NDEV * P_SIZE, F)
    return (out_field, row_grads, conv_grad, proj_grad)
```

```python
import functools
import math

import jax
import jax.numpy as jnp
from jax import lax
from jax.experimental import pallas as pl
from jax.experimental.pallas import tpu as pltpu
from jax.sharding import PartitionSpec as P

MESH = pl.DeviceIdType.MESH
F32 = jnp.float32
BF16 = jnp.bfloat16

F_CHUNKS = ((0, 4), (12, 4), (4, 4), (8, 4))
F_ROWS = ((0, 3), (13, 3), (3, 4), (7, 6))
G_ROWS = ((0, 2), (14, 2), (2, 4), (6, 8))
N_TAPS = 9


def nt_dot(a, b):
    return lax.dot_general(a, b, (((1,), (1,)), ((), ())), preferred_element_type=F32)


def roll_z(x, shift):
    return pltpu.roll(x, shift % x.shape[1], 1)


def kernel(
    ngx,
    ngy,
    counts_ref,
    cells_ref,
    rows_ref,
    base_ref,
    cot_ref,
    wf_ref,
    wb_ref,
    wp_ref,
    wpt_ref,
    out_ref,
    rowg_ref,
    convg_ref,
    projg_ref,
    send,
    arr,
    onehot_t,
    paint_a,
    paint_b,
    fld,
    pgr,
    fg,
    sgt,
    acc,
    tiles,
    rs,
    ag,
    sgs,
    sgr,
    a2a_sem,
    rev_sem,
    rs_sem,
    ag_sem,
    fx_send,
    fx_recv,
    fy_send,
    fy_recv,
    gx_send,
    gx_recv,
    gy_send,
    gy_recv,
):
    n = ngx * ngy
    nrows, feats = rows_ref.shape
    cy, chans, nz = base_ref.shape
    nslots = cells_ref.shape[1]
    cap = nslots // n
    ntile = tiles.shape[0] * tiles.shape[1]
    per = tiles.shape[1]
    nconv = 120 // per
    gi = lax.axis_index("gx")
    gj = lax.axis_index("gy")
    me = gi * ngy + gj

    def coords(d):
        return (lax.div(d, ngy), lax.rem(d, ngy))

    def peer_of(k):
        return lax.rem(me + k, n)

    barrier = pltpu.get_barrier_semaphore()

    @pl.loop(1, n)
    def _(k):
        pl.semaphore_signal(barrier, inc=1, device_id=coords(peer_of(k)), device_id_type=MESH)

    counts = counts_ref[...].astype(F32)
    lane = lax.broadcasted_iota(jnp.int32, (nslots, n), 1)
    slot = lax.broadcasted_iota(jnp.int32, (nslots, n), 0)
    owner = lax.div(slot, cap)
    offs = jnp.sum(jnp.where(lane < owner, counts, 0.0), axis=1, keepdims=True)
    mine = jnp.sum(jnp.where(lane == owner, counts, 0.0), axis=1, keepdims=True)
    place = (slot - owner * cap)[:, :1]
    index = jnp.where(place < mine.astype(jnp.int32), offs.astype(jnp.int32) + place, -1)
    pick = lax.broadcasted_iota(jnp.int32, (nslots, nrows), 1) == index
    outgoing = jnp.dot(pick.astype(F32).astype(BF16), rows_ref[...], preferred_element_type=F32)
    send[...] = outgoing.astype(BF16).reshape(send.shape)

    pl.semaphore_wait(barrier, n - 1)

    def spread(src, dst, sems):
        @pl.loop(1, n)
        def _(k):
            peer = peer_of(k)
            pltpu.make_async_remote_copy(
                src_ref=src.at[peer],
                dst_ref=dst.at[me],
                send_sem=sems.at[0],
                recv_sem=sems.at[1],
                device_id=coords(peer),
                device_id_type=MESH,
            ).start()

        dst[pl.ds(me, 1)] = src[pl.ds(me, 1)]

    def waits(src, dst, sems, count):
        return pltpu.make_async_remote_copy(
            src_ref=src.at[pl.ds(0, count)],
            dst_ref=dst.at[pl.ds(0, count)],
            send_sem=sems.at[0],
            recv_sem=sems.at[1],
            device_id=coords(peer_of(1)),
            device_id_type=MESH,
        )

    spread(send, arr, a2a_sem)

    counts_b = jnp.broadcast_to(counts, (8, n)).astype(BF16)
    upper = lax.broadcasted_iota(jnp.int32, (n, n), 0) <= lax.broadcasted_iota(jnp.int32, (n, n), 1)
    ends = jnp.dot(counts_b, upper.astype(F32).astype(BF16), preferred_element_type=F32)[:1]
    places = lax.broadcasted_iota(jnp.int32, (nrows, n), 0)
    below = ends <= places.astype(F32)
    owner_of = jnp.sum(jnp.where(below, 1.0, 0.0), axis=1, keepdims=True)
    start_of = jnp.max(jnp.where(below, ends, 0.0), axis=1, keepdims=True)
    slot_of = (owner_of * cap - start_of).astype(jnp.int32) + places[:, :1]
    hit = lax.broadcasted_iota(jnp.int32, (nrows, nslots), 1) == slot_of
    onehot_t[...] = hit.astype(F32).astype(BF16)
    cell_y = lax.div(cells_ref[...], nz)
    cell_z = lax.rem(cells_ref[...], nz)
    at_z = lax.broadcasted_iota(jnp.int32, (nz, nslots), 0) == cell_z
    paint_b[...] = at_z.astype(F32).astype(BF16)
    acc[...] = jnp.zeros_like(acc)
    sgt[...] = jnp.zeros_like(sgt)

    waits(send, arr, a2a_sem, n - 1).wait_recv()

    arrived = arr[...].reshape(nslots, feats)
    projected = lax.dot_general(
        wp_ref[...], arrived, (((0,), (1,)), ((), ())), preferred_element_type=F32
    )
    projected = projected.astype(BF16).astype(F32)
    for y in range(cy):
        paint_a[y] = jnp.where(cell_y == y, projected, 0.0).astype(BF16)

    def edge_copy(buf, row, side, b, send_sems, recv_sems):
        to_y = lax.rem(gj + (1 if side == 0 else ngy - 1), ngy)
        to_x = lax.rem(gi + b + ngx, ngx)
        return pltpu.make_async_remote_copy(
            src_ref=buf.at[row, 1],
            dst_ref=buf.at[0 if side == 0 else cy + 1, 1 - b],
            send_sem=send_sems.at[side, 1 - b],
            recv_sem=recv_sems.at[side, 1 - b],
            device_id=(to_x, to_y),
            device_id_type=MESH,
        )

    def plane_copy(buf, c, first, count, b, send_sems, recv_sems):
        to_x = lax.rem(gi + b + ngx, ngx)
        rows = pl.ds(first + 1, count)
        return pltpu.make_async_remote_copy(
            src_ref=buf.at[rows, 1],
            dst_ref=buf.at[rows, 1 - b],
            send_sem=send_sems.at[c, (1 - b) // 2],
            recv_sem=recv_sems.at[c, (1 - b) // 2],
            device_id=(to_x, gj),
            device_id_type=MESH,
        )

    f_planes = [
        [plane_copy(fld, c, first, count, b, fx_send, fx_recv) for b in (-1, 1)]
        for c, (first, count) in enumerate(F_CHUNKS)
    ]
    g_planes = [
        [plane_copy(pgr, c, first, count, b, gx_send, gx_recv) for b in (-1, 1)]
        for c, (first, count) in enumerate(F_ROWS)
    ]
    f_edges = [
        [edge_copy(fld, row, side, b, fy_send, fy_recv) for b in (-1, 0, 1)]
        for side, row in ((0, cy), (1, 1))
    ]
    g_edges = [
        [edge_copy(pgr, row, side, b, gy_send, gy_recv) for b in (-1, 0, 1)]
        for side, row in ((0, cy), (1, 1))
    ]

    for c, (first, count) in enumerate(F_CHUNKS):
        rows = slice(first, first + count)
        painted = nt_dot(paint_a[rows].reshape(count * chans, nslots), paint_b[...])
        painted = painted.reshape(count, chans, nz)
        fld[first + 1 : first + count + 1, 1] = (base_ref[rows].astype(F32) + painted).astype(BF16)
        if first == 0:
            for copy in f_edges[1]:
                copy.start()
        if first + count == cy:
            for copy in f_edges[0]:
                copy.start()
        for copy in f_planes[c]:
            copy.start()

    def forward_row(y, _):
        slab = fld[pl.ds(y, 3)].reshape(N_TAPS * chans, nz)
        part = jnp.dot(wf_ref[...], slab, preferred_element_type=F32)
        pre = roll_z(part[:chans], 1) + part[chans : 2 * chans] + roll_z(part[2 * chans :], -1)
        sig = jax.nn.sigmoid(pre)
        out_ref[y] = (fld[y + 1, 1].astype(F32) + pre * sig).astype(BF16)
        grad = cot_ref[y].astype(F32) * sig * (1.0 + pre * (1.0 - sig))
        grad = grad.astype(BF16)
        pgr[y + 1, 1] = grad
        wide = grad.astype(F32)
        three = jnp.concatenate([roll_z(wide, -1), wide, roll_z(wide, 1)], axis=0)
        acc[:, : N_TAPS * chans] += nt_dot(three.astype(BF16), slab)
        return 0

    for c, (first, count) in enumerate(F_ROWS):
        for copy in f_planes[c]:
            copy.wait_recv()
        if c < 2:
            for copy in f_edges[c]:
                copy.wait_recv()
        lax.fori_loop(first, first + count, forward_row, 0)
        if first == 0:
            for copy in g_edges[1]:
                copy.start()
        if first + count == cy:
            for copy in g_edges[0]:
                copy.start()
        for copy in g_planes[c]:
            copy.start()

    per_row = acc.shape[1] // 128
    for t in range(120):
        r, q = divmod(t, per_row)
        tiles[t // per, t % per] = acc[8 * r : 8 * r + 8, 128 * q : 128 * q + 128]

    def scatter(lo, hi, s):
        @pl.loop(1, n)
        def _(k):
            peer = peer_of(k)

            @pl.when((peer >= lo) & (peer < hi))
            def _():
                pltpu.make_async_remote_copy(
                    src_ref=tiles.at[peer],
                    dst_ref=rs.at[me],
                    send_sem=rs_sem.at[s, 0],
                    recv_sem=rs_sem.at[s, 1],
                    device_id=coords(peer),
                    device_id_type=MESH,
                ).start()

    def reduce_gather(lo, hi, s):
        @pl.when((me >= lo) & (me < hi))
        def _():
            waits(tiles, rs, rs_sem.at[s], n - 1).wait_recv()
            rs[pl.ds(me, 1)] = tiles[pl.ds(me, 1)]
            ag[pl.ds(me, 1)] = jnp.sum(rs[...], axis=0, keepdims=True)

            @pl.loop(1, n)
            def _(k):
                pltpu.make_async_remote_copy(
                    src_ref=ag.at[me],
                    dst_ref=ag.at[me],
                    send_sem=ag_sem.at[s, 0],
                    recv_sem=ag_sem.at[s, 1],
                    device_id=coords(peer_of(k)),
                    device_id_type=MESH,
                ).start()

    def finish(lo, hi, s):
        own = (me >= lo) & (me < hi)

        @pl.when(own)
        def _():
            waits(tiles, rs, ag_sem.at[s], n - 1).wait_send()
            if hi - lo > 1:
                waits(tiles, ag, rs_sem.at[s], hi - lo - 1).wait_send()
                waits(tiles, ag, ag_sem.at[s], hi - lo - 1).wait_recv()

        @pl.when(jnp.logical_not(own))
        def _():
            waits(tiles, ag, rs_sem.at[s], hi - lo).wait_send()
            waits(tiles, ag, ag_sem.at[s], hi - lo).wait_recv()

    scatter(0, nconv, 0)

    def backward_row(y, _):
        slab = pgr[pl.ds(y, 3)].reshape(N_TAPS * chans, nz)
        part = jnp.dot(wb_ref[...], slab, preferred_element_type=F32)
        got = roll_z(part[:chans], 1) + part[chans : 2 * chans] + roll_z(part[2 * chans :], -1)
        fg[y] = (cot_ref[y].astype(F32) + got).astype(BF16)
        return 0

    for c, (first, count) in enumerate(G_ROWS):
        for copy in g_planes[c]:
            copy.wait_recv()
        if c < 2:
            for copy in g_edges[c]:
                copy.wait_recv()
        lax.fori_loop(first, first + count, backward_row, 0)
        rows = fg[first : first + count].reshape(count * chans, nz)
        at_slots = jnp.dot(rows, paint_b[...], preferred_element_type=F32)
        total = sgt[:chans]
        for y in range(count):
            part = at_slots[y * chans : (y + 1) * chans]
            total = total + jnp.where(cell_y == first + y, part, 0.0)
        sgt[:chans] = total

    sgs[...] = sgt[...].T.astype(BF16).reshape(sgs.shape)
    spread(sgs, sgr, rev_sem)
    proj_part = jnp.dot(sgt[:chans].astype(BF16), arrived, preferred_element_type=F32)
    for r in range(chans // 8):
        t = 120 + r
        tiles[t // per, t % per] = proj_part[8 * r : 8 * r + 8]
    scatter(nconv, n, 1)
    reduce_gather(0, nconv, 0)
    waits(sgs, sgr, rev_sem, n - 1).wait_recv()
    back = sgr[...].reshape(nslots, feats)
    row_slot_grads = jnp.dot(onehot_t[...], back, preferred_element_type=F32).astype(BF16)
    rowg_ref[...] = jnp.dot(row_slot_grads, wpt_ref[...], preferred_element_type=F32)
    reduce_gather(nconv, n, 1)
    finish(0, nconv, 0)
    for t in range(120):
        r, q = divmod(t, per_row)
        acc[8 * r : 8 * r + 8, 128 * q : 128 * q + 128] = ag[t // per, t % per]
    conv_scale = 1.0 / math.sqrt(cy * nz * n)
    for x in range(3):
        for y in range(3):
            for z in range(3):
                at = (y * 3 + x) * chans
                block = acc[z * chans : (z + 1) * chans, at : at + chans]
                convg_ref[x * 9 + y * 3 + z] = block * conv_scale
    finish(nconv, n, 1)
    proj_scale = 1.0 / math.sqrt(nrows * n)
    for r in range(chans // 8):
        t = 120 + r
        projg_ref[8 * r : 8 * r + 8] = ag[t // per, t % per] * proj_scale

    waits(send, arr, a2a_sem, n - 1).wait_send()
    waits(sgs, sgr, rev_sem, n - 1).wait_send()
    for group in (f_planes, g_planes, f_edges, g_edges):
        for copies in group:
            for copy in copies:
                copy.wait_send()


def local(ngx, ngy, particles, send_counts, cell_lists, base_field, proj_weight, conv_weight, cotangent):
    n = ngx * ngy
    nrows, feats = particles.shape
    chans, _, cy, nz = base_field.shape
    nslots = cell_lists.shape[1]
    base = base_field.reshape(chans, cy, nz).transpose(1, 0, 2)
    cot = cotangent.reshape(chans, cy, nz).transpose(1, 0, 2)
    taps = conv_weight.reshape(3, 3, 3, chans, chans)
    wf = taps.transpose(2, 3, 1, 0, 4).reshape(3 * chans, N_TAPS * chans)
    wb = taps[::-1, ::-1, ::-1].transpose(2, 4, 1, 0, 3).reshape(3 * chans, N_TAPS * chans)
    wpt = jnp.pad(proj_weight.T, ((0, feats - chans), (0, 0)))
    per = 128 // n
    dma = pltpu.SemaphoreType.DMA
    vmem = pl.BlockSpec(memory_space=pltpu.VMEM)
    out, rowg, convg, projg = pl.pallas_call(
        functools.partial(kernel, ngx, ngy),
        out_shape=(
            jax.ShapeDtypeStruct((cy, chans, nz), BF16),
            jax.ShapeDtypeStruct((nrows, feats), F32),
            jax.ShapeDtypeStruct((27, chans, chans), F32),
            jax.ShapeDtypeStruct((chans, feats), F32),
        ),
        in_specs=[vmem] * 9,
        out_specs=[vmem] * 4,
        scratch_shapes=[
            pltpu.VMEM((n, nslots // n, feats), BF16),
            pltpu.VMEM((n, nslots // n, feats), BF16),
            pltpu.VMEM((nrows, nslots), BF16),
            pltpu.VMEM((cy, chans, nslots), BF16),
            pltpu.VMEM((nz, nslots), BF16),
            pltpu.VMEM((cy + 2, 3, chans, nz), BF16),
            pltpu.VMEM((cy + 2, 3, chans, nz), BF16),
            pltpu.VMEM((cy, chans, nz), BF16),
            pltpu.VMEM((feats, nslots), F32),
            pltpu.VMEM((3 * chans, 640), F32),
            pltpu.VMEM((n, per, 8, 128), F32),
            pltpu.VMEM((n, per, 8, 128), F32),
            pltpu.VMEM((n, per, 8, 128), F32),
            pltpu.VMEM((n, nslots // n, feats), BF16),
            pltpu.VMEM((n, nslots // n, feats), BF16),
            dma((2,)),
            dma((2,)),
            dma((2, 2)),
            dma((2, 2)),
            dma((4, 2)),
            dma((4, 2)),
            dma((2, 3)),
            dma((2, 3)),
            dma((4, 2)),
            dma((4, 2)),
            dma((2, 3)),
            dma((2, 3)),
        ],
        compiler_params=pltpu.CompilerParams(
            collective_id=0, has_side_effects=True, vmem_limit_bytes=56 * 1024 * 1024
        ),
        name="section",
    )(send_counts, cell_lists, particles, base, cot, wf, wb, proj_weight, wpt)
    out_field = out.transpose(1, 0, 2).reshape(chans, 1, cy, nz)
    return out_field, rowg, convg, projg.T


def solution(mesh):
    in_specs = (
        P(("gx", "gy"), None),
        P(("gx", "gy"), None),
        P(("gx", "gy"), None),
        P(None, "gx", "gy", None),
        P(),
        P(),
        P(None, "gx", "gy", None),
    )
    out_specs = (P(None, "gx", "gy", None), P(("gx", "gy"), None), P(), P())
    body = functools.partial(local, mesh.shape["gx"], mesh.shape["gy"])
    return jax.shard_map(body, mesh=mesh, in_specs=in_specs, out_specs=out_specs, check_vma=False)
```

```python
import functools
import math

import jax
import jax.numpy as jnp
from jax import lax
from jax.experimental import pallas as pl
from jax.experimental.pallas import tpu as pltpu
from jax.sharding import PartitionSpec as P

MESH = pl.DeviceIdType.MESH
F32 = jnp.float32
BF16 = jnp.bfloat16

F_CHUNKS = ((0, 4), (12, 4), (4, 4), (8, 4))
F_ROWS = ((0, 3), (13, 3), (3, 4), (7, 6))
N_TAPS = 9


def nt_dot(a, b):
    return lax.dot_general(a, b, (((1,), (1,)), ((), ())), preferred_element_type=F32)


def roll_z(x, shift):
    return pltpu.roll(x, shift % x.shape[1], 1)


def kernel(
    ngx,
    ngy,
    counts_ref,
    cells_ref,
    rows_ref,
    base_ref,
    cot_ref,
    taps_ref,
    wpt_ref,
    out_ref,
    back_ref,
    sums_ref,
    psum_ref,
    send,
    arr,
    paint_a,
    paint_b,
    perm,
    perm_back,
    wf,
    wb,
    base,
    cot,
    outs,
    fld,
    pgr,
    grads,
    near_cells,
    near_out,
    near_in,
    acc,
    tiles,
    rs,
    ag,
    ptiles,
    prs,
    pag,
    sgs,
    sgr,
    a2a_sem,
    rev_sem,
    cell_sem,
    near_sem,
    rs_sem,
    ag_sem,
    prs_sem,
    pag_sem,
    fx_send,
    fx_recv,
    fy_send,
    fy_recv,
    gy_send,
    gy_recv,
):
    n = ngx * ngy
    nrows, feats = rows_ref.shape
    cy, chans, nz = base.shape
    nslots = cells_ref.shape[1]
    cap = nslots // n
    per = tiles.shape[1]
    nconv = 120 // per
    gi = lax.axis_index("gx")
    gj = lax.axis_index("gy")
    me = gi * ngy + gj

    def coords(d):
        return (lax.div(d, ngy), lax.rem(d, ngy))

    def peer_of(k):
        return lax.rem(me + k, n)

    def beside(b):
        return (lax.rem(gi + b + ngx, ngx), gj)

    barrier = pltpu.get_barrier_semaphore()

    @pl.loop(1, n)
    def _(k):
        pl.semaphore_signal(barrier, inc=1, device_id=coords(peer_of(k)), device_id_type=MESH)

    counts = counts_ref[...].astype(F32)
    lane = lax.broadcasted_iota(jnp.int32, (nslots, n), 1)
    slot = lax.broadcasted_iota(jnp.int32, (nslots, 1), 0)
    owner = slot // cap
    offs = jnp.sum(jnp.where(lane < owner, counts, 0.0), axis=1, keepdims=True)
    mine = jnp.sum(jnp.where(lane == owner, counts, 0.0), axis=1, keepdims=True)
    place = slot - owner * cap
    index = jnp.where(place < mine.astype(jnp.int32), offs.astype(jnp.int32) + place, -1)
    pick = lax.broadcasted_iota(jnp.int32, (nslots, nrows), 1) == index
    outgoing = jnp.dot(pick.astype(F32).astype(BF16), rows_ref[...], preferred_element_type=F32)
    send[...] = outgoing.astype(BF16).reshape(send.shape)

    pl.semaphore_wait(barrier, n - 1)

    def remote(src, dst, send_sem, recv_sem, device):
        return pltpu.make_async_remote_copy(
            src_ref=src,
            dst_ref=dst,
            send_sem=send_sem,
            recv_sem=recv_sem,
            device_id=device,
            device_id_type=MESH,
        )

    def spread(src, dst, sems):
        @pl.loop(1, n)
        def _(k):
            peer = peer_of(k)
            remote(src.at[peer], dst.at[me], sems.at[0], sems.at[1], coords(peer)).start()

        dst[pl.ds(me, 1)] = src[pl.ds(me, 1)]

    def waits(src, dst, sems, count):
        part = pl.ds(0, count)
        return remote(src.at[part], dst.at[part], sems.at[0], sems.at[1], coords(peer_of(1)))

    spread(send, arr, a2a_sem)
    cell_copies = [
        remote(
            cells_ref,
            near_cells.at[(1 - b) // 2],
            cell_sem.at[0, (1 - b) // 2],
            cell_sem.at[1, (1 - b) // 2],
            beside(b),
        )
        for b in (-1, 1)
    ]
    for copy in cell_copies:
        copy.start()

    def at_depth(cells):
        hit = lax.broadcasted_iota(jnp.int32, (nz, nslots), 0) == cells % nz
        return hit.astype(F32).astype(BF16)

    cell_y = cells_ref[...] // nz
    paint_b[0] = at_depth(cells_ref[...])
    full = cy * chans
    row = lax.broadcasted_iota(jnp.int32, (full, 1), 0)
    col = lax.broadcasted_iota(jnp.int32, (full, full), 1)
    perm[...] = (col == (row % chans) * cy + row // chans).astype(F32).astype(BF16)
    base[...] = (
        jnp.dot(perm[...], base_ref[...], preferred_element_type=F32).astype(BF16).reshape(base.shape)
    )
    cot[...] = (
        jnp.dot(perm[...], cot_ref[...], preferred_element_type=F32).astype(BF16).reshape(cot.shape)
    )
    for x in range(3):
        for y in range(3):
            for z in range(3):
                tap = taps_ref[x * 9 + y * 3 + z]
                at = (y * 3 + x) * chans
                wf[z * chans : (z + 1) * chans, at : at + chans] = tap
                at = (x * 3 + 2 - z) * chans
                side = (2 - y) * chans
                wb[at : at + chans, side : side + chans] = tap.astype(F32).T.astype(BF16)
    acc[...] = jnp.zeros_like(acc)

    waits(send, arr, a2a_sem, n - 1).wait_recv()

    arrived = arr[...].reshape(nslots, feats)
    projected = nt_dot(wpt_ref[...], arrived).astype(BF16).astype(F32)
    for y in range(cy):
        paint_a[y] = jnp.where(cell_y == y, projected, 0.0).astype(BF16)

    def edge_copy(side, b):
        to = (lax.rem(gi + b + ngx, ngx), lax.rem(gj + (1 if side == 0 else ngy - 1), ngy))
        row = cy if side == 0 else 1
        dst = 0 if side == 0 else cy + 1
        sem = (side, 1 - b)
        return remote(fld.at[row, 1], fld.at[dst, 1 - b], fy_send.at[sem], fy_recv.at[sem], to)

    def grad_edge(side):
        to = (gi, lax.rem(gj + (1 if side == 0 else ngy - 1), ngy))
        row = cy if side == 0 else 1
        dst = 0 if side == 0 else cy + 1
        return remote(pgr.at[row], pgr.at[dst], gy_send.at[side], gy_recv.at[side], to)

    def plane_copy(c, first, count, b):
        rows = pl.ds(first + 1, count)
        sem = (c, (1 - b) // 2)
        return remote(
            fld.at[rows, 1], fld.at[rows, 1 - b], fx_send.at[sem], fx_recv.at[sem], beside(b)
        )

    f_planes = [
        [plane_copy(c, first, count, b) for b in (-1, 1)]
        for c, (first, count) in enumerate(F_CHUNKS)
    ]
    f_edges = [[edge_copy(side, b) for b in (-1, 0, 1)] for side in (0, 1)]
    g_edges = [grad_edge(side) for side in (0, 1)]

    for c, (first, count) in enumerate(F_CHUNKS):
        rows = slice(first, first + count)
        painted = nt_dot(paint_a[rows].reshape(count * chans, nslots), paint_b[0])
        painted = painted.reshape(count, chans, nz)
        fld[first + 1 : first + count + 1, 1] = (base[rows].astype(F32) + painted).astype(BF16)
        if first == 0:
            for copy in f_edges[1]:
                copy.start()
        if first + count == cy:
            for copy in f_edges[0]:
                copy.start()
        if c < 2:
            for copy in f_planes[c]:
                copy.start()

    for copy in cell_copies:
        copy.wait()
    near_y = [near_cells[e] // nz for e in (0, 1)]
    for e in (0, 1):
        paint_b[1 + e] = at_depth(near_cells[e])

    for c, (first, count) in enumerate(F_ROWS):
        for copy in f_planes[c]:
            copy.wait()
        if c + 2 < len(F_CHUNKS):
            for copy in f_planes[c + 2]:
                copy.start()
        if c < 2:
            for copy in f_edges[c]:
                copy.wait_recv()
        slabs, threes = [], []
        for y in range(first, first + count):
            slab = fld[y : y + 3].reshape(N_TAPS * chans, nz)
            part = jnp.dot(wf[...], slab, preferred_element_type=F32)
            pre = roll_z(part[:chans], 1) + part[chans : 2 * chans] + roll_z(part[2 * chans :], -1)
            sig = jax.nn.sigmoid(pre)
            outs[y] = (fld[y + 1, 1].astype(F32) + pre * sig).astype(BF16)
            grad = (cot[y].astype(F32) * sig * (1.0 + pre * (1.0 - sig))).astype(BF16)
            pgr[y + 1] = grad
            wide = grad.astype(F32)
            three = jnp.concatenate([roll_z(wide, -1), wide, roll_z(wide, 1)], axis=0)
            slabs.append(slab)
            threes.append(three.astype(BF16))
        if c < 2:
            g_edges[1 - c].start()
        acc[:, : N_TAPS * chans] += nt_dot(
            jnp.concatenate(threes, axis=1), jnp.concatenate(slabs, axis=1)
        )

    per_row = acc.shape[1] // 128
    for t in range(120):
        r, q = divmod(t, per_row)
        tiles[t // per, t % per] = acc[8 * r : 8 * r + 8, 128 * q : 128 * q + 128]

    def scatter(src, dst, sems, count, step):
        @pl.loop(1, n)
        def _(k):
            peer = peer_of(k)
            share = lax.div(peer, step)

            @pl.when((share < count) & (share * step == peer))
            def _():
                remote(src.at[share], dst.at[me], sems.at[0], sems.at[1], coords(peer)).start()

    def mine_of(count, step):
        share = lax.div(me, step)
        return share, (share < count) & (share * step == me)

    def reduce_gather(src, part, dst, sems, gather_sems, count, step):
        share, own = mine_of(count, step)

        @pl.when(own)
        def _():
            waits(part, part, sems, n - 1).wait_recv()
            part[pl.ds(me, 1)] = src[pl.ds(share, 1)]
            dst[pl.ds(share, 1)] = jnp.sum(part[...], axis=0, keepdims=True)

            @pl.loop(1, n)
            def _(k):
                there = dst.at[share]
                remote(
                    there, there, gather_sems.at[0], gather_sems.at[1], coords(peer_of(k))
                ).start()

    def finish(part, dst, sems, gather_sems, count, step):
        _, own = mine_of(count, step)

        @pl.when(own)
        def _():
            waits(part, part, gather_sems, n - 1).wait_send()
            if count > 1:
                waits(dst, dst, sems, count - 1).wait_send()
                waits(dst, dst, gather_sems, count - 1).wait_recv()

        @pl.when(jnp.logical_not(own))
        def _():
            waits(dst, dst, sems, count).wait_send()
            waits(dst, dst, gather_sems, count).wait_recv()

    scatter(tiles, rs, rs_sem, nconv, 1)

    for c, (first, count) in enumerate(((1, cy - 2), (0, 1), (cy - 1, 1))):
        if c == 1:
            for copy in g_edges:
                copy.wait_recv()
        for y in range(first, first + count):
            slab = pgr[y : y + 3].reshape(3 * chans, nz)
            part = jnp.dot(wb[...], slab, preferred_element_type=F32)
            for x in range(3):
                p = part[3 * x * chans : 3 * (x + 1) * chans]
                got = roll_z(p[:chans], 1) + p[chans : 2 * chans] + roll_z(p[2 * chans :], -1)
                if x == 1:
                    got = got + cot[y].astype(F32)
                    high = got.astype(BF16)
                    grads[3, y] = (got - high.astype(F32)).astype(BF16)
                    grads[1, y] = high
                else:
                    grads[x, y] = got.astype(BF16)

    def at_slots(which, depth, ys, total):
        step = 4
        for first in range(0, cy, step):
            rows = grads[which, first : first + step].reshape(step * chans, nz)
            got = jnp.dot(rows, paint_b[depth], preferred_element_type=F32)
            for y in range(step):
                part = got[y * chans : (y + 1) * chans]
                total = total + jnp.where(ys == first + y, part, 0.0)
        return total

    zero = jnp.zeros((chans, nslots), F32)
    near_copies = []
    for e, b in ((0, -1), (1, 1)):
        near_out[e] = at_slots(1 + b, 1 + e, near_y[e], zero).astype(BF16)
        copy = remote(
            near_out.at[e], near_in.at[1 - e], near_sem.at[0, e], near_sem.at[1, 1 - e], beside(b)
        )
        copy.start()
        near_copies.append(copy)
    slot_grad = at_slots(1, 0, cell_y, at_slots(3, 0, cell_y, zero))
    reduce_gather(tiles, rs, ag, rs_sem, ag_sem, nconv, 1)
    for copy in near_copies:
        copy.wait()
    slot_grad = slot_grad + near_in[0].astype(F32) + near_in[1].astype(F32)

    slot_grad = slot_grad.astype(BF16)
    wide = jnp.concatenate([slot_grad.astype(F32), jnp.zeros((feats - chans, nslots), F32)], axis=0)
    sgs[...] = wide.T.astype(BF16).reshape(sgs.shape)
    spread(sgs, sgr, rev_sem)
    proj_part = jnp.dot(slot_grad, arrived, preferred_element_type=F32)
    ptiles[...] = proj_part.reshape(ptiles.shape)
    step = n // min(n, chans)
    pcount = ptiles.shape[0]
    scatter(ptiles, prs, prs_sem, pcount, step)

    row = lax.broadcasted_iota(jnp.int32, (full, 1), 0)
    perm_back[...] = (col == (row % cy) * chans + row // cy).astype(F32).astype(BF16)
    out_ref[...] = jnp.dot(
        perm_back[...], outs[...].reshape(full, nz), preferred_element_type=F32
    ).astype(BF16)

    reduce_gather(ptiles, prs, pag, prs_sem, pag_sem, pcount, step)
    waits(sgs, sgr, rev_sem, n - 1).wait_recv()
    back_ref[...] = sgr[...].reshape(nslots, feats)
    finish(rs, ag, rs_sem, ag_sem, nconv, 1)
    sums_ref[...] = ag[:nconv]
    finish(prs, pag, prs_sem, pag_sem, pcount, step)
    psum_ref[...] = pag[...].reshape(psum_ref.shape)

    waits(send, arr, a2a_sem, n - 1).wait_send()
    waits(sgs, sgr, rev_sem, n - 1).wait_send()
    for copies in f_edges:
        for copy in copies:
            copy.wait_send()
    for copy in g_edges:
        copy.wait_send()


def ending(
    count_all, counts_ref, back_ref, sums_ref, psum_ref, outf_ref, wpt_ref, out_ref, rowg_ref, convg_ref, projg_ref
):
    n = counts_ref.shape[1]
    nslots, feats = back_ref.shape
    chans = wpt_ref.shape[0]
    nrows = rowg_ref.shape[0]
    cap = nslots // n
    out_ref[...] = outf_ref[...]
    counts = jnp.broadcast_to(counts_ref[...].astype(F32), (8, n)).astype(BF16)
    upper = lax.broadcasted_iota(jnp.int32, (n, n), 0) <= lax.broadcasted_iota(jnp.int32, (n, n), 1)
    ends = jnp.dot(counts, upper.astype(F32).astype(BF16), preferred_element_type=F32)[:1]
    places = lax.broadcasted_iota(jnp.int32, (nrows, 1), 0)
    below = ends <= places.astype(F32)
    owner_of = jnp.sum(jnp.where(below, 1.0, 0.0), axis=1, keepdims=True)
    start_of = jnp.max(jnp.where(below, ends, 0.0), axis=1, keepdims=True)
    slot_of = (owner_of * cap - start_of).astype(jnp.int32) + places
    hit = lax.broadcasted_iota(jnp.int32, (nrows, nslots), 1) == slot_of
    back = jnp.dot(hit.astype(F32).astype(BF16), back_ref[...], preferred_element_type=F32)
    rowg_ref[...] = jnp.dot(
        back[:, :chans].astype(BF16), wpt_ref[...], preferred_element_type=F32
    )
    per = sums_ref.shape[1]
    rows = []
    for r in range(3 * chans // 8):
        tiles = [sums_ref[t // per, t % per] for t in range(5 * r, 5 * r + 5)]
        rows.append(jnp.concatenate(tiles, axis=1))
    sums = jnp.concatenate(rows, axis=0) * (1.0 / math.sqrt(count_all))
    for x in range(3):
        for y in range(3):
            for z in range(3):
                at = (y * 3 + x) * chans
                convg_ref[x * 9 + y * 3 + z] = sums[z * chans : (z + 1) * chans, at : at + chans]
    projg_ref[...] = psum_ref[...] * (1.0 / math.sqrt(nrows * n))


def local(ngx, ngy, particles, send_counts, cell_lists, base_field, proj_weight, conv_weight, cotangent):
    n = ngx * ngy
    nrows, feats = particles.shape
    chans, _, cy, nz = base_field.shape
    nslots = cell_lists.shape[1]
    full = chans * cy
    cap = nslots // n
    per = 128 // n
    pcount = min(n, chans)
    prow = chans // pcount
    weight_t = proj_weight.T
    dma = pltpu.SemaphoreType.DMA
    vmem = pl.BlockSpec(memory_space=pltpu.VMEM)
    plane = (cy, chans, nz)
    out, back, sums, psum = pl.pallas_call(
        functools.partial(kernel, ngx, ngy),
        out_shape=(
            jax.ShapeDtypeStruct((full, nz), BF16),
            jax.ShapeDtypeStruct((nslots, feats), BF16),
            jax.ShapeDtypeStruct((120 // per, per, 8, 128), F32),
            jax.ShapeDtypeStruct((chans, feats), F32),
        ),
        in_specs=[vmem] * 7,
        out_specs=[vmem] * 4,
        scratch_shapes=[
            pltpu.VMEM((n, cap, feats), BF16),
            pltpu.VMEM((n, cap, feats), BF16),
            pltpu.VMEM((cy, chans, nslots), BF16),
            pltpu.VMEM((3, nz, nslots), BF16),
            pltpu.VMEM((full, full), BF16),
            pltpu.VMEM((full, full), BF16),
            pltpu.VMEM((3 * chans, N_TAPS * chans), BF16),
            pltpu.VMEM((N_TAPS * chans, 3 * chans), BF16),
            pltpu.VMEM(plane, BF16),
            pltpu.VMEM(plane, BF16),
            pltpu.VMEM(plane, BF16),
            pltpu.VMEM((cy + 2, 3, chans, nz), BF16),
            pltpu.VMEM((cy + 2, chans, nz), BF16),
            pltpu.VMEM((4, cy, chans, nz), BF16),
            pltpu.VMEM((2, 1, nslots), jnp.int32),
            pltpu.VMEM((2, chans, nslots), BF16),
            pltpu.VMEM((2, chans, nslots), BF16),
            pltpu.VMEM((3 * chans, 640), F32),
            pltpu.VMEM((n, per, 8, 128), F32),
            pltpu.VMEM((n, per, 8, 128), F32),
            pltpu.VMEM((n, per, 8, 128), F32),
            pltpu.VMEM((pcount, prow, feats), F32),
            pltpu.VMEM((n, prow, feats), F32),
            pltpu.VMEM((pcount, prow, feats), F32),
            pltpu.VMEM((n, cap, feats), BF16),
            pltpu.VMEM((n, cap, feats), BF16),
            dma((2,)),
            dma((2,)),
            dma((2, 2)),
            dma((2, 2)),
            dma((2,)),
            dma((2,)),
            dma((2,)),
            dma((2,)),
            dma((4, 2)),
            dma((4, 2)),
            dma((2, 3)),
            dma((2, 3)),
            dma((2,)),
            dma((2,)),
        ],
        compiler_params=pltpu.CompilerParams(
            collective_id=0, has_side_effects=True, vmem_limit_bytes=44 * 1024 * 1024
        ),
        name="section",
    )(
        send_counts,
        cell_lists,
        particles,
        base_field.reshape(full, nz),
        cotangent.reshape(full, nz),
        conv_weight,
        weight_t,
    )
    out_field, row_grads, conv_grad, proj_t = pl.pallas_call(
        functools.partial(ending, cy * nz * n),
        out_shape=(
            jax.ShapeDtypeStruct((full, nz), BF16),
            jax.ShapeDtypeStruct((nrows, feats), F32),
            jax.ShapeDtypeStruct((27, chans, chans), F32),
            jax.ShapeDtypeStruct((chans, feats), F32),
        ),
        in_specs=[vmem] * 6,
        out_specs=[vmem] * 4,
        compiler_params=pltpu.CompilerParams(vmem_limit_bytes=16 * 1024 * 1024),
        name="ending",
    )(send_counts, back, sums, psum, out, weight_t)
    return out_field.reshape(base_field.shape), row_grads, conv_grad, proj_t.T


def solution(mesh):
    in_specs = (
        P(("gx", "gy"), None),
        P(("gx", "gy"), None),
        P(("gx", "gy"), None),
        P(None, "gx", "gy", None),
        P(),
        P(),
        P(None, "gx", "gy", None),
    )
    out_specs = (P(None, "gx", "gy", None), P(("gx", "gy"), None), P(), P())
    body = functools.partial(local, mesh.shape["gx"], mesh.shape["gy"])
    return jax.shard_map(body, mesh=mesh, in_specs=in_specs, out_specs=out_specs, check_vma=False)
```

```python
import functools
import math

import jax
import jax.numpy as jnp
from jax import lax
from jax.experimental import pallas as pl
from jax.experimental.pallas import tpu as pltpu
from jax.sharding import PartitionSpec as P

MESH = pl.DeviceIdType.MESH
F32 = jnp.float32
BF16 = jnp.bfloat16

F_CHUNKS = ((0, 4), (12, 4), (4, 4), (8, 4))
F_ROWS = ((0, 3), (13, 3), (3, 4), (7, 6))
N_TAPS = 9


def nt_dot(a, b):
    return lax.dot_general(a, b, (((1,), (1,)), ((), ())), preferred_element_type=F32)


def roll_z(x, shift):
    return pltpu.roll(x, shift % x.shape[1], 1)


def kernel(
    ngx,
    ngy,
    counts_ref,
    cells_ref,
    rows_ref,
    base_hbm,
    cot_hbm,
    taps_hbm,
    wpt_ref,
    out_ref,
    back_ref,
    sums_ref,
    psum_ref,
    base_ref,
    cot_ref,
    taps_ref,
    load_sem,
    send,
    arr,
    paint_a,
    paint_b,
    perm,
    perm_back,
    wf,
    wb,
    base,
    cot,
    outs,
    fld,
    pgr,
    grads,
    near_cells,
    near_out,
    near_in,
    acc,
    tiles,
    pair_in,
    rs,
    ag,
    ptiles,
    prs,
    pag,
    sgs,
    sgr,
    a2a_sem,
    rev_sem,
    cell_sem,
    near_sem,
    pair_sem,
    rs_sem,
    ag_sem,
    prs_sem,
    pag_sem,
    fx_send,
    fx_recv,
    fy_send,
    fy_recv,
    gy_send,
    gy_recv,
):
    n = ngx * ngy
    nrows, feats = rows_ref.shape
    cy, chans, nz = base.shape
    nslots = cells_ref.shape[1]
    cap = nslots // n
    per = tiles.shape[2]
    half = n // 2
    gi = lax.axis_index("gx")
    gj = lax.axis_index("gy")
    me = gi * ngy + gj

    def coords(d):
        return (lax.div(d, ngy), lax.rem(d, ngy))

    def peer_of(k):
        return lax.rem(me + k, n)

    def beside(b):
        return (lax.rem(gi + b + ngx, ngx), gj)

    barrier = pltpu.get_barrier_semaphore()

    @pl.loop(1, n)
    def _(k):
        pl.semaphore_signal(barrier, inc=1, device_id=coords(peer_of(k)), device_id_type=MESH)

    loads = [
        pltpu.make_async_copy(src, dst, load_sem.at[j])
        for j, (src, dst) in enumerate(
            ((base_hbm, base_ref), (taps_hbm, taps_ref), (cot_hbm, cot_ref))
        )
    ]
    for load in loads:
        load.start()

    counts = counts_ref[...].astype(F32)
    lane = lax.broadcasted_iota(jnp.int32, (nslots, n), 1)
    slot = lax.broadcasted_iota(jnp.int32, (nslots, 1), 0)
    owner = slot // cap
    offs = jnp.sum(jnp.where(lane < owner, counts, 0.0), axis=1, keepdims=True)
    mine = jnp.sum(jnp.where(lane == owner, counts, 0.0), axis=1, keepdims=True)
    place = slot - owner * cap
    index = jnp.where(place < mine.astype(jnp.int32), offs.astype(jnp.int32) + place, -1)
    pick = lax.broadcasted_iota(jnp.int32, (nslots, nrows), 1) == index
    outgoing = jnp.dot(pick.astype(F32).astype(BF16), rows_ref[...], preferred_element_type=F32)
    send[...] = outgoing.astype(BF16).reshape(send.shape)

    pl.semaphore_wait(barrier, n - 1)

    def remote(src, dst, send_sem, recv_sem, device):
        return pltpu.make_async_remote_copy(
            src_ref=src,
            dst_ref=dst,
            send_sem=send_sem,
            recv_sem=recv_sem,
            device_id=device,
            device_id_type=MESH,
        )

    def spread(src, dst, sems):
        @pl.loop(1, n)
        def _(k):
            peer = peer_of(k)
            remote(src.at[peer], dst.at[me], sems.at[0], sems.at[1], coords(peer)).start()

        dst[pl.ds(me, 1)] = src[pl.ds(me, 1)]

    def waits(src, dst, sems, count):
        part = pl.ds(0, count)
        return remote(src.at[part], dst.at[part], sems.at[0], sems.at[1], coords(peer_of(1)))

    spread(send, arr, a2a_sem)
    cell_copies = [
        remote(
            cells_ref,
            near_cells.at[(1 - b) // 2],
            cell_sem.at[0, (1 - b) // 2],
            cell_sem.at[1, (1 - b) // 2],
            beside(b),
        )
        for b in (-1, 1)
    ]
    for copy in cell_copies:
        copy.start()

    def at_depth(cells):
        hit = lax.broadcasted_iota(jnp.int32, (nz, nslots), 0) == cells % nz
        return hit.astype(F32).astype(BF16)

    cell_y = cells_ref[...] // nz
    paint_b[0] = at_depth(cells_ref[...])
    full = cy * chans
    row = lax.broadcasted_iota(jnp.int32, (full, 1), 0)
    col = lax.broadcasted_iota(jnp.int32, (full, full), 1)
    perm[...] = (col == (row % chans) * cy + row // chans).astype(F32).astype(BF16)
    for load in loads:
        load.wait()
    base[...] = (
        jnp.dot(perm[...], base_ref[...], preferred_element_type=F32).astype(BF16).reshape(base.shape)
    )
    cot[...] = (
        jnp.dot(perm[...], cot_ref[...], preferred_element_type=F32).astype(BF16).reshape(cot.shape)
    )
    for x in range(3):
        for y in range(3):
            for z in range(3):
                tap = taps_ref[x * 9 + y * 3 + z]
                at = (y * 3 + x) * chans
                wf[z * chans : (z + 1) * chans, at : at + chans] = tap
                at = (x * 3 + 2 - z) * chans
                side = (2 - y) * chans
                wb[at : at + chans, side : side + chans] = tap.astype(F32).T.astype(BF16)
    acc[...] = jnp.zeros_like(acc)

    waits(send, arr, a2a_sem, n - 1).wait_recv()

    arrived = arr[...].reshape(nslots, feats)
    projected = nt_dot(wpt_ref[...], arrived).astype(BF16).astype(F32)
    for y in range(cy):
        paint_a[y] = jnp.where(cell_y == y, projected, 0.0).astype(BF16)

    def edge_copy(side, b):
        to = (lax.rem(gi + b + ngx, ngx), lax.rem(gj + (1 if side == 0 else ngy - 1), ngy))
        row = cy if side == 0 else 1
        dst = 0 if side == 0 else cy + 1
        sem = (side, 1 - b)
        return remote(fld.at[row, 1], fld.at[dst, 1 - b], fy_send.at[sem], fy_recv.at[sem], to)

    def grad_edge(side):
        to = (gi, lax.rem(gj + (1 if side == 0 else ngy - 1), ngy))
        row = cy if side == 0 else 1
        dst = 0 if side == 0 else cy + 1
        return remote(pgr.at[row], pgr.at[dst], gy_send.at[side], gy_recv.at[side], to)

    def plane_copy(c, first, count, b):
        rows = pl.ds(first + 1, count)
        sem = (c, (1 - b) // 2)
        return remote(
            fld.at[rows, 1], fld.at[rows, 1 - b], fx_send.at[sem], fx_recv.at[sem], beside(b)
        )

    f_planes = [
        [plane_copy(c, first, count, b) for b in (-1, 1)]
        for c, (first, count) in enumerate(F_CHUNKS)
    ]
    f_edges = [[edge_copy(side, b) for b in (-1, 0, 1)] for side in (0, 1)]
    g_edges = [grad_edge(side) for side in (0, 1)]

    for c, (first, count) in enumerate(F_CHUNKS):
        rows = slice(first, first + count)
        painted = nt_dot(paint_a[rows].reshape(count * chans, nslots), paint_b[0])
        painted = painted.reshape(count, chans, nz)
        fld[first + 1 : first + count + 1, 1] = (base[rows].astype(F32) + painted).astype(BF16)
        if first == 0:
            for copy in f_edges[1]:
                copy.start()
        if first + count == cy:
            for copy in f_edges[0]:
                copy.start()
        for copy in f_planes[c]:
            copy.start()

    for copy in cell_copies:
        copy.wait()
    near_y = [near_cells[e] // nz for e in (0, 1)]
    for e in (0, 1):
        paint_b[1 + e] = at_depth(near_cells[e])

    for c, (first, count) in enumerate(F_ROWS):
        for copy in f_planes[c]:
            copy.wait_recv()
        if c < 2:
            for copy in f_edges[c]:
                copy.wait_recv()
        slabs, threes = [], []
        for y in range(first, first + count):
            slab = fld[y : y + 3].reshape(N_TAPS * chans, nz)
            part = jnp.dot(wf[...], slab, preferred_element_type=F32)
            pre = roll_z(part[:chans], 1) + part[chans : 2 * chans] + roll_z(part[2 * chans :], -1)
            sig = jax.nn.sigmoid(pre)
            outs[y] = (fld[y + 1, 1].astype(F32) + pre * sig).astype(BF16)
            grad = (cot[y].astype(F32) * sig * (1.0 + pre * (1.0 - sig))).astype(BF16)
            pgr[y + 1] = grad
            wide = grad.astype(F32)
            three = jnp.concatenate([roll_z(wide, -1), wide, roll_z(wide, 1)], axis=0)
            slabs.append(slab)
            threes.append(three.astype(BF16))
        if c < 2:
            g_edges[1 - c].start()
        acc[:, : N_TAPS * chans] += nt_dot(
            jnp.concatenate(threes, axis=1), jnp.concatenate(slabs, axis=1)
        )

    per_row = acc.shape[1] // 128
    for t in range(128):
        r, q = divmod(t, per_row)
        share = t // per
        if t < 120:
            part = acc[8 * r : 8 * r + 8, 128 * q : 128 * q + 128]
        else:
            part = jnp.zeros((8, 128), F32)
        tiles[share % 2, share // 2, t % per] = part
    core = lax.rem(me, 2)
    chip = lax.div(me, 2)
    pair_copy = remote(
        tiles.at[1 - core], pair_in, pair_sem.at[0], pair_sem.at[1], coords(me + 1 - 2 * core)
    )
    pair_copy.start()

    def scatter(src, dst, sems, count, step):
        @pl.loop(1, n)
        def _(k):
            peer = peer_of(k)
            share = lax.div(peer, step)

            @pl.when((share < count) & (share * step == peer))
            def _():
                remote(src.at[share], dst.at[me], sems.at[0], sems.at[1], coords(peer)).start()

    def mine_of(count, step):
        share = lax.div(me, step)
        return share, (share < count) & (share * step == me)

    def reduce_gather(src, part, dst, sems, gather_sems, count, step):
        share, own = mine_of(count, step)

        @pl.when(own)
        def _():
            waits(part, part, sems, n - 1).wait_recv()
            part[pl.ds(me, 1)] = src[pl.ds(share, 1)]
            dst[pl.ds(share, 1)] = jnp.sum(part[...], axis=0, keepdims=True)

            @pl.loop(1, n)
            def _(k):
                there = dst.at[share]
                remote(
                    there, there, gather_sems.at[0], gather_sems.at[1], coords(peer_of(k))
                ).start()

    def finish(part, dst, sems, gather_sems, count, step):
        _, own = mine_of(count, step)

        @pl.when(own)
        def _():
            waits(part, part, gather_sems, n - 1).wait_send()
            if count > 1:
                waits(dst, dst, sems, count - 1).wait_send()
                waits(dst, dst, gather_sems, count - 1).wait_recv()

        @pl.when(jnp.logical_not(own))
        def _():
            waits(dst, dst, sems, count).wait_send()
            waits(dst, dst, gather_sems, count).wait_recv()


    for c, (first, count) in enumerate(((1, cy - 2), (0, 1), (cy - 1, 1))):
        if c == 1:
            for copy in g_edges:
                copy.wait_recv()
        for y in range(first, first + count):
            slab = pgr[y : y + 3].reshape(3 * chans, nz)
            part = jnp.dot(wb[...], slab, preferred_element_type=F32)
            for x in range(3):
                p = part[3 * x * chans : 3 * (x + 1) * chans]
                got = roll_z(p[:chans], 1) + p[chans : 2 * chans] + roll_z(p[2 * chans :], -1)
                if x == 1:
                    got = got + cot[y].astype(F32)
                    high = got.astype(BF16)
                    grads[3, y] = (got - high.astype(F32)).astype(BF16)
                    grads[1, y] = high
                else:
                    grads[x, y] = got.astype(BF16)

    def at_slots(which, depth, ys, total):
        step = 4
        for first in range(0, cy, step):
            rows = grads[which, first : first + step].reshape(step * chans, nz)
            got = jnp.dot(rows, paint_b[depth], preferred_element_type=F32)
            for y in range(step):
                part = got[y * chans : (y + 1) * chans]
                total = total + jnp.where(ys == first + y, part, 0.0)
        return total

    zero = jnp.zeros((chans, nslots), F32)
    near_copies = []
    for e, b in ((0, -1), (1, 1)):
        near_out[e] = at_slots(1 + b, 1 + e, near_y[e], zero).astype(BF16)
        copy = remote(
            near_out.at[e], near_in.at[1 - e], near_sem.at[0, e], near_sem.at[1, 1 - e], beside(b)
        )
        copy.start()
        near_copies.append(copy)
    pair_copy.wait()
    tiles[pl.ds(core, 1)] = tiles[pl.ds(core, 1)] + pair_in[...][None]

    @pl.loop(1, half)
    def _(k):
        there = lax.rem(chip + k, half)
        device = coords(2 * there + core)
        remote(tiles.at[core, there], rs.at[chip], rs_sem.at[0], rs_sem.at[1], device).start()

    slot_grad = at_slots(1, 0, cell_y, at_slots(3, 0, cell_y, zero))
    for copy in near_copies:
        copy.wait()
    slot_grad = slot_grad + near_in[0].astype(F32) + near_in[1].astype(F32)

    slot_grad = slot_grad.astype(BF16)
    wide = jnp.concatenate([slot_grad.astype(F32), jnp.zeros((feats - chans, nslots), F32)], axis=0)
    sgs[...] = wide.T.astype(BF16).reshape(sgs.shape)
    spread(sgs, sgr, rev_sem)
    proj_part = jnp.dot(slot_grad, arrived, preferred_element_type=F32)
    ptiles[...] = proj_part.reshape(ptiles.shape)
    step = n // min(n, chans)
    pcount = ptiles.shape[0]
    scatter(ptiles, prs, prs_sem, pcount, step)

    waits(rs, rs, rs_sem, half - 1).wait_recv()
    rs[pl.ds(chip, 1)] = tiles[core, pl.ds(chip, 1)]
    ag[pl.ds(me, 1)] = jnp.sum(rs[...], axis=0, keepdims=True)

    @pl.loop(1, n)
    def _(k):
        there = ag.at[me]
        remote(there, there, ag_sem.at[0], ag_sem.at[1], coords(peer_of(k))).start()

    row = lax.broadcasted_iota(jnp.int32, (full, 1), 0)
    perm_back[...] = (col == (row % cy) * chans + row // cy).astype(F32).astype(BF16)
    out_ref[...] = jnp.dot(
        perm_back[...], outs[...].reshape(full, nz), preferred_element_type=F32
    ).astype(BF16)

    reduce_gather(ptiles, prs, pag, prs_sem, pag_sem, pcount, step)
    waits(sgs, sgr, rev_sem, n - 1).wait_recv()
    back_ref[...] = sgr[...].reshape(nslots, feats)
    waits(ag, ag, ag_sem, n - 1).wait_recv()
    sums_ref[...] = ag[: sums_ref.shape[0]]
    finish(prs, pag, prs_sem, pag_sem, pcount, step)
    psum_ref[...] = pag[...].reshape(psum_ref.shape)

    waits(send, arr, a2a_sem, n - 1).wait_send()
    waits(sgs, sgr, rev_sem, n - 1).wait_send()
    waits(rs, rs, rs_sem, half - 1).wait_send()
    waits(ag, ag, ag_sem, n - 1).wait_send()
    for copies in f_edges + f_planes:
        for copy in copies:
            copy.wait_send()
    for copy in g_edges:
        copy.wait_send()


def ending(
    count_all, counts_ref, back_ref, sums_ref, psum_ref, outf_ref, wpt_ref, out_ref, rowg_ref, convg_ref, projg_ref
):
    n = counts_ref.shape[1]
    nslots, feats = back_ref.shape
    chans = wpt_ref.shape[0]
    nrows = rowg_ref.shape[0]
    cap = nslots // n
    out_ref[...] = outf_ref[...]
    counts = jnp.broadcast_to(counts_ref[...].astype(F32), (8, n)).astype(BF16)
    upper = lax.broadcasted_iota(jnp.int32, (n, n), 0) <= lax.broadcasted_iota(jnp.int32, (n, n), 1)
    ends = jnp.dot(counts, upper.astype(F32).astype(BF16), preferred_element_type=F32)[:1]
    places = lax.broadcasted_iota(jnp.int32, (nrows, 1), 0)
    below = ends <= places.astype(F32)
    owner_of = jnp.sum(jnp.where(below, 1.0, 0.0), axis=1, keepdims=True)
    start_of = jnp.max(jnp.where(below, ends, 0.0), axis=1, keepdims=True)
    slot_of = (owner_of * cap - start_of).astype(jnp.int32) + places
    hit = lax.broadcasted_iota(jnp.int32, (nrows, nslots), 1) == slot_of
    back = jnp.dot(hit.astype(F32).astype(BF16), back_ref[...], preferred_element_type=F32)
    rowg_ref[...] = jnp.dot(
        back[:, :chans].astype(BF16), wpt_ref[...], preferred_element_type=F32
    )
    per = sums_ref.shape[1]
    rows = []
    for r in range(3 * chans // 8):
        tiles = [sums_ref[t // per, t % per] for t in range(5 * r, 5 * r + 5)]
        rows.append(jnp.concatenate(tiles, axis=1))
    sums = jnp.concatenate(rows, axis=0) * (1.0 / math.sqrt(count_all))
    for x in range(3):
        for y in range(3):
            for z in range(3):
                at = (y * 3 + x) * chans
                convg_ref[x * 9 + y * 3 + z] = sums[z * chans : (z + 1) * chans, at : at + chans]
    projg_ref[...] = psum_ref[...] * (1.0 / math.sqrt(nrows * n))


def local(ngx, ngy, particles, send_counts, cell_lists, base_field, proj_weight, conv_weight, cotangent):
    n = ngx * ngy
    nrows, feats = particles.shape
    chans, _, cy, nz = base_field.shape
    nslots = cell_lists.shape[1]
    full = chans * cy
    cap = nslots // n
    per = 128 // n
    pcount = min(n, chans)
    prow = chans // pcount
    weight_t = proj_weight.T
    dma = pltpu.SemaphoreType.DMA
    vmem = pl.BlockSpec(memory_space=pltpu.VMEM)
    plane = (cy, chans, nz)
    out, back, sums, psum = pl.pallas_call(
        functools.partial(kernel, ngx, ngy),
        out_shape=(
            jax.ShapeDtypeStruct((full, nz), BF16),
            jax.ShapeDtypeStruct((nslots, feats), BF16),
            jax.ShapeDtypeStruct((120 // per, per, 8, 128), F32),
            jax.ShapeDtypeStruct((chans, feats), F32),
        ),
        in_specs=[vmem] * 3 + [pl.BlockSpec(memory_space=pl.ANY)] * 3 + [vmem],
        out_specs=[vmem] * 4,
        scratch_shapes=[
            pltpu.VMEM((full, nz), BF16),
            pltpu.VMEM((full, nz), BF16),
            pltpu.VMEM((27, chans, chans), BF16),
            dma((3,)),
            pltpu.VMEM((n, cap, feats), BF16),
            pltpu.VMEM((n, cap, feats), BF16),
            pltpu.VMEM((cy, chans, nslots), BF16),
            pltpu.VMEM((3, nz, nslots), BF16),
            pltpu.VMEM((full, full), BF16),
            pltpu.VMEM((full, full), BF16),
            pltpu.VMEM((3 * chans, N_TAPS * chans), BF16),
            pltpu.VMEM((N_TAPS * chans, 3 * chans), BF16),
            pltpu.VMEM(plane, BF16),
            pltpu.VMEM(plane, BF16),
            pltpu.VMEM(plane, BF16),
            pltpu.VMEM((cy + 2, 3, chans, nz), BF16),
            pltpu.VMEM((cy + 2, chans, nz), BF16),
            pltpu.VMEM((4, cy, chans, nz), BF16),
            pltpu.VMEM((2, 1, nslots), jnp.int32),
            pltpu.VMEM((2, chans, nslots), BF16),
            pltpu.VMEM((2, chans, nslots), BF16),
            pltpu.VMEM((3 * chans, 640), F32),
            pltpu.VMEM((2, n // 2, per, 8, 128), F32),
            pltpu.VMEM((n // 2, per, 8, 128), F32),
            pltpu.VMEM((n // 2, per, 8, 128), F32),
            pltpu.VMEM((n, per, 8, 128), F32),
            pltpu.VMEM((pcount, prow, feats), F32),
            pltpu.VMEM((n, prow, feats), F32),
            pltpu.VMEM((pcount, prow, feats), F32),
            pltpu.VMEM((n, cap, feats), BF16),
            pltpu.VMEM((n, cap, feats), BF16),
            dma((2,)),
            dma((2,)),
            dma((2, 2)),
            dma((2, 2)),
            dma((2,)),
            dma((2,)),
            dma((2,)),
            dma((2,)),
            dma((2,)),
            dma((4, 2)),
            dma((4, 2)),
            dma((2, 3)),
            dma((2, 3)),
            dma((2,)),
            dma((2,)),
        ],
        compiler_params=pltpu.CompilerParams(
            collective_id=0, has_side_effects=True, vmem_limit_bytes=60 * 1024 * 1024
        ),
        name="section",
    )(
        send_counts,
        cell_lists,
        particles,
        base_field.reshape(full, nz),
        cotangent.reshape(full, nz),
        conv_weight,
        weight_t,
    )
    out_field, row_grads, conv_grad, proj_t = pl.pallas_call(
        functools.partial(ending, cy * nz * n),
        out_shape=(
            jax.ShapeDtypeStruct((full, nz), BF16),
            jax.ShapeDtypeStruct((nrows, feats), F32),
            jax.ShapeDtypeStruct((27, chans, chans), F32),
            jax.ShapeDtypeStruct((chans, feats), F32),
        ),
        in_specs=[vmem] * 6,
        out_specs=[vmem] * 4,
        compiler_params=pltpu.CompilerParams(vmem_limit_bytes=60 * 1024 * 1024),
        name="ending",
    )(send_counts, back, sums, psum, out, weight_t)
    return out_field.reshape(base_field.shape), row_grads, conv_grad, proj_t.T


def solution(mesh):
    in_specs = (
        P(("gx", "gy"), None),
        P(("gx", "gy"), None),
        P(("gx", "gy"), None),
        P(None, "gx", "gy", None),
        P(),
        P(),
        P(None, "gx", "gy", None),
    )
    out_specs = (P(None, "gx", "gy", None), P(("gx", "gy"), None), P(), P())
    body = functools.partial(local, mesh.shape["gx"], mesh.shape["gy"])
    return jax.shard_map(body, mesh=mesh, in_specs=in_specs, out_specs=out_specs, check_vma=False)
```

```python
import functools
import math

import jax
import jax.numpy as jnp
from jax import lax
from jax.experimental import pallas as pl
from jax.experimental.pallas import tpu as pltpu
from jax.sharding import PartitionSpec as P

MESH = pl.DeviceIdType.MESH
FLAT = pl.DeviceIdType.LOGICAL
F32 = jnp.float32
BF16 = jnp.bfloat16

F_CHUNKS = ((0, 4), (12, 4), (4, 4), (8, 4))
F_ROWS = ((0, 3), (13, 3), (3, 4), (7, 6))
N_TAPS = 9


def nt_dot(a, b):
    return lax.dot_general(a, b, (((1,), (1,)), ((), ())), preferred_element_type=F32)


def roll_z(x, shift):
    return pltpu.roll(x, shift % x.shape[1], 1)


def kernel(
    ngx,
    ngy,
    counts_ref,
    cells_ref,
    rows_ref,
    base_hbm,
    cot_hbm,
    taps_hbm,
    wpt_ref,
    out_ref,
    back_ref,
    sums_ref,
    psum_ref,
    base_ref,
    cot_ref,
    taps_ref,
    load_sem,
    send,
    arr,
    paint_a,
    paint_b,
    perm,
    perm_back,
    wf,
    wb,
    base,
    cot,
    outs,
    fld,
    pgr,
    grads,
    near_cells,
    near_out,
    near_in,
    acc,
    tiles,
    pair_in,
    rs,
    ag,
    ptiles,
    prs,
    sgs,
    sgr,
    a2a_sem,
    rev_sem,
    cell_sem,
    near_sem,
    pair_sem,
    rs_sem,
    ag_sem,
    prs_sem,
    fx_send,
    fx_recv,
    fy_send,
    fy_recv,
    gy_send,
    gy_recv,
):
    n = ngx * ngy
    nrows, feats = rows_ref.shape
    cy, chans, nz = base.shape
    nslots = cells_ref.shape[1]
    cap = nslots // n
    per = tiles.shape[2]
    half = n // 2
    gi = lax.axis_index("gx")
    gj = lax.axis_index("gy")
    me = gi * ngy + gj

    low = 2 if ngx >= 8 else 1
    dims = (ngx // (4 * low), 4, ngy // 2 * low, 2)
    core = gj % 2
    chip = me // 2
    at = (gi // (4 * low), gi % 4, gj // 2 * low + gi // 4 % low, core)
    moved = [[(at[a] + d) % dims[a] for d in range(dims[a])] for a in range(4)]
    places = [
        [v * (4 * low * ngy) for v in moved[0]],
        [v * ngy for v in moved[1]],
        [v % low * (4 * ngy) + v // low * 2 for v in moved[2]],
        moved[3],
    ]
    steps = [
        (a, b, c, d)
        for a in range(dims[0])
        for b in range(dims[1])
        for c in range(dims[2])
        for d in range(dims[3])
        if (a, b, c, d) != (0, 0, 0, 0)
    ]

    def hops(step):
        return -sum(min(v, size - v) for v, size in zip(step[:3], dims)), -step[3]

    steps.sort(key=hops)
    chips = [
        [places[0][a] + places[1][b] for b in range(dims[1])] for a in range(dims[0])
    ]
    ends = [[places[2][c] + places[3][d] for d in range(2)] for c in range(dims[2])]
    peers = [(chips[a][b] + ends[c][d], d) for a, b, c, d in steps]

    def beside(b):
        return (lax.rem(gi + b + ngx, ngx), gj)

    barrier = pltpu.get_barrier_semaphore()

    for peer, _ in peers:
        pl.semaphore_signal(barrier, inc=1, device_id=peer, device_id_type=FLAT)

    loads = [
        pltpu.make_async_copy(src, dst, load_sem.at[j])
        for j, (src, dst) in enumerate(
            ((base_hbm, base_ref), (taps_hbm, taps_ref), (cot_hbm, cot_ref))
        )
    ]
    for load in loads:
        load.start()

    counts = counts_ref[...].astype(F32)
    lane = lax.broadcasted_iota(jnp.int32, (nslots, n), 1)
    slot = lax.broadcasted_iota(jnp.int32, (nslots, 1), 0)
    owner = slot // cap
    offs = jnp.sum(jnp.where(lane < owner, counts, 0.0), axis=1, keepdims=True)
    mine = jnp.sum(jnp.where(lane == owner, counts, 0.0), axis=1, keepdims=True)
    place = slot - owner * cap
    index = jnp.where(place < mine.astype(jnp.int32), offs.astype(jnp.int32) + place, -1)
    pick = lax.broadcasted_iota(jnp.int32, (nslots, nrows), 1) == index
    outgoing = jnp.dot(pick.astype(F32).astype(BF16), rows_ref[...], preferred_element_type=F32)
    send[...] = outgoing.astype(BF16).reshape(send.shape)

    pl.semaphore_wait(barrier, n - 1)

    def remote(src, dst, send_sem, recv_sem, device):
        return pltpu.make_async_remote_copy(
            src_ref=src,
            dst_ref=dst,
            send_sem=send_sem,
            recv_sem=recv_sem,
            device_id=device,
            device_id_type=MESH if isinstance(device, tuple) else FLAT,
        )

    def spread(src, dst, sems):
        for peer, _ in peers:
            remote(src.at[peer], dst.at[me], sems.at[0], sems.at[1], peer).start()
        dst[pl.ds(me, 1)] = src[pl.ds(me, 1)]

    def waits(src, dst, sems, count):
        part = pl.ds(0, count)
        return remote(src.at[part], dst.at[part], sems.at[0], sems.at[1], peers[0][0])

    spread(send, arr, a2a_sem)
    cell_copies = [
        remote(
            cells_ref,
            near_cells.at[(1 - b) // 2],
            cell_sem.at[0, (1 - b) // 2],
            cell_sem.at[1, (1 - b) // 2],
            beside(b),
        )
        for b in (-1, 1)
    ]
    for copy in cell_copies:
        copy.start()

    def at_depth(cells):
        hit = lax.broadcasted_iota(jnp.int32, (nz, nslots), 0) == cells % nz
        return hit.astype(F32).astype(BF16)

    cell_y = cells_ref[...] // nz
    paint_b[0] = at_depth(cells_ref[...])
    full = cy * chans
    row = lax.broadcasted_iota(jnp.int32, (full, 1), 0)
    col = lax.broadcasted_iota(jnp.int32, (full, full), 1)
    perm[...] = (col == (row % chans) * cy + row // chans).astype(F32).astype(BF16)
    for load in loads:
        load.wait()
    base[...] = (
        jnp.dot(perm[...], base_ref[...], preferred_element_type=F32).astype(BF16).reshape(base.shape)
    )
    cot[...] = (
        jnp.dot(perm[...], cot_ref[...], preferred_element_type=F32).astype(BF16).reshape(cot.shape)
    )
    for x in range(3):
        for y in range(3):
            for z in range(3):
                tap = taps_ref[x * 9 + y * 3 + z]
                at = (y * 3 + x) * chans
                wf[z * chans : (z + 1) * chans, at : at + chans] = tap
                at = (x * 3 + 2 - z) * chans
                side = (2 - y) * chans
                wb[at : at + chans, side : side + chans] = tap.astype(F32).T.astype(BF16)
    acc[...] = jnp.zeros_like(acc)

    waits(send, arr, a2a_sem, n - 1).wait_recv()

    arrived = arr[...].reshape(nslots, feats)
    projected = nt_dot(wpt_ref[...], arrived).astype(BF16).astype(F32)
    for y in range(cy):
        paint_a[y] = jnp.where(cell_y == y, projected, 0.0).astype(BF16)

    def edge_copy(side, b):
        to = (lax.rem(gi + b + ngx, ngx), lax.rem(gj + (1 if side == 0 else ngy - 1), ngy))
        row = cy if side == 0 else 1
        dst = 0 if side == 0 else cy + 1
        sem = (side, 1 - b)
        return remote(fld.at[row, 1], fld.at[dst, 1 - b], fy_send.at[sem], fy_recv.at[sem], to)

    def grad_edge(side):
        to = (gi, lax.rem(gj + (1 if side == 0 else ngy - 1), ngy))
        row = cy if side == 0 else 1
        dst = 0 if side == 0 else cy + 1
        return remote(pgr.at[row], pgr.at[dst], gy_send.at[side], gy_recv.at[side], to)

    def plane_copy(c, first, count, b):
        rows = pl.ds(first + 1, count)
        sem = (c, (1 - b) // 2)
        return remote(
            fld.at[rows, 1], fld.at[rows, 1 - b], fx_send.at[sem], fx_recv.at[sem], beside(b)
        )

    f_planes = [
        [plane_copy(c, first, count, b) for b in (-1, 1)]
        for c, (first, count) in enumerate(F_CHUNKS)
    ]
    f_edges = [[edge_copy(side, b) for b in (-1, 0, 1)] for side in (0, 1)]
    g_edges = [grad_edge(side) for side in (0, 1)]

    for c, (first, count) in enumerate(F_CHUNKS):
        rows = slice(first, first + count)
        painted = nt_dot(paint_a[rows].reshape(count * chans, nslots), paint_b[0])
        painted = painted.reshape(count, chans, nz)
        fld[first + 1 : first + count + 1, 1] = (base[rows].astype(F32) + painted).astype(BF16)
        if first == 0:
            for copy in f_edges[1]:
                copy.start()
        if first + count == cy:
            for copy in f_edges[0]:
                copy.start()
        for copy in f_planes[c]:
            copy.start()

    for copy in cell_copies:
        copy.wait()
    near_y = [near_cells[e] // nz for e in (0, 1)]
    for e in (0, 1):
        paint_b[1 + e] = at_depth(near_cells[e])

    def backward_row(y):
        slab = pgr[y : y + 3].reshape(3 * chans, nz)
        part = jnp.dot(wb[...], slab, preferred_element_type=F32)
        for x in range(3):
            p = part[3 * x * chans : 3 * (x + 1) * chans]
            got = roll_z(p[:chans], 1) + p[chans : 2 * chans] + roll_z(p[2 * chans :], -1)
            if x == 1:
                got = got + cot[y].astype(F32)
                high = got.astype(BF16)
                grads[3, y] = (got - high.astype(F32)).astype(BF16)
                grads[1, y] = high
            else:
                grads[x, y] = got.astype(BF16)

    def tap_terms(slabs, threes):
        acc[:, : N_TAPS * chans] += nt_dot(
            jnp.concatenate(threes, axis=1), jnp.concatenate(slabs, axis=1)
        )

    for c, (first, count) in enumerate(F_ROWS):
        for copy in f_planes[c]:
            copy.wait_recv()
        if c < 2:
            for copy in f_edges[c]:
                copy.wait_recv()
        slabs, threes = [], []
        for y in range(first, first + count):
            slab = fld[y : y + 3].reshape(N_TAPS * chans, nz)
            part = jnp.dot(wf[...], slab, preferred_element_type=F32)
            pre = roll_z(part[:chans], 1) + part[chans : 2 * chans] + roll_z(part[2 * chans :], -1)
            sig = jax.nn.sigmoid(pre)
            outs[y] = (fld[y + 1, 1].astype(F32) + pre * sig).astype(BF16)
            grad = (cot[y].astype(F32) * sig * (1.0 + pre * (1.0 - sig))).astype(BF16)
            pgr[y + 1] = grad
            wide = grad.astype(F32)
            three = jnp.concatenate([roll_z(wide, -1), wide, roll_z(wide, 1)], axis=0)
            slabs.append(slab)
            threes.append(three.astype(BF16))
        if c < 2:
            g_edges[1 - c].start()
        if c < 3:
            tap_terms(slabs, threes)
        if c == 2:
            for y in (1, 2, 3, 4, 5, 14):
                backward_row(y)

    for y in range(6, 14):
        backward_row(y)
    for copy in g_edges:
        copy.wait_recv()
    backward_row(0)
    backward_row(15)

    def at_slots(which, depth, ys, total):
        step = 4
        for first in range(0, cy, step):
            rows = grads[which, first : first + step].reshape(step * chans, nz)
            got = jnp.dot(rows, paint_b[depth], preferred_element_type=F32)
            for y in range(step):
                part = got[y * chans : (y + 1) * chans]
                total = total + jnp.where(ys == first + y, part, 0.0)
        return total

    zero = jnp.zeros((chans, nslots), F32)
    near_copies = []
    for e, b in ((0, -1), (1, 1)):
        near_out[e] = at_slots(1 + b, 1 + e, near_y[e], zero).astype(BF16)
        copy = remote(
            near_out.at[e], near_in.at[1 - e], near_sem.at[0, e], near_sem.at[1, 1 - e], beside(b)
        )
        copy.start()
        near_copies.append(copy)

    tap_terms(slabs, threes)
    per_row = acc.shape[1] // 128
    proj_shares = 8 // per
    stride = n // proj_shares
    proj_at = [stride * m + 5 * (m % 4) for m in range(proj_shares)]
    conv_at = [d for d in range(n) if d not in proj_at]
    for t in range(120):
        r, q = divmod(t, per_row)
        d = conv_at[t // per]
        tiles[d % 2, d // 2, t % per] = acc[8 * r : 8 * r + 8, 128 * q : 128 * q + 128]
    for d in proj_at:
        tiles[d % 2, d // 2] = jnp.zeros((per, 8, 128), F32)
    pair_copy = remote(
        tiles.at[1 - core], pair_in, pair_sem.at[0], pair_sem.at[1], me + 1 - 2 * core
    )
    pair_copy.start()
    slot_grad = at_slots(1, 0, cell_y, at_slots(3, 0, cell_y, zero))
    pair_copy.wait()
    tiles[pl.ds(core, 1)] = tiles[pl.ds(core, 1)] + pair_in[...][None]
    for peer, d in peers:
        if d == 0:
            remote(
                tiles.at[core, peer // 2], rs.at[chip], rs_sem.at[0], rs_sem.at[1], peer
            ).start()

    for copy in near_copies:
        copy.wait()
    slot_grad = slot_grad + near_in[0].astype(F32) + near_in[1].astype(F32)

    slot_grad = slot_grad.astype(BF16)
    wide = jnp.concatenate([slot_grad.astype(F32), jnp.zeros((feats - chans, nslots), F32)], axis=0)
    sgs[...] = wide.T.astype(BF16).reshape(sgs.shape)
    spread(sgs, sgr, rev_sem)
    proj_part = jnp.dot(slot_grad, arrived, preferred_element_type=F32)
    for t in range(8):
        ptiles[t // per, t % per] = proj_part[8 * t : 8 * t + 8]
    group = me // stride
    proj_owner = me % stride == 5 * (group % 4)
    for m, d in enumerate(proj_at):

        @pl.when(me != d)
        def _(m=m, d=d):
            remote(ptiles.at[m], prs.at[me], prs_sem.at[0], prs_sem.at[1], d).start()

    def gather():
        there = ag.at[me]
        for peer, _ in peers:
            remote(there, there, ag_sem.at[0], ag_sem.at[1], peer).start()

    waits(rs, rs, rs_sem, half - 1).wait_recv()

    @pl.when(jnp.logical_not(proj_owner))
    def _():
        rs[pl.ds(chip, 1)] = tiles[core, pl.ds(chip, 1)]
        ag[pl.ds(me, 1)] = jnp.sum(rs[...], axis=0, keepdims=True)
        gather()

    @pl.when(proj_owner)
    def _():
        waits(prs, prs, prs_sem, n - 1).wait_recv()
        prs[pl.ds(me, 1)] = ptiles[pl.ds(group, 1)]
        ag[pl.ds(me, 1)] = jnp.sum(prs[...], axis=0, keepdims=True)
        gather()

    row = lax.broadcasted_iota(jnp.int32, (full, 1), 0)
    perm_back[...] = (col == (row % cy) * chans + row // cy).astype(F32).astype(BF16)
    out_ref[...] = jnp.dot(
        perm_back[...], outs[...].reshape(full, nz), preferred_element_type=F32
    ).astype(BF16)

    waits(sgs, sgr, rev_sem, n - 1).wait_recv()
    back_ref[...] = sgr[...].reshape(nslots, feats)
    waits(ag, ag, ag_sem, n - 1).wait_recv()
    for t in range(120):
        sums_ref[t // per, t % per] = ag[conv_at[t // per], t % per]
    for t in range(8):
        psum_ref[8 * t : 8 * t + 8] = ag[proj_at[t // per], t % per]

    @pl.when(proj_owner)
    def _():
        if proj_shares > 1:
            waits(ptiles, ptiles, prs_sem, proj_shares - 1).wait_send()

    @pl.when(jnp.logical_not(proj_owner))
    def _():
        waits(ptiles, ptiles, prs_sem, proj_shares).wait_send()

    waits(send, arr, a2a_sem, n - 1).wait_send()
    waits(sgs, sgr, rev_sem, n - 1).wait_send()
    waits(rs, rs, rs_sem, half - 1).wait_send()
    waits(ag, ag, ag_sem, n - 1).wait_send()
    for copies in f_edges + f_planes:
        for copy in copies:
            copy.wait_send()
    for copy in g_edges:
        copy.wait_send()


def ending(
    count_all, counts_ref, back_ref, sums_ref, psum_ref, outf_ref, wpt_ref, out_ref, rowg_ref, convg_ref, projg_ref
):
    n = counts_ref.shape[1]
    nslots, feats = back_ref.shape
    chans = wpt_ref.shape[0]
    nrows = rowg_ref.shape[0]
    cap = nslots // n
    out_ref[...] = outf_ref[...]
    counts = jnp.broadcast_to(counts_ref[...].astype(F32), (8, n)).astype(BF16)
    upper = lax.broadcasted_iota(jnp.int32, (n, n), 0) <= lax.broadcasted_iota(jnp.int32, (n, n), 1)
    ends = jnp.dot(counts, upper.astype(F32).astype(BF16), preferred_element_type=F32)[:1]
    places = lax.broadcasted_iota(jnp.int32, (nrows, 1), 0)
    below = ends <= places.astype(F32)
    owner_of = jnp.sum(jnp.where(below, 1.0, 0.0), axis=1, keepdims=True)
    start_of = jnp.max(jnp.where(below, ends, 0.0), axis=1, keepdims=True)
    slot_of = (owner_of * cap - start_of).astype(jnp.int32) + places
    hit = lax.broadcasted_iota(jnp.int32, (nrows, nslots), 1) == slot_of
    back = jnp.dot(hit.astype(F32).astype(BF16), back_ref[...], preferred_element_type=F32)
    rowg_ref[...] = jnp.dot(
        back[:, :chans].astype(BF16), wpt_ref[...], preferred_element_type=F32
    )
    per = sums_ref.shape[1]
    rows = []
    for r in range(3 * chans // 8):
        tiles = [sums_ref[t // per, t % per] for t in range(5 * r, 5 * r + 5)]
        rows.append(jnp.concatenate(tiles, axis=1))
    sums = jnp.concatenate(rows, axis=0) * (1.0 / math.sqrt(count_all))
    for x in range(3):
        for y in range(3):
            for z in range(3):
                at = (y * 3 + x) * chans
                convg_ref[x * 9 + y * 3 + z] = sums[z * chans : (z + 1) * chans, at : at + chans]
    projg_ref[...] = psum_ref[...] * (1.0 / math.sqrt(nrows * n))


def local(ngx, ngy, particles, send_counts, cell_lists, base_field, proj_weight, conv_weight, cotangent):
    n = ngx * ngy
    nrows, feats = particles.shape
    chans, _, cy, nz = base_field.shape
    nslots = cell_lists.shape[1]
    full = chans * cy
    cap = nslots // n
    per = 128 // n
    weight_t = proj_weight.T
    dma = pltpu.SemaphoreType.DMA
    vmem = pl.BlockSpec(memory_space=pltpu.VMEM)
    plane = (cy, chans, nz)
    out, back, sums, psum = pl.pallas_call(
        functools.partial(kernel, ngx, ngy),
        out_shape=(
            jax.ShapeDtypeStruct((full, nz), BF16),
            jax.ShapeDtypeStruct((nslots, feats), BF16),
            jax.ShapeDtypeStruct((120 // per, per, 8, 128), F32),
            jax.ShapeDtypeStruct((chans, feats), F32),
        ),
        in_specs=[vmem] * 3 + [pl.BlockSpec(memory_space=pl.ANY)] * 3 + [vmem],
        out_specs=[vmem] * 4,
        scratch_shapes=[
            pltpu.VMEM((full, nz), BF16),
            pltpu.VMEM((full, nz), BF16),
            pltpu.VMEM((27, chans, chans), BF16),
            dma((3,)),
            pltpu.VMEM((n, cap, feats), BF16),
            pltpu.VMEM((n, cap, feats), BF16),
            pltpu.VMEM((cy, chans, nslots), BF16),
            pltpu.VMEM((3, nz, nslots), BF16),
            pltpu.VMEM((full, full), BF16),
            pltpu.VMEM((full, full), BF16),
            pltpu.VMEM((3 * chans, N_TAPS * chans), BF16),
            pltpu.VMEM((N_TAPS * chans, 3 * chans), BF16),
            pltpu.VMEM(plane, BF16),
            pltpu.VMEM(plane, BF16),
            pltpu.VMEM(plane, BF16),
            pltpu.VMEM((cy + 2, 3, chans, nz), BF16),
            pltpu.VMEM((cy + 2, chans, nz), BF16),
            pltpu.VMEM((4, cy, chans, nz), BF16),
            pltpu.VMEM((2, 1, nslots), jnp.int32),
            pltpu.VMEM((2, chans, nslots), BF16),
            pltpu.VMEM((2, chans, nslots), BF16),
            pltpu.VMEM((3 * chans, 640), F32),
            pltpu.VMEM((2, n // 2, per, 8, 128), F32),
            pltpu.VMEM((n // 2, per, 8, 128), F32),
            pltpu.VMEM((n // 2, per, 8, 128), F32),
            pltpu.VMEM((n, per, 8, 128), F32),
            pltpu.VMEM((8 // per, per, 8, 128), F32),
            pltpu.VMEM((n, per, 8, 128), F32),
            pltpu.VMEM((n, cap, feats), BF16),
            pltpu.VMEM((n, cap, feats), BF16),
            dma((2,)),
            dma((2,)),
            dma((2, 2)),
            dma((2, 2)),
            dma((2,)),
            dma((2,)),
            dma((2,)),
            dma((2,)),
            dma((4, 2)),
            dma((4, 2)),
            dma((2, 3)),
            dma((2, 3)),
            dma((2,)),
            dma((2,)),
        ],
        compiler_params=pltpu.CompilerParams(
            collective_id=0, has_side_effects=True, vmem_limit_bytes=60 * 1024 * 1024
        ),
        name="section",
    )(
        send_counts,
        cell_lists,
        particles,
        base_field.reshape(full, nz),
        cotangent.reshape(full, nz),
        conv_weight,
        weight_t,
    )
    out_field, row_grads, conv_grad, proj_t = pl.pallas_call(
        functools.partial(ending, cy * nz * n),
        out_shape=(
            jax.ShapeDtypeStruct((full, nz), BF16),
            jax.ShapeDtypeStruct((nrows, feats), F32),
            jax.ShapeDtypeStruct((27, chans, chans), F32),
            jax.ShapeDtypeStruct((chans, feats), F32),
        ),
        in_specs=[vmem] * 6,
        out_specs=[vmem] * 4,
        compiler_params=pltpu.CompilerParams(vmem_limit_bytes=60 * 1024 * 1024),
        name="ending",
    )(send_counts, back, sums, psum, out, weight_t)
    return out_field.reshape(base_field.shape), row_grads, conv_grad, proj_t.T


def solution(mesh):
    in_specs = (
        P(("gx", "gy"), None),
        P(("gx", "gy"), None),
        P(("gx", "gy"), None),
        P(None, "gx", "gy", None),
        P(),
        P(),
        P(None, "gx", "gy", None),
    )
    out_specs = (P(None, "gx", "gy", None), P(("gx", "gy"), None), P(), P())
    body = functools.partial(local, mesh.shape["gx"], mesh.shape["gy"])
    return jax.shard_map(body, mesh=mesh, in_specs=in_specs, out_specs=out_specs, check_vma=False)
```

```python
import functools
import math

import jax
import jax.numpy as jnp
from jax import lax
from jax.experimental import pallas as pl
from jax.experimental.pallas import tpu as pltpu
from jax.sharding import PartitionSpec as P

MESH = pl.DeviceIdType.MESH
FLAT = pl.DeviceIdType.LOGICAL
F32 = jnp.float32
BF16 = jnp.bfloat16

F_CHUNKS = ((0, 4), (12, 4), (4, 3), (7, 3), (10, 2))
F_ROWS = ((0, 3), (13, 3), (3, 3), (6, 3), (9, 4))
G_ROWS = ((), (), (1, 2, 3, 4, 14), (5, 6, 7, 0, 15), (8, 9, 10, 11, 12, 13))
EARLY = ((0, 4), (4, 4), (14, 2))
LATE = ((8, 3), (11, 3))
N_TAPS = 9


def nt_dot(a, b):
    return lax.dot_general(a, b, (((1,), (1,)), ((), ())), preferred_element_type=F32)


def roll_z(x, shift):
    return pltpu.roll(x, shift % x.shape[1], 1)


def kernel(
    ngx,
    ngy,
    counts_ref,
    cells_ref,
    rows_ref,
    base_hbm,
    cot_hbm,
    taps_hbm,
    wpt_ref,
    out_ref,
    rowg_ref,
    sums_ref,
    psum_ref,
    base_ref,
    cot_ref,
    taps_ref,
    load_sem,
    send,
    arr,
    onehot_t,
    paint_a,
    paint_b,
    perm,
    perm_back,
    wf,
    wb,
    base,
    cot,
    outs,
    fld,
    pgr,
    grads,
    near_cells,
    near_out,
    near_in,
    acc,
    tiles,
    pair_in,
    rs,
    ag,
    ptiles,
    prs,
    pag,
    sgs,
    sgr,
    a2a_sem,
    rev_sem,
    cell_sem,
    near_sem,
    pair_sem,
    rs_sem,
    ag_sem,
    prs_sem,
    pag_sem,
    share_sem,
    fx_send,
    fx_recv,
    fy_send,
    fy_recv,
    gy_send,
    gy_recv,
):
    n = ngx * ngy
    nrows, feats = rows_ref.shape
    cy, chans, nz = base.shape
    nslots = cells_ref.shape[1]
    cap = nslots // n
    per = tiles.shape[2]
    half = n // 2
    gi = lax.axis_index("gx")
    gj = lax.axis_index("gy")
    me = gi * ngy + gj

    low = 2 if ngx >= 8 else 1
    dims = (ngx // (4 * low), 4, ngy // 2 * low, 2)
    core = gj % 2
    chip = me // 2
    at = (gi // (4 * low), gi % 4, gj // 2 * low + gi // 4 % low, core)
    moved = [[(at[a] + d) % dims[a] for d in range(dims[a])] for a in range(4)]
    places = [
        [v * (4 * low * ngy) for v in moved[0]],
        [v * ngy for v in moved[1]],
        [v % low * (4 * ngy) + v // low * 2 for v in moved[2]],
        moved[3],
    ]
    steps = [
        (a, b, c, d)
        for a in range(dims[0])
        for b in range(dims[1])
        for c in range(dims[2])
        for d in range(dims[3])
        if (a, b, c, d) != (0, 0, 0, 0)
    ]

    def hops(step):
        return -sum(min(v, size - v) for v, size in zip(step[:3], dims)), -step[3]

    steps.sort(key=hops)
    chips = [
        [places[0][a] + places[1][b] for b in range(dims[1])] for a in range(dims[0])
    ]
    ends = [[places[2][c] + places[3][d] for d in range(2)] for c in range(dims[2])]
    peers = [(chips[a][b] + ends[c][d], d) for a, b, c, d in steps]

    def beside(b):
        return (lax.rem(gi + b + ngx, ngx), gj)

    barrier = pltpu.get_barrier_semaphore()

    for peer, _ in peers:
        pl.semaphore_signal(barrier, inc=1, device_id=peer, device_id_type=FLAT)

    loads = [
        pltpu.make_async_copy(src, dst, load_sem.at[j])
        for j, (src, dst) in enumerate(
            ((base_hbm, base_ref), (taps_hbm, taps_ref), (cot_hbm, cot_ref))
        )
    ]
    for load in loads:
        load.start()

    counts = counts_ref[...].astype(F32)
    lane = lax.broadcasted_iota(jnp.int32, (nslots, n), 1)
    slot = lax.broadcasted_iota(jnp.int32, (nslots, 1), 0)
    owner = slot // cap
    offs = jnp.sum(jnp.where(lane < owner, counts, 0.0), axis=1, keepdims=True)
    mine = jnp.sum(jnp.where(lane == owner, counts, 0.0), axis=1, keepdims=True)
    place = slot - owner * cap
    index = jnp.where(place < mine.astype(jnp.int32), offs.astype(jnp.int32) + place, -1)
    pick = lax.broadcasted_iota(jnp.int32, (nslots, nrows), 1) == index
    outgoing = jnp.dot(pick.astype(F32).astype(BF16), rows_ref[...], preferred_element_type=F32)
    send[...] = outgoing.astype(BF16).reshape(send.shape)

    pl.semaphore_wait(barrier, n - 1)

    def remote(src, dst, send_sem, recv_sem, device):
        return pltpu.make_async_remote_copy(
            src_ref=src,
            dst_ref=dst,
            send_sem=send_sem,
            recv_sem=recv_sem,
            device_id=device,
            device_id_type=MESH if isinstance(device, tuple) else FLAT,
        )

    def spread(src, dst, sems):
        for peer, _ in peers:
            remote(src.at[peer], dst.at[me], sems.at[0], sems.at[1], peer).start()
        dst[pl.ds(me, 1)] = src[pl.ds(me, 1)]

    def waits(src, dst, sems, count):
        part = pl.ds(0, count)
        return remote(src.at[part], dst.at[part], sems.at[0], sems.at[1], peers[0][0])

    spread(send, arr, a2a_sem)
    cell_copies = [
        remote(
            cells_ref,
            near_cells.at[(1 - b) // 2],
            cell_sem.at[0, (1 - b) // 2],
            cell_sem.at[1, (1 - b) // 2],
            beside(b),
        )
        for b in (-1, 1)
    ]
    for copy in cell_copies:
        copy.start()

    def at_depth(cells):
        hit = lax.broadcasted_iota(jnp.int32, (nz, nslots), 0) == cells % nz
        return hit.astype(F32).astype(BF16)

    cell_y = cells_ref[...] // nz
    paint_b[0] = at_depth(cells_ref[...])
    full = cy * chans
    row = lax.broadcasted_iota(jnp.int32, (full, 1), 0)
    col = lax.broadcasted_iota(jnp.int32, (full, full), 1)
    perm[...] = (col == (row % chans) * cy + row // chans).astype(F32).astype(BF16)
    for load in loads:
        load.wait()
    base[...] = (
        jnp.dot(perm[...], base_ref[...], preferred_element_type=F32).astype(BF16).reshape(base.shape)
    )
    cot[...] = (
        jnp.dot(perm[...], cot_ref[...], preferred_element_type=F32).astype(BF16).reshape(cot.shape)
    )
    for x in range(3):
        for y in range(3):
            for z in range(3):
                tap = taps_ref[x * 9 + y * 3 + z]
                at = (y * 3 + x) * chans
                wf[z * chans : (z + 1) * chans, at : at + chans] = tap
                at = (x * 3 + 2 - z) * chans
                side = (2 - y) * chans
                wb[at : at + chans, side : side + chans] = tap.astype(F32).T.astype(BF16)
    acc[...] = jnp.zeros_like(acc)
    upper = lax.broadcasted_iota(jnp.int32, (n, n), 0) <= lax.broadcasted_iota(jnp.int32, (n, n), 1)
    ends_at = jnp.dot(
        jnp.broadcast_to(counts, (8, n)).astype(BF16),
        upper.astype(F32).astype(BF16),
        preferred_element_type=F32,
    )[:1]
    order = lax.broadcasted_iota(jnp.int32, (nrows, 1), 0)
    below = ends_at <= order.astype(F32)
    owner_of = jnp.sum(jnp.where(below, 1.0, 0.0), axis=1, keepdims=True)
    start_of = jnp.max(jnp.where(below, ends_at, 0.0), axis=1, keepdims=True)
    slot_of = (owner_of * cap - start_of).astype(jnp.int32) + order
    hit = lax.broadcasted_iota(jnp.int32, (nrows, nslots), 1) == slot_of
    onehot_t[...] = hit.astype(F32).astype(BF16)
    perm_back[...] = (col == (row % cy) * chans + row // cy).astype(F32).astype(BF16)

    waits(send, arr, a2a_sem, n - 1).wait_recv()

    arrived = arr[...].reshape(nslots, feats)
    projected = nt_dot(wpt_ref[...], arrived).astype(BF16).astype(F32)
    def edge_copy(side, b):
        to = (lax.rem(gi + b + ngx, ngx), lax.rem(gj + (1 if side == 0 else ngy - 1), ngy))
        row = cy if side == 0 else 1
        dst = 0 if side == 0 else cy + 1
        sem = (side, 1 - b)
        return remote(fld.at[row, 1], fld.at[dst, 1 - b], fy_send.at[sem], fy_recv.at[sem], to)

    def grad_edge(side):
        to = (gi, lax.rem(gj + (1 if side == 0 else ngy - 1), ngy))
        row = cy if side == 0 else 1
        dst = 0 if side == 0 else cy + 1
        return remote(pgr.at[row], pgr.at[dst], gy_send.at[side], gy_recv.at[side], to)

    def plane_copy(c, first, count, b):
        rows = pl.ds(first + 1, count)
        sem = (c, (1 - b) // 2)
        return remote(
            fld.at[rows, 1], fld.at[rows, 1 - b], fx_send.at[sem], fx_recv.at[sem], beside(b)
        )

    f_planes = [
        [plane_copy(c, first, count, b) for b in (-1, 1)]
        for c, (first, count) in enumerate(F_CHUNKS)
    ]
    f_edges = [[edge_copy(side, b) for b in (-1, 0, 1)] for side in (0, 1)]
    g_edges = [grad_edge(side) for side in (0, 1)]

    for c, (first, count) in enumerate(F_CHUNKS):
        rows = slice(first, first + count)
        for y in range(first, first + count):
            paint_a[y] = jnp.where(cell_y == y, projected, 0.0).astype(BF16)
        painted = nt_dot(paint_a[rows].reshape(count * chans, nslots), paint_b[0])
        painted = painted.reshape(count, chans, nz)
        fld[first + 1 : first + count + 1, 1] = (base[rows].astype(F32) + painted).astype(BF16)
        if first == 0:
            for copy in f_edges[1]:
                copy.start()
        if first + count == cy:
            for copy in f_edges[0]:
                copy.start()
        for copy in f_planes[c]:
            copy.start()

    for copy in cell_copies:
        copy.wait()
    near_y = [near_cells[e] // nz for e in (0, 1)]
    for e in (0, 1):
        paint_b[1 + e] = at_depth(near_cells[e])

    def backward_row(y):
        slab = pgr[y : y + 3].reshape(3 * chans, nz)
        part = jnp.dot(wb[...], slab, preferred_element_type=F32)
        for x in range(3):
            p = part[3 * x * chans : 3 * (x + 1) * chans]
            got = roll_z(p[:chans], 1) + p[chans : 2 * chans] + roll_z(p[2 * chans :], -1)
            if x == 1:
                got = got + cot[y].astype(F32)
                high = got.astype(BF16)
                grads[3, y] = (got - high.astype(F32)).astype(BF16)
                grads[1, y] = high
            else:
                grads[x, y] = got.astype(BF16)

    def tap_terms(slabs, threes):
        acc[:, : N_TAPS * chans] += nt_dot(
            jnp.concatenate(threes, axis=1), jnp.concatenate(slabs, axis=1)
        )

    def at_slots(which, depth, ys, total, ranges):
        for first, count in ranges:
            rows = grads[which, first : first + count].reshape(count * chans, nz)
            got = jnp.dot(rows, paint_b[depth], preferred_element_type=F32)
            for y in range(count):
                part = got[y * chans : (y + 1) * chans]
                total = total + jnp.where(ys == first + y, part, 0.0)
        return total

    zero = jnp.zeros((chans, nslots), F32)
    late_slabs, late_threes = [], []
    for c, (first, count) in enumerate(F_ROWS):
        for copy in f_planes[c]:
            copy.wait_recv()
        if c < 2:
            for copy in f_edges[c]:
                copy.wait_recv()
        slabs, threes = [], []
        for y in range(first, first + count):
            slab = fld[y : y + 3].reshape(N_TAPS * chans, nz)
            part = jnp.dot(wf[...], slab, preferred_element_type=F32)
            pre = roll_z(part[:chans], 1) + part[chans : 2 * chans] + roll_z(part[2 * chans :], -1)
            sig = jax.nn.sigmoid(pre)
            outs[y] = (fld[y + 1, 1].astype(F32) + pre * sig).astype(BF16)
            grad = (cot[y].astype(F32) * sig * (1.0 + pre * (1.0 - sig))).astype(BF16)
            pgr[y + 1] = grad
            wide = grad.astype(F32)
            three = jnp.concatenate([roll_z(wide, -1), wide, roll_z(wide, 1)], axis=0)
            slabs.append(slab)
            threes.append(three.astype(BF16))
        if c < 2:
            g_edges[1 - c].start()
        if c < 3:
            tap_terms(slabs, threes)
        else:
            late_slabs += slabs
            late_threes += threes
        if c == 3:
            for copy in g_edges:
                copy.wait_recv()
        for y in G_ROWS[c]:
            backward_row(y)
        if c == 3:
            sums = [at_slots(2 * e, 1 + e, near_y[e], zero, EARLY) for e in (0, 1)]

    near_copies = []
    for e, b in ((0, -1), (1, 1)):
        near_out[e] = at_slots(2 * e, 1 + e, near_y[e], sums[e], LATE).astype(BF16)
        copy = remote(
            near_out.at[e], near_in.at[1 - e], near_sem.at[0, e], near_sem.at[1, 1 - e], beside(b)
        )
        copy.start()
        near_copies.append(copy)

    tap_terms(late_slabs, late_threes)
    per_row = acc.shape[1] // 128
    proj_shares = 8 // per
    stride = n // proj_shares
    proj_at = [stride * m + 5 * (m % 4) for m in range(proj_shares)]
    conv_at = [d for d in range(n) if d not in proj_at]
    for t in range(120):
        r, q = divmod(t, per_row)
        d = conv_at[t // per]
        tiles[d % 2, d // 2, t % per] = acc[8 * r : 8 * r + 8, 128 * q : 128 * q + 128]
    for d in proj_at:
        tiles[d % 2, d // 2] = jnp.zeros((per, 8, 128), F32)
    pair_copy = remote(
        tiles.at[1 - core], pair_in, pair_sem.at[0], pair_sem.at[1], me + 1 - 2 * core
    )
    pair_copy.start()
    slot_grad = at_slots(3, 0, cell_y, zero, EARLY + LATE)
    slot_grad = at_slots(1, 0, cell_y, slot_grad, EARLY + LATE)
    pair_copy.wait()
    tiles[pl.ds(core, 1)] = tiles[pl.ds(core, 1)] + pair_in[...][None]
    for peer, d in peers:
        if d == 0:
            remote(
                tiles.at[core, peer // 2], rs.at[chip], rs_sem.at[0], rs_sem.at[1], peer
            ).start()

    out_ref[...] = jnp.dot(
        perm_back[...], outs[...].reshape(full, nz), preferred_element_type=F32
    ).astype(BF16)

    for copy in near_copies:
        copy.wait()
    slot_grad = slot_grad + near_in[0].astype(F32) + near_in[1].astype(F32)

    slot_grad = slot_grad.astype(BF16)
    wide = jnp.concatenate([slot_grad.astype(F32), jnp.zeros((feats - chans, nslots), F32)], axis=0)
    sgs[...] = wide.T.astype(BF16).reshape(sgs.shape)
    spread(sgs, sgr, rev_sem)
    proj_part = jnp.dot(slot_grad, arrived, preferred_element_type=F32)
    for t in range(8):
        ptiles[t // per, t % per] = proj_part[8 * t : 8 * t + 8]
    group = me // stride
    proj_owner = me % stride == 5 * (group % 4)
    for m, d in enumerate(proj_at):

        @pl.when(me != d)
        def _(m=m, d=d):
            remote(ptiles.at[m], prs.at[me], prs_sem.at[0], prs_sem.at[1], d).start()

    waits(rs, rs, rs_sem, half - 1).wait_recv()
    rs[pl.ds(chip, 1)] = tiles[core, pl.ds(chip, 1)]
    ag[core, pl.ds(chip, 1)] = jnp.sum(rs[...], axis=0, keepdims=True)
    there = ag.at[core, chip]
    for peer, d in peers:
        if d == 0:
            remote(there, there, ag_sem.at[0], ag_sem.at[1], peer).start()

    @pl.when(proj_owner)
    def _():
        waits(prs, prs, prs_sem, n - 1).wait_recv()
        prs[pl.ds(me, 1)] = ptiles[pl.ds(group, 1)]
        pag[pl.ds(group, 1)] = jnp.sum(prs[...], axis=0, keepdims=True)
        for peer, _ in peers:
            remote(pag.at[group], pag.at[group], pag_sem.at[0], pag_sem.at[1], peer).start()

    waits(rs, rs, ag_sem, half - 1).wait_recv()
    share_copy = remote(
        ag.at[core], ag.at[core], share_sem.at[0], share_sem.at[1], me + 1 - 2 * core
    )
    share_copy.start()
    waits(sgs, sgr, rev_sem, n - 1).wait_recv()
    back = sgr[...].reshape(nslots, feats)
    back = jnp.dot(onehot_t[...], back, preferred_element_type=F32)
    rowg_ref[...] = jnp.dot(
        back[:, :chans].astype(BF16), wpt_ref[...], preferred_element_type=F32
    )
    remote(
        ag.at[core], ag.at[1 - core], share_sem.at[0], share_sem.at[1], me + 1 - 2 * core
    ).wait()
    for t in range(120):
        d = conv_at[t // per]
        sums_ref[t // per, t % per] = ag[d % 2, d // 2, t % per]

    @pl.when(proj_owner)
    def _():
        waits(prs, prs, pag_sem, n - 1).wait_send()
        if proj_shares > 1:
            waits(ptiles, ptiles, prs_sem, proj_shares - 1).wait_send()
            waits(ptiles, ptiles, pag_sem, proj_shares - 1).wait_recv()

    @pl.when(jnp.logical_not(proj_owner))
    def _():
        waits(ptiles, ptiles, prs_sem, proj_shares).wait_send()
        waits(ptiles, ptiles, pag_sem, proj_shares).wait_recv()

    for t in range(8):
        psum_ref[8 * t : 8 * t + 8] = pag[t // per, t % per]

    waits(send, arr, a2a_sem, n - 1).wait_send()
    waits(sgs, sgr, rev_sem, n - 1).wait_send()
    waits(rs, rs, rs_sem, half - 1).wait_send()
    waits(rs, rs, ag_sem, half - 1).wait_send()
    for copies in f_edges + f_planes:
        for copy in copies:
            copy.wait_send()
    for copy in g_edges:
        copy.wait_send()


def ending(conv_scale, proj_scale, rows_ref, sums_ref, psum_ref, outf_ref, out_ref, rowg_ref, convg_ref, projg_ref):
    out_ref[...] = outf_ref[...]
    rowg_ref[...] = rows_ref[...]
    per = sums_ref.shape[1]
    chans = convg_ref.shape[1]
    rows = []
    for r in range(3 * chans // 8):
        tiles = [sums_ref[t // per, t % per] for t in range(5 * r, 5 * r + 5)]
        rows.append(jnp.concatenate(tiles, axis=1))
    sums = jnp.concatenate(rows, axis=0) * conv_scale
    for x in range(3):
        for y in range(3):
            for z in range(3):
                at = (y * 3 + x) * chans
                convg_ref[x * 9 + y * 3 + z] = sums[z * chans : (z + 1) * chans, at : at + chans]
    projg_ref[...] = psum_ref[...] * proj_scale


def local(ngx, ngy, particles, send_counts, cell_lists, base_field, proj_weight, conv_weight, cotangent):
    n = ngx * ngy
    nrows, feats = particles.shape
    chans, _, cy, nz = base_field.shape
    nslots = cell_lists.shape[1]
    full = chans * cy
    cap = nslots // n
    per = 128 // n
    weight_t = proj_weight.T
    dma = pltpu.SemaphoreType.DMA
    vmem = pl.BlockSpec(memory_space=pltpu.VMEM)
    plane = (cy, chans, nz)
    out, rows, sums, psum = pl.pallas_call(
        functools.partial(kernel, ngx, ngy),
        out_shape=(
            jax.ShapeDtypeStruct((full, nz), BF16),
            jax.ShapeDtypeStruct((nrows, feats), F32),
            jax.ShapeDtypeStruct((120 // per, per, 8, 128), F32),
            jax.ShapeDtypeStruct((chans, feats), F32),
        ),
        in_specs=[vmem] * 3 + [pl.BlockSpec(memory_space=pl.ANY)] * 3 + [vmem],
        out_specs=[vmem] * 4,
        scratch_shapes=[
            pltpu.VMEM((full, nz), BF16),
            pltpu.VMEM((full, nz), BF16),
            pltpu.VMEM((27, chans, chans), BF16),
            dma((3,)),
            pltpu.VMEM((n, cap, feats), BF16),
            pltpu.VMEM((n, cap, feats), BF16),
            pltpu.VMEM((nrows, nslots), BF16),
            pltpu.VMEM((cy, chans, nslots), BF16),
            pltpu.VMEM((3, nz, nslots), BF16),
            pltpu.VMEM((full, full), BF16),
            pltpu.VMEM((full, full), BF16),
            pltpu.VMEM((3 * chans, N_TAPS * chans), BF16),
            pltpu.VMEM((N_TAPS * chans, 3 * chans), BF16),
            pltpu.VMEM(plane, BF16),
            pltpu.VMEM(plane, BF16),
            pltpu.VMEM(plane, BF16),
            pltpu.VMEM((cy + 2, 3, chans, nz), BF16),
            pltpu.VMEM((cy + 2, chans, nz), BF16),
            pltpu.VMEM((4, cy, chans, nz), BF16),
            pltpu.VMEM((2, 1, nslots), jnp.int32),
            pltpu.VMEM((2, chans, nslots), BF16),
            pltpu.VMEM((2, chans, nslots), BF16),
            pltpu.VMEM((3 * chans, 640), F32),
            pltpu.VMEM((2, n // 2, per, 8, 128), F32),
            pltpu.VMEM((n // 2, per, 8, 128), F32),
            pltpu.VMEM((n // 2, per, 8, 128), F32),
            pltpu.VMEM((2, n // 2, per, 8, 128), F32),
            pltpu.VMEM((8 // per, per, 8, 128), F32),
            pltpu.VMEM((n, per, 8, 128), F32),
            pltpu.VMEM((8 // per, per, 8, 128), F32),
            pltpu.VMEM((n, cap, feats), BF16),
            pltpu.VMEM((n, cap, feats), BF16),
            dma((2,)),
            dma((2,)),
            dma((2, 2)),
            dma((2, 2)),
            dma((2,)),
            dma((2,)),
            dma((2,)),
            dma((2,)),
            dma((2,)),
            dma((2,)),
            dma((5, 2)),
            dma((5, 2)),
            dma((2, 3)),
            dma((2, 3)),
            dma((2,)),
            dma((2,)),
        ],
        compiler_params=pltpu.CompilerParams(
            collective_id=0, has_side_effects=True, vmem_limit_bytes=60 * 1024 * 1024
        ),
        name="section",
    )(
        send_counts,
        cell_lists,
        particles,
        base_field.reshape(full, nz),
        cotangent.reshape(full, nz),
        conv_weight,
        weight_t,
    )
    out_field, row_grads, conv_grad, proj_t = pl.pallas_call(
        functools.partial(ending, 1.0 / math.sqrt(cy * nz * n), 1.0 / math.sqrt(nrows * n)),
        out_shape=(
            jax.ShapeDtypeStruct((full, nz), BF16),
            jax.ShapeDtypeStruct((nrows, feats), F32),
            jax.ShapeDtypeStruct((27, chans, chans), F32),
            jax.ShapeDtypeStruct((chans, feats), F32),
        ),
        in_specs=[vmem] * 4,
        out_specs=[vmem] * 4,
        compiler_params=pltpu.CompilerParams(vmem_limit_bytes=60 * 1024 * 1024),
        name="ending",
    )(rows, sums, psum, out)
    return out_field.reshape(base_field.shape), row_grads, conv_grad, proj_t.T


def solution(mesh):
    in_specs = (
        P(("gx", "gy"), None),
        P(("gx", "gy"), None),
        P(("gx", "gy"), None),
        P(None, "gx", "gy", None),
        P(),
        P(),
        P(None, "gx", "gy", None),
    )
    out_specs = (P(None, "gx", "gy", None), P(("gx", "gy"), None), P(), P())
    body = functools.partial(local, mesh.shape["gx"], mesh.shape["gy"])
    return jax.shard_map(body, mesh=mesh, in_specs=in_specs, out_specs=out_specs, check_vma=False)
```

```python
import functools
import math

import jax
import jax.numpy as jnp
from jax import lax
from jax.experimental import pallas as pl
from jax.experimental.pallas import tpu as pltpu
from jax.sharding import PartitionSpec as P

MESH = pl.DeviceIdType.MESH
FLAT = pl.DeviceIdType.LOGICAL
F32 = jnp.float32
BF16 = jnp.bfloat16

F_CHUNKS = ((0, 4), (12, 4), (4, 3), (7, 3), (10, 2))
F_ROWS = ((0, 3), (13, 3), (3, 3), (6, 3), (9, 4))
G_ROWS = ((), (), (1, 2, 3, 4, 14), (5, 6, 7, 0, 15), (8, 9, 10, 11, 12, 13))
EARLY = ((0, 4), (4, 4), (14, 2))
LATE = ((8, 3), (11, 3))
N_TAPS = 9


def nt_dot(a, b):
    return lax.dot_general(a, b, (((1,), (1,)), ((), ())), preferred_element_type=F32)


def roll_z(x, shift):
    return pltpu.roll(x, shift % x.shape[1], 1)


def kernel(
    ngx,
    ngy,
    counts_ref,
    cells_ref,
    rows_ref,
    base_hbm,
    cot_hbm,
    taps_hbm,
    wpt_ref,
    out_ref,
    rowg_ref,
    sums_ref,
    psum_ref,
    base_ref,
    cot_ref,
    taps_ref,
    load_sem,
    send,
    arr,
    onehot_t,
    paint_a,
    paint_b,
    perm,
    perm_back,
    wf,
    wb,
    base,
    cot,
    outs,
    fld,
    pgr,
    grads,
    near_cells,
    near_out,
    near_in,
    acc,
    tiles,
    pair_in,
    rs,
    ag,
    ptiles,
    prs,
    pag,
    sgs,
    sgr,
    a2a_sem,
    rev_sem,
    cell_sem,
    near_sem,
    pair_sem,
    rs_sem,
    ag_sem,
    prs_sem,
    pag_sem,
    share_sem,
    fx_send,
    fx_recv,
    fy_send,
    fy_recv,
    gy_send,
    gy_recv,
):
    n = ngx * ngy
    nrows, feats = rows_ref.shape
    cy, chans, nz = base.shape
    nslots = cells_ref.shape[1]
    cap = nslots // n
    per = tiles.shape[2]
    half = n // 2
    gi = lax.axis_index("gx")
    gj = lax.axis_index("gy")
    me = gi * ngy + gj

    low = 2 if ngx >= 8 else 1
    dims = (ngx // (4 * low), 4, ngy // 2 * low, 2)
    core = gj % 2
    chip = me // 2
    at = (gi // (4 * low), gi % 4, gj // 2 * low + gi // 4 % low, core)
    moved = [[(at[a] + d) % dims[a] for d in range(dims[a])] for a in range(4)]
    places = [
        [v * (4 * low * ngy) for v in moved[0]],
        [v * ngy for v in moved[1]],
        [v % low * (4 * ngy) + v // low * 2 for v in moved[2]],
        moved[3],
    ]
    steps = [
        (a, b, c, d)
        for a in range(dims[0])
        for b in range(dims[1])
        for c in range(dims[2])
        for d in range(dims[3])
        if (a, b, c, d) != (0, 0, 0, 0)
    ]

    def hops(step):
        return -sum(min(v, size - v) for v, size in zip(step[:3], dims)), -step[3]

    steps.sort(key=hops)
    chips = [
        [places[0][a] + places[1][b] for b in range(dims[1])] for a in range(dims[0])
    ]
    ends = [[places[2][c] + places[3][d] for d in range(2)] for c in range(dims[2])]
    peers = [(chips[a][b] + ends[c][d], d) for a, b, c, d in steps]

    def beside(b):
        return (lax.rem(gi + b + ngx, ngx), gj)

    barrier = pltpu.get_barrier_semaphore()

    for peer, _ in peers:
        pl.semaphore_signal(barrier, inc=1, device_id=peer, device_id_type=FLAT)

    loads = [
        pltpu.make_async_copy(src, dst, load_sem.at[j])
        for j, (src, dst) in enumerate(
            ((base_hbm, base_ref), (taps_hbm, taps_ref), (cot_hbm, cot_ref))
        )
    ]
    for load in loads:
        load.start()

    counts = counts_ref[...].astype(F32)
    lane = lax.broadcasted_iota(jnp.int32, (nslots, n), 1)
    slot = lax.broadcasted_iota(jnp.int32, (nslots, 1), 0)
    owner = slot // cap
    offs = jnp.sum(jnp.where(lane < owner, counts, 0.0), axis=1, keepdims=True)
    mine = jnp.sum(jnp.where(lane == owner, counts, 0.0), axis=1, keepdims=True)
    place = slot - owner * cap
    index = jnp.where(place < mine.astype(jnp.int32), offs.astype(jnp.int32) + place, -1)
    pick = lax.broadcasted_iota(jnp.int32, (nslots, nrows), 1) == index
    outgoing = jnp.dot(pick.astype(F32).astype(BF16), rows_ref[...], preferred_element_type=F32)
    send[...] = outgoing.astype(BF16).reshape(send.shape)

    pl.semaphore_wait(barrier, n - 1)

    def remote(src, dst, send_sem, recv_sem, device):
        return pltpu.make_async_remote_copy(
            src_ref=src,
            dst_ref=dst,
            send_sem=send_sem,
            recv_sem=recv_sem,
            device_id=device,
            device_id_type=MESH if isinstance(device, tuple) else FLAT,
        )

    def spread(src, dst, sems):
        for peer, _ in peers:
            remote(src.at[peer], dst.at[me], sems.at[0], sems.at[1], peer).start()
        dst[pl.ds(me, 1)] = src[pl.ds(me, 1)]

    def waits(src, dst, sems, count):
        part = pl.ds(0, count)
        return remote(src.at[part], dst.at[part], sems.at[0], sems.at[1], peers[0][0])

    spread(send, arr, a2a_sem)
    cell_copies = [
        remote(
            cells_ref,
            near_cells.at[(1 - b) // 2],
            cell_sem.at[0, (1 - b) // 2],
            cell_sem.at[1, (1 - b) // 2],
            beside(b),
        )
        for b in (-1, 1)
    ]
    for copy in cell_copies:
        copy.start()

    def at_depth(cells):
        hit = lax.broadcasted_iota(jnp.int32, (nz, nslots), 0) == cells % nz
        return hit.astype(F32).astype(BF16)

    cell_y = cells_ref[...] // nz
    paint_b[0] = at_depth(cells_ref[...])
    full = cy * chans
    row = lax.broadcasted_iota(jnp.int32, (full, 1), 0)
    col = lax.broadcasted_iota(jnp.int32, (full, full), 1)
    perm[...] = (col == (row % chans) * cy + row // chans).astype(F32).astype(BF16)
    for load in loads:
        load.wait()
    base[...] = (
        jnp.dot(perm[...], base_ref[...], preferred_element_type=F32).astype(BF16).reshape(base.shape)
    )
    cot[...] = (
        jnp.dot(perm[...], cot_ref[...], preferred_element_type=F32).astype(BF16).reshape(cot.shape)
    )
    for x in range(3):
        for y in range(3):
            for z in range(3):
                tap = taps_ref[x * 9 + y * 3 + z]
                at = (y * 3 + x) * chans
                wf[z * chans : (z + 1) * chans, at : at + chans] = tap
                at = (x * 3 + 2 - z) * chans
                side = (2 - y) * chans
                wb[at : at + chans, side : side + chans] = tap.astype(F32).T.astype(BF16)
    acc[...] = jnp.zeros_like(acc)
    upper = lax.broadcasted_iota(jnp.int32, (n, n), 0) <= lax.broadcasted_iota(jnp.int32, (n, n), 1)
    ends_at = jnp.dot(
        jnp.broadcast_to(counts, (8, n)).astype(BF16),
        upper.astype(F32).astype(BF16),
        preferred_element_type=F32,
    )[:1]
    order = lax.broadcasted_iota(jnp.int32, (nrows, 1), 0)
    below = ends_at <= order.astype(F32)
    owner_of = jnp.sum(jnp.where(below, 1.0, 0.0), axis=1, keepdims=True)
    start_of = jnp.max(jnp.where(below, ends_at, 0.0), axis=1, keepdims=True)
    slot_of = (owner_of * cap - start_of).astype(jnp.int32) + order
    hit = lax.broadcasted_iota(jnp.int32, (nrows, nslots), 1) == slot_of
    onehot_t[...] = hit.astype(F32).astype(BF16)
    perm_back[...] = (col == (row % cy) * chans + row // cy).astype(F32).astype(BF16)

    waits(send, arr, a2a_sem, n - 1).wait_recv()

    arrived = arr[...].reshape(nslots, feats)
    projected = nt_dot(wpt_ref[...], arrived).astype(BF16).astype(F32)
    def edge_copy(side, b):
        to = (lax.rem(gi + b + ngx, ngx), lax.rem(gj + (1 if side == 0 else ngy - 1), ngy))
        row = cy if side == 0 else 1
        dst = 0 if side == 0 else cy + 1
        sem = (side, 1 - b)
        return remote(fld.at[row, 1], fld.at[dst, 1 - b], fy_send.at[sem], fy_recv.at[sem], to)

    def grad_edge(side):
        to = (gi, lax.rem(gj + (1 if side == 0 else ngy - 1), ngy))
        row = cy if side == 0 else 1
        dst = 0 if side == 0 else cy + 1
        return remote(pgr.at[row], pgr.at[dst], gy_send.at[side], gy_recv.at[side], to)

    def plane_copy(c, first, count, b):
        rows = pl.ds(first + 1, count)
        sem = (c, (1 - b) // 2)
        return remote(
            fld.at[rows, 1], fld.at[rows, 1 - b], fx_send.at[sem], fx_recv.at[sem], beside(b)
        )

    f_planes = [
        [plane_copy(c, first, count, b) for b in (-1, 1)]
        for c, (first, count) in enumerate(F_CHUNKS)
    ]
    f_edges = [[edge_copy(side, b) for b in (-1, 0, 1)] for side in (0, 1)]
    g_edges = [grad_edge(side) for side in (0, 1)]

    for c, (first, count) in enumerate(F_CHUNKS):
        rows = slice(first, first + count)
        for y in range(first, first + count):
            paint_a[y] = jnp.where(cell_y == y, projected, 0.0).astype(BF16)
        painted = nt_dot(paint_a[rows].reshape(count * chans, nslots), paint_b[0])
        painted = painted.reshape(count, chans, nz)
        fld[first + 1 : first + count + 1, 1] = (base[rows].astype(F32) + painted).astype(BF16)
        if first == 0:
            for copy in f_edges[1]:
                copy.start()
        if first + count == cy:
            for copy in f_edges[0]:
                copy.start()
        for copy in f_planes[c]:
            copy.start()

    for copy in cell_copies:
        copy.wait()
    near_y = [near_cells[e] // nz for e in (0, 1)]
    for e in (0, 1):
        paint_b[1 + e] = at_depth(near_cells[e])

    def backward_row(y):
        slab = pgr[y : y + 3].reshape(3 * chans, nz)
        part = jnp.dot(wb[...], slab, preferred_element_type=F32)
        for x in range(3):
            p = part[3 * x * chans : 3 * (x + 1) * chans]
            got = roll_z(p[:chans], 1) + p[chans : 2 * chans] + roll_z(p[2 * chans :], -1)
            if x == 1:
                got = got + cot[y].astype(F32)
                high = got.astype(BF16)
                grads[3, y] = (got - high.astype(F32)).astype(BF16)
                grads[1, y] = high
            else:
                grads[x, y] = got.astype(BF16)

    def tap_terms(slabs, threes):
        acc[:, : N_TAPS * chans] += nt_dot(
            jnp.concatenate(threes, axis=1), jnp.concatenate(slabs, axis=1)
        )

    def at_slots(which, depth, ys, total, ranges):
        for first, count in ranges:
            rows = grads[which, first : first + count].reshape(count * chans, nz)
            got = jnp.dot(rows, paint_b[depth], preferred_element_type=F32)
            for y in range(count):
                part = got[y * chans : (y + 1) * chans]
                total = total + jnp.where(ys == first + y, part, 0.0)
        return total

    zero = jnp.zeros((chans, nslots), F32)
    late_slabs, late_threes = [], []
    for c, (first, count) in enumerate(F_ROWS):
        for copy in f_planes[c]:
            copy.wait_recv()
        if c < 2:
            for copy in f_edges[c]:
                copy.wait_recv()
        slabs, threes = [], []
        for y in range(first, first + count):
            slab = fld[y : y + 3].reshape(N_TAPS * chans, nz)
            part = jnp.dot(wf[...], slab, preferred_element_type=F32)
            pre = roll_z(part[:chans], 1) + part[chans : 2 * chans] + roll_z(part[2 * chans :], -1)
            sig = jax.nn.sigmoid(pre)
            outs[y] = (fld[y + 1, 1].astype(F32) + pre * sig).astype(BF16)
            grad = (cot[y].astype(F32) * sig * (1.0 + pre * (1.0 - sig))).astype(BF16)
            pgr[y + 1] = grad
            wide = grad.astype(F32)
            three = jnp.concatenate([roll_z(wide, -1), wide, roll_z(wide, 1)], axis=0)
            slabs.append(slab)
            threes.append(three.astype(BF16))
        if c < 2:
            g_edges[1 - c].start()
        if c < 2:
            tap_terms(slabs, threes)
        else:
            late_slabs += slabs
            late_threes += threes
        if c == 3:
            for copy in g_edges:
                copy.wait_recv()
        for y in G_ROWS[c]:
            backward_row(y)
        if c == 3:
            sums = [at_slots(2 * e, 1 + e, near_y[e], zero, EARLY) for e in (0, 1)]

    near_copies = []
    for e, b in ((0, -1), (1, 1)):
        near_out[e] = at_slots(2 * e, 1 + e, near_y[e], sums[e], LATE).astype(BF16)
        copy = remote(
            near_out.at[e], near_in.at[1 - e], near_sem.at[0, e], near_sem.at[1, 1 - e], beside(b)
        )
        copy.start()
        near_copies.append(copy)

    tap_terms(late_slabs, late_threes)
    per_row = acc.shape[1] // 128
    proj_shares = 8 // per
    stride = n // proj_shares
    proj_at = [stride * m + 5 * (m % 4) for m in range(proj_shares)]
    conv_at = [d for d in range(n) if d not in proj_at]
    for t in range(120):
        r, q = divmod(t, per_row)
        d = conv_at[t // per]
        tiles[d % 2, d // 2, t % per] = acc[8 * r : 8 * r + 8, 128 * q : 128 * q + 128]
    for d in proj_at:
        tiles[d % 2, d // 2] = jnp.zeros((per, 8, 128), F32)
    pair_copy = remote(
        tiles.at[1 - core], pair_in, pair_sem.at[0], pair_sem.at[1], me + 1 - 2 * core
    )
    pair_copy.start()
    slot_grad = at_slots(3, 0, cell_y, zero, EARLY + LATE)
    slot_grad = at_slots(1, 0, cell_y, slot_grad, EARLY + LATE)
    pair_copy.wait()
    tiles[pl.ds(core, 1)] = tiles[pl.ds(core, 1)] + pair_in[...][None]
    for peer, d in peers:
        if d == 0:
            remote(
                tiles.at[core, peer // 2], rs.at[chip], rs_sem.at[0], rs_sem.at[1], peer
            ).start()

    out_ref[...] = jnp.dot(
        perm_back[...], outs[...].reshape(full, nz), preferred_element_type=F32
    ).astype(BF16)

    for copy in near_copies:
        copy.wait()
    slot_grad = slot_grad + near_in[0].astype(F32) + near_in[1].astype(F32)

    slot_grad = slot_grad.astype(BF16)
    proj_part = jnp.dot(slot_grad, arrived, preferred_element_type=F32)
    for t in range(8):
        ptiles[t // per, t % per] = proj_part[8 * t : 8 * t + 8]
    group = me // stride
    proj_owner = me % stride == 5 * (group % 4)
    for m, d in enumerate(proj_at):

        @pl.when(me != d)
        def _(m=m, d=d):
            remote(ptiles.at[m], prs.at[me], prs_sem.at[0], prs_sem.at[1], d).start()

    wide = jnp.concatenate([slot_grad.astype(F32), jnp.zeros((feats - chans, nslots), F32)], axis=0)
    sgs[...] = wide.T.astype(BF16).reshape(sgs.shape)
    spread(sgs, sgr, rev_sem)

    waits(rs, rs, rs_sem, half - 1).wait_recv()
    rs[pl.ds(chip, 1)] = tiles[core, pl.ds(chip, 1)]
    ag[core, pl.ds(chip, 1)] = jnp.sum(rs[...], axis=0, keepdims=True)
    there = ag.at[core, chip]
    for peer, d in peers:
        if d == 0:
            remote(there, there, ag_sem.at[0], ag_sem.at[1], peer).start()

    @pl.when(proj_owner)
    def _():
        waits(prs, prs, prs_sem, n - 1).wait_recv()
        prs[pl.ds(me, 1)] = ptiles[pl.ds(group, 1)]
        pag[pl.ds(group, 1)] = jnp.sum(prs[...], axis=0, keepdims=True)
        for peer, _ in peers:
            remote(pag.at[group], pag.at[group], pag_sem.at[0], pag_sem.at[1], peer).start()

    waits(rs, rs, ag_sem, half - 1).wait_recv()
    share_copy = remote(
        ag.at[core], ag.at[core], share_sem.at[0], share_sem.at[1], me + 1 - 2 * core
    )
    share_copy.start()
    waits(sgs, sgr, rev_sem, n - 1).wait_recv()
    back = sgr[...].reshape(nslots, feats)
    back = jnp.dot(onehot_t[...], back, preferred_element_type=F32)
    rowg_ref[...] = jnp.dot(
        back[:, :chans].astype(BF16), wpt_ref[...], preferred_element_type=F32
    )
    remote(
        ag.at[core], ag.at[1 - core], share_sem.at[0], share_sem.at[1], me + 1 - 2 * core
    ).wait()
    for t in range(120):
        d = conv_at[t // per]
        sums_ref[t // per, t % per] = ag[d % 2, d // 2, t % per]

    @pl.when(proj_owner)
    def _():
        waits(prs, prs, pag_sem, n - 1).wait_send()
        if proj_shares > 1:
            waits(ptiles, ptiles, prs_sem, proj_shares - 1).wait_send()
            waits(ptiles, ptiles, pag_sem, proj_shares - 1).wait_recv()

    @pl.when(jnp.logical_not(proj_owner))
    def _():
        waits(ptiles, ptiles, prs_sem, proj_shares).wait_send()
        waits(ptiles, ptiles, pag_sem, proj_shares).wait_recv()

    for t in range(8):
        psum_ref[8 * t : 8 * t + 8] = pag[t // per, t % per]

    waits(send, arr, a2a_sem, n - 1).wait_send()
    waits(sgs, sgr, rev_sem, n - 1).wait_send()
    waits(rs, rs, rs_sem, half - 1).wait_send()
    waits(rs, rs, ag_sem, half - 1).wait_send()
    for copies in f_edges + f_planes:
        for copy in copies:
            copy.wait_send()
    for copy in g_edges:
        copy.wait_send()


def ending(conv_scale, proj_scale, rows_ref, sums_ref, psum_ref, outf_ref, out_ref, rowg_ref, convg_ref, projg_ref):
    out_ref[...] = outf_ref[...]
    rowg_ref[...] = rows_ref[...]
    per = sums_ref.shape[1]
    chans = convg_ref.shape[1]
    rows = []
    for r in range(3 * chans // 8):
        tiles = [sums_ref[t // per, t % per] for t in range(5 * r, 5 * r + 5)]
        rows.append(jnp.concatenate(tiles, axis=1))
    sums = jnp.concatenate(rows, axis=0) * conv_scale
    for x in range(3):
        for y in range(3):
            for z in range(3):
                at = (y * 3 + x) * chans
                convg_ref[x * 9 + y * 3 + z] = sums[z * chans : (z + 1) * chans, at : at + chans]
    projg_ref[...] = psum_ref[...] * proj_scale


def local(ngx, ngy, particles, send_counts, cell_lists, base_field, proj_weight, conv_weight, cotangent):
    n = ngx * ngy
    nrows, feats = particles.shape
    chans, _, cy, nz = base_field.shape
    nslots = cell_lists.shape[1]
    full = chans * cy
    cap = nslots // n
    per = 128 // n
    weight_t = proj_weight.T
    dma = pltpu.SemaphoreType.DMA
    vmem = pl.BlockSpec(memory_space=pltpu.VMEM)
    plane = (cy, chans, nz)
    out, rows, sums, psum = pl.pallas_call(
        functools.partial(kernel, ngx, ngy),
        out_shape=(
            jax.ShapeDtypeStruct((full, nz), BF16),
            jax.ShapeDtypeStruct((nrows, feats), F32),
            jax.ShapeDtypeStruct((120 // per, per, 8, 128), F32),
            jax.ShapeDtypeStruct((chans, feats), F32),
        ),
        in_specs=[vmem] * 3 + [pl.BlockSpec(memory_space=pl.ANY)] * 3 + [vmem],
        out_specs=[vmem] * 4,
        scratch_shapes=[
            pltpu.VMEM((full, nz), BF16),
            pltpu.VMEM((full, nz), BF16),
            pltpu.VMEM((27, chans, chans), BF16),
            dma((3,)),
            pltpu.VMEM((n, cap, feats), BF16),
            pltpu.VMEM((n, cap, feats), BF16),
            pltpu.VMEM((nrows, nslots), BF16),
            pltpu.VMEM((cy, chans, nslots), BF16),
            pltpu.VMEM((3, nz, nslots), BF16),
            pltpu.VMEM((full, full), BF16),
            pltpu.VMEM((full, full), BF16),
            pltpu.VMEM((3 * chans, N_TAPS * chans), BF16),
            pltpu.VMEM((N_TAPS * chans, 3 * chans), BF16),
            pltpu.VMEM(plane, BF16),
            pltpu.VMEM(plane, BF16),
            pltpu.VMEM(plane, BF16),
            pltpu.VMEM((cy + 2, 3, chans, nz), BF16),
            pltpu.VMEM((cy + 2, chans, nz), BF16),
            pltpu.VMEM((4, cy, chans, nz), BF16),
            pltpu.VMEM((2, 1, nslots), jnp.int32),
            pltpu.VMEM((2, chans, nslots), BF16),
            pltpu.VMEM((2, chans, nslots), BF16),
            pltpu.VMEM((3 * chans, 640), F32),
            pltpu.VMEM((2, n // 2, per, 8, 128), F32),
            pltpu.VMEM((n // 2, per, 8, 128), F32),
            pltpu.VMEM((n // 2, per, 8, 128), F32),
            pltpu.VMEM((2, n // 2, per, 8, 128), F32),
            pltpu.VMEM((8 // per, per, 8, 128), F32),
            pltpu.VMEM((n, per, 8, 128), F32),
            pltpu.VMEM((8 // per, per, 8, 128), F32),
            pltpu.VMEM((n, cap, feats), BF16),
            pltpu.VMEM((n, cap, feats), BF16),
            dma((2,)),
            dma((2,)),
            dma((2, 2)),
            dma((2, 2)),
            dma((2,)),
            dma((2,)),
            dma((2,)),
            dma((2,)),
            dma((2,)),
            dma((2,)),
            dma((5, 2)),
            dma((5, 2)),
            dma((2, 3)),
            dma((2, 3)),
            dma((2,)),
            dma((2,)),
        ],
        compiler_params=pltpu.CompilerParams(
            collective_id=0, has_side_effects=True, vmem_limit_bytes=60 * 1024 * 1024
        ),
        name="section",
    )(
        send_counts,
        cell_lists,
        particles,
        base_field.reshape(full, nz),
        cotangent.reshape(full, nz),
        conv_weight,
        weight_t,
    )
    out_field, row_grads, conv_grad, proj_t = pl.pallas_call(
        functools.partial(ending, 1.0 / math.sqrt(cy * nz * n), 1.0 / math.sqrt(nrows * n)),
        out_shape=(
            jax.ShapeDtypeStruct((full, nz), BF16),
            jax.ShapeDtypeStruct((nrows, feats), F32),
            jax.ShapeDtypeStruct((27, chans, chans), F32),
            jax.ShapeDtypeStruct((chans, feats), F32),
        ),
        in_specs=[vmem] * 4,
        out_specs=[vmem] * 4,
        compiler_params=pltpu.CompilerParams(vmem_limit_bytes=60 * 1024 * 1024),
        name="ending",
    )(rows, sums, psum, out)
    return out_field.reshape(base_field.shape), row_grads, conv_grad, proj_t.T


def solution(mesh):
    in_specs = (
        P(("gx", "gy"), None),
        P(("gx", "gy"), None),
        P(("gx", "gy"), None),
        P(None, "gx", "gy", None),
        P(),
        P(),
        P(None, "gx", "gy", None),
    )
    out_specs = (P(None, "gx", "gy", None), P(("gx", "gy"), None), P(), P())
    body = functools.partial(local, mesh.shape["gx"], mesh.shape["gy"])
    return jax.shard_map(body, mesh=mesh, in_specs=in_specs, out_specs=out_specs, check_vma=False)
```

```python
import functools
import math

import jax
import jax.numpy as jnp
from jax import lax
from jax.experimental import pallas as pl
from jax.experimental.pallas import tpu as pltpu
from jax.sharding import PartitionSpec as P

MESH = pl.DeviceIdType.MESH
FLAT = pl.DeviceIdType.LOGICAL
F32 = jnp.float32
BF16 = jnp.bfloat16

F_CHUNKS = ((0, 4), (12, 4), (4, 3), (7, 3), (10, 2))
F_ROWS = ((0, 3), (13, 3), (3, 3), (6, 3), (9, 4))
G_ROWS = ((), (), (1, 2, 3, 4, 14), (5, 6, 7, 0, 15), (8, 9, 10, 11, 12, 13))
EARLY = ((0, 4), (4, 4), (14, 2))
LATE = ((8, 3), (11, 3))
N_TAPS = 9


def nt_dot(a, b):
    return lax.dot_general(a, b, (((1,), (1,)), ((), ())), preferred_element_type=F32)


def roll_z(x, shift):
    return pltpu.roll(x, shift % x.shape[1], 1)


def kernel(
    ngx,
    ngy,
    counts_ref,
    cells_ref,
    rows_ref,
    base_hbm,
    cot_hbm,
    taps_hbm,
    wpt_ref,
    out_ref,
    rowg_ref,
    sums_ref,
    psum_ref,
    base_ref,
    cot_ref,
    taps_ref,
    load_sem,
    send,
    arr,
    onehot_t,
    paint_a,
    paint_b,
    perm,
    perm_back,
    wf,
    wb,
    base,
    cot,
    outs,
    fld,
    pgr,
    grads,
    near_cells,
    near_out,
    near_in,
    acc,
    tiles,
    pair_in,
    rs,
    ag,
    ptiles,
    prs,
    pag,
    sgs,
    sgr,
    a2a_sem,
    rev_sem,
    cell_sem,
    near_sem,
    pair_sem,
    rs_sem,
    ag_sem,
    prs_sem,
    pag_sem,
    share_sem,
    fx_send,
    fx_recv,
    fy_send,
    fy_recv,
    gy_send,
    gy_recv,
):
    n = ngx * ngy
    nrows, feats = rows_ref.shape
    cy, chans, nz = base.shape
    nslots = cells_ref.shape[1]
    cap = nslots // n
    per = tiles.shape[2]
    half = n // 2
    gi = lax.axis_index("gx")
    gj = lax.axis_index("gy")
    me = gi * ngy + gj

    low = 2 if ngx >= 8 else 1
    dims = (ngx // (4 * low), 4, ngy // 2 * low, 2)
    core = gj % 2
    chip = me // 2
    at = (gi // (4 * low), gi % 4, gj // 2 * low + gi // 4 % low, core)
    moved = [[(at[a] + d) % dims[a] for d in range(dims[a])] for a in range(4)]
    places = [
        [v * (4 * low * ngy) for v in moved[0]],
        [v * ngy for v in moved[1]],
        [v % low * (4 * ngy) + v // low * 2 for v in moved[2]],
        moved[3],
    ]
    steps = [
        (a, b, c, d)
        for a in range(dims[0])
        for b in range(dims[1])
        for c in range(dims[2])
        for d in range(dims[3])
        if (a, b, c, d) != (0, 0, 0, 0)
    ]

    def hops(step):
        return -sum(min(v, size - v) for v, size in zip(step[:3], dims)), -step[3]

    steps.sort(key=hops)
    chips = [
        [places[0][a] + places[1][b] for b in range(dims[1])] for a in range(dims[0])
    ]
    ends = [[places[2][c] + places[3][d] for d in range(2)] for c in range(dims[2])]
    peers = [(chips[a][b] + ends[c][d], d) for a, b, c, d in steps]

    def beside(b):
        return (lax.rem(gi + b + ngx, ngx), gj)

    barrier = pltpu.get_barrier_semaphore()

    for peer, _ in peers:
        pl.semaphore_signal(barrier, inc=1, device_id=peer, device_id_type=FLAT)

    loads = [
        pltpu.make_async_copy(src, dst, load_sem.at[j])
        for j, (src, dst) in enumerate(
            ((base_hbm, base_ref), (taps_hbm, taps_ref), (cot_hbm, cot_ref))
        )
    ]
    for load in loads:
        load.start()

    counts = counts_ref[...].astype(F32)
    lane = lax.broadcasted_iota(jnp.int32, (nslots, n), 1)
    slot = lax.broadcasted_iota(jnp.int32, (nslots, 1), 0)
    owner = slot // cap
    offs = jnp.sum(jnp.where(lane < owner, counts, 0.0), axis=1, keepdims=True)
    mine = jnp.sum(jnp.where(lane == owner, counts, 0.0), axis=1, keepdims=True)
    place = slot - owner * cap
    index = jnp.where(place < mine.astype(jnp.int32), offs.astype(jnp.int32) + place, -1)
    pick = lax.broadcasted_iota(jnp.int32, (nslots, nrows), 1) == index
    outgoing = jnp.dot(pick.astype(F32).astype(BF16), rows_ref[...], preferred_element_type=F32)
    send[...] = outgoing.astype(BF16).reshape(send.shape)

    pl.semaphore_wait(barrier, n - 1)

    def remote(src, dst, send_sem, recv_sem, device):
        return pltpu.make_async_remote_copy(
            src_ref=src,
            dst_ref=dst,
            send_sem=send_sem,
            recv_sem=recv_sem,
            device_id=device,
            device_id_type=MESH if isinstance(device, tuple) else FLAT,
        )

    def spread(src, dst, sems):
        for peer, _ in peers:
            remote(src.at[peer], dst.at[me], sems.at[0], sems.at[1], peer).start()
        dst[pl.ds(me, 1)] = src[pl.ds(me, 1)]

    def waits(src, dst, sems, count):
        part = pl.ds(0, count)
        return remote(src.at[part], dst.at[part], sems.at[0], sems.at[1], peers[0][0])

    spread(send, arr, a2a_sem)
    cell_copies = [
        remote(
            cells_ref,
            near_cells.at[(1 - b) // 2],
            cell_sem.at[0, (1 - b) // 2],
            cell_sem.at[1, (1 - b) // 2],
            beside(b),
        )
        for b in (-1, 1)
    ]
    for copy in cell_copies:
        copy.start()

    def at_depth(cells):
        hit = lax.broadcasted_iota(jnp.int32, (nz, nslots), 0) == cells % nz
        return hit.astype(F32).astype(BF16)

    cell_y = cells_ref[...] // nz
    paint_b[0] = at_depth(cells_ref[...])
    full = cy * chans
    row = lax.broadcasted_iota(jnp.int32, (full, 1), 0)
    col = lax.broadcasted_iota(jnp.int32, (full, full), 1)
    perm[...] = (col == (row % chans) * cy + row // chans).astype(F32).astype(BF16)
    for load in loads:
        load.wait()
    base[...] = (
        jnp.dot(perm[...], base_ref[...], preferred_element_type=F32).astype(BF16).reshape(base.shape)
    )
    cot[...] = (
        jnp.dot(perm[...], cot_ref[...], preferred_element_type=F32).astype(BF16).reshape(cot.shape)
    )
    for x in range(3):
        for y in range(3):
            for z in range(3):
                tap = taps_ref[x * 9 + y * 3 + z]
                at = (y * 3 + x) * chans
                wf[z * chans : (z + 1) * chans, at : at + chans] = tap
                at = (x * 3 + 2 - z) * chans
                side = (2 - y) * chans
                wb[at : at + chans, side : side + chans] = tap.astype(F32).T.astype(BF16)
    acc[...] = jnp.zeros_like(acc)
    upper = lax.broadcasted_iota(jnp.int32, (n, n), 0) <= lax.broadcasted_iota(jnp.int32, (n, n), 1)
    ends_at = jnp.dot(
        jnp.broadcast_to(counts, (8, n)).astype(BF16),
        upper.astype(F32).astype(BF16),
        preferred_element_type=F32,
    )[:1]
    order = lax.broadcasted_iota(jnp.int32, (nrows, 1), 0)
    below = ends_at <= order.astype(F32)
    owner_of = jnp.sum(jnp.where(below, 1.0, 0.0), axis=1, keepdims=True)
    start_of = jnp.max(jnp.where(below, ends_at, 0.0), axis=1, keepdims=True)
    slot_of = (owner_of * cap - start_of).astype(jnp.int32) + order
    hit = lax.broadcasted_iota(jnp.int32, (nrows, nslots), 1) == slot_of
    onehot_t[...] = hit.astype(F32).astype(BF16)
    perm_back[...] = (col == (row % cy) * chans + row // cy).astype(F32).astype(BF16)

    waits(send, arr, a2a_sem, n - 1).wait_recv()

    arrived = arr[...].reshape(nslots, feats)
    projected = nt_dot(wpt_ref[...], arrived).astype(BF16).astype(F32)
    def edge_copy(side, b):
        to = (lax.rem(gi + b + ngx, ngx), lax.rem(gj + (1 if side == 0 else ngy - 1), ngy))
        row = cy if side == 0 else 1
        dst = 0 if side == 0 else cy + 1
        sem = (side, 1 - b)
        return remote(fld.at[row, 1], fld.at[dst, 1 - b], fy_send.at[sem], fy_recv.at[sem], to)

    def grad_edge(side):
        to = (gi, lax.rem(gj + (1 if side == 0 else ngy - 1), ngy))
        row = cy if side == 0 else 1
        dst = 0 if side == 0 else cy + 1
        return remote(pgr.at[row], pgr.at[dst], gy_send.at[side], gy_recv.at[side], to)

    def plane_copy(c, first, count, b):
        rows = pl.ds(first + 1, count)
        sem = (c, (1 - b) // 2)
        return remote(
            fld.at[rows, 1], fld.at[rows, 1 - b], fx_send.at[sem], fx_recv.at[sem], beside(b)
        )

    f_planes = [
        [plane_copy(c, first, count, b) for b in (-1, 1)]
        for c, (first, count) in enumerate(F_CHUNKS)
    ]
    f_edges = [[edge_copy(side, b) for b in (-1, 0, 1)] for side in (0, 1)]
    g_edges = [grad_edge(side) for side in (0, 1)]

    for c, (first, count) in enumerate(F_CHUNKS):
        rows = slice(first, first + count)
        for y in range(first, first + count):
            paint_a[y] = jnp.where(cell_y == y, projected, 0.0).astype(BF16)
        painted = nt_dot(paint_a[rows].reshape(count * chans, nslots), paint_b[0])
        painted = painted.reshape(count, chans, nz)
        fld[first + 1 : first + count + 1, 1] = (base[rows].astype(F32) + painted).astype(BF16)
        if first == 0:
            for copy in f_edges[1]:
                copy.start()
        if first + count == cy:
            for copy in f_edges[0]:
                copy.start()
        for copy in f_planes[c]:
            copy.start()

    for copy in cell_copies:
        copy.wait()
    near_y = [near_cells[e] // nz for e in (0, 1)]
    for e in (0, 1):
        paint_b[1 + e] = at_depth(near_cells[e])

    def backward_row(y):
        slab = pgr[y : y + 3].reshape(3 * chans, nz)
        part = jnp.dot(wb[...], slab, preferred_element_type=F32)
        for x in range(3):
            p = part[3 * x * chans : 3 * (x + 1) * chans]
            got = roll_z(p[:chans], 1) + p[chans : 2 * chans] + roll_z(p[2 * chans :], -1)
            if x == 1:
                got = got + cot[y].astype(F32)
                high = got.astype(BF16)
                grads[3, y] = (got - high.astype(F32)).astype(BF16)
                grads[1, y] = high
            else:
                grads[x, y] = got.astype(BF16)

    def tap_terms(slabs, threes):
        acc[:, : N_TAPS * chans] += nt_dot(
            jnp.concatenate(threes, axis=1), jnp.concatenate(slabs, axis=1)
        )

    def at_slots(which, depth, ys, total, ranges):
        for first, count in ranges:
            rows = grads[which, first : first + count].reshape(count * chans, nz)
            got = jnp.dot(rows, paint_b[depth], preferred_element_type=F32)
            for y in range(count):
                part = got[y * chans : (y + 1) * chans]
                total = total + jnp.where(ys == first + y, part, 0.0)
        return total

    zero = jnp.zeros((chans, nslots), F32)
    late_slabs, late_threes = [], []
    for c, (first, count) in enumerate(F_ROWS):
        for copy in f_planes[c]:
            copy.wait_recv()
        if c < 2:
            for copy in f_edges[c]:
                copy.wait_recv()
        slabs, threes = [], []
        for y in range(first, first + count):
            slab = fld[y : y + 3].reshape(N_TAPS * chans, nz)
            part = jnp.dot(wf[...], slab, preferred_element_type=F32)
            pre = roll_z(part[:chans], 1) + part[chans : 2 * chans] + roll_z(part[2 * chans :], -1)
            sig = jax.nn.sigmoid(pre)
            outs[y] = (fld[y + 1, 1].astype(F32) + pre * sig).astype(BF16)
            grad = (cot[y].astype(F32) * sig * (1.0 + pre * (1.0 - sig))).astype(BF16)
            pgr[y + 1] = grad
            wide = grad.astype(F32)
            three = jnp.concatenate([roll_z(wide, -1), wide, roll_z(wide, 1)], axis=0)
            slabs.append(slab)
            threes.append(three.astype(BF16))
        if c < 2:
            g_edges[1 - c].start()
        if c < 2:
            tap_terms(slabs, threes)
        else:
            late_slabs += slabs
            late_threes += threes
        if c == 3:
            for copy in g_edges:
                copy.wait_recv()
        for y in G_ROWS[c]:
            backward_row(y)
        if c == 3:
            sums = [at_slots(2 * e, 1 + e, near_y[e], zero, EARLY) for e in (0, 1)]

    near_copies = []
    for e, b in ((0, -1), (1, 1)):
        near_out[e] = at_slots(2 * e, 1 + e, near_y[e], sums[e], LATE).astype(BF16)
        copy = remote(
            near_out.at[e], near_in.at[1 - e], near_sem.at[0, e], near_sem.at[1, 1 - e], beside(b)
        )
        copy.start()
        near_copies.append(copy)

    tap_terms(late_slabs, late_threes)
    per_row = acc.shape[1] // 128
    proj_shares, prow, _ = ptiles.shape
    stride = n // proj_shares
    proj_at = [stride * m + m % stride for m in range(proj_shares)]
    for t in range(120):
        r, q = divmod(t, per_row)
        d = t // per
        tiles[d % 2, d // 2, t % per] = acc[8 * r : 8 * r + 8, 128 * q : 128 * q + 128]
    for d in range(120 // per, n):
        tiles[d % 2, d // 2] = jnp.zeros((per, 8, 128), F32)
    pair_copy = remote(
        tiles.at[1 - core], pair_in, pair_sem.at[0], pair_sem.at[1], me + 1 - 2 * core
    )
    pair_copy.start()
    slot_grad = at_slots(3, 0, cell_y, zero, EARLY + LATE)
    slot_grad = at_slots(1, 0, cell_y, slot_grad, EARLY + LATE)
    pair_copy.wait()
    tiles[pl.ds(core, 1)] = tiles[pl.ds(core, 1)] + pair_in[...][None]
    for peer, d in peers:
        if d == 0:
            remote(
                tiles.at[core, peer // 2], rs.at[chip], rs_sem.at[0], rs_sem.at[1], peer
            ).start()

    out_ref[...] = jnp.dot(
        perm_back[...], outs[...].reshape(full, nz), preferred_element_type=F32
    ).astype(BF16)

    for copy in near_copies:
        copy.wait()
    slot_grad = slot_grad + near_in[0].astype(F32) + near_in[1].astype(F32)

    slot_grad = slot_grad.astype(BF16)
    proj_part = jnp.dot(slot_grad, arrived, preferred_element_type=F32)
    for m in range(proj_shares):
        ptiles[m] = proj_part[prow * m : prow * m + prow]
    group = me // stride
    proj_owner = me % stride == group % stride
    for m, d in enumerate(proj_at):

        @pl.when(me != d)
        def _(m=m, d=d):
            remote(ptiles.at[m], prs.at[me], prs_sem.at[0], prs_sem.at[1], d).start()

    wide = jnp.concatenate([slot_grad.astype(F32), jnp.zeros((feats - chans, nslots), F32)], axis=0)
    sgs[...] = wide.T.astype(BF16).reshape(sgs.shape)
    spread(sgs, sgr, rev_sem)

    waits(rs, rs, rs_sem, half - 1).wait_recv()
    rs[pl.ds(chip, 1)] = tiles[core, pl.ds(chip, 1)]
    ag[core, pl.ds(chip, 1)] = jnp.sum(rs[...], axis=0, keepdims=True)
    there = ag.at[core, chip]
    for peer, d in peers:
        if d == 0:
            remote(there, there, ag_sem.at[0], ag_sem.at[1], peer).start()

    @pl.when(proj_owner)
    def _():
        waits(prs, prs, prs_sem, n - 1).wait_recv()
        prs[pl.ds(me, 1)] = ptiles[pl.ds(group, 1)]
        pag[pl.ds(group, 1)] = jnp.sum(prs[...], axis=0, keepdims=True)
        for peer, _ in peers:
            remote(pag.at[group], pag.at[group], pag_sem.at[0], pag_sem.at[1], peer).start()

    waits(rs, rs, ag_sem, half - 1).wait_recv()
    share_copy = remote(
        ag.at[core], ag.at[core], share_sem.at[0], share_sem.at[1], me + 1 - 2 * core
    )
    share_copy.start()
    waits(sgs, sgr, rev_sem, n - 1).wait_recv()
    back = sgr[...].reshape(nslots, feats)
    back = jnp.dot(onehot_t[...], back, preferred_element_type=F32)
    rowg_ref[...] = jnp.dot(
        back[:, :chans].astype(BF16), wpt_ref[...], preferred_element_type=F32
    )
    remote(
        ag.at[core], ag.at[1 - core], share_sem.at[0], share_sem.at[1], me + 1 - 2 * core
    ).wait()
    for t in range(120):
        d = t // per
        sums_ref[t // per, t % per] = ag[d % 2, d // 2, t % per]

    @pl.when(proj_owner)
    def _():
        waits(prs, prs, pag_sem, n - 1).wait_send()
        if proj_shares > 1:
            waits(ptiles, ptiles, prs_sem, proj_shares - 1).wait_send()
            waits(ptiles, ptiles, pag_sem, proj_shares - 1).wait_recv()

    @pl.when(jnp.logical_not(proj_owner))
    def _():
        waits(ptiles, ptiles, prs_sem, proj_shares).wait_send()
        waits(ptiles, ptiles, pag_sem, proj_shares).wait_recv()

    for m in range(proj_shares):
        psum_ref[prow * m : prow * m + prow] = pag[m]

    waits(send, arr, a2a_sem, n - 1).wait_send()
    waits(sgs, sgr, rev_sem, n - 1).wait_send()
    waits(rs, rs, rs_sem, half - 1).wait_send()
    waits(rs, rs, ag_sem, half - 1).wait_send()
    for copies in f_edges + f_planes:
        for copy in copies:
            copy.wait_send()
    for copy in g_edges:
        copy.wait_send()


def ending(conv_scale, proj_scale, rows_ref, sums_ref, psum_ref, outf_ref, out_ref, rowg_ref, convg_ref, projg_ref):
    out_ref[...] = outf_ref[...]
    rowg_ref[...] = rows_ref[...]
    per = sums_ref.shape[1]
    chans = convg_ref.shape[1]
    rows = []
    for r in range(3 * chans // 8):
        tiles = [sums_ref[t // per, t % per] for t in range(5 * r, 5 * r + 5)]
        rows.append(jnp.concatenate(tiles, axis=1))
    sums = jnp.concatenate(rows, axis=0) * conv_scale
    for x in range(3):
        for y in range(3):
            for z in range(3):
                at = (y * 3 + x) * chans
                convg_ref[x * 9 + y * 3 + z] = sums[z * chans : (z + 1) * chans, at : at + chans]
    projg_ref[...] = psum_ref[...] * proj_scale


def local(ngx, ngy, particles, send_counts, cell_lists, base_field, proj_weight, conv_weight, cotangent):
    n = ngx * ngy
    nrows, feats = particles.shape
    chans, _, cy, nz = base_field.shape
    nslots = cell_lists.shape[1]
    full = chans * cy
    cap = nslots // n
    per = 128 // n
    pcount = min(n, 32)
    weight_t = proj_weight.T
    dma = pltpu.SemaphoreType.DMA
    vmem = pl.BlockSpec(memory_space=pltpu.VMEM)
    plane = (cy, chans, nz)
    out, rows, sums, psum = pl.pallas_call(
        functools.partial(kernel, ngx, ngy),
        out_shape=(
            jax.ShapeDtypeStruct((full, nz), BF16),
            jax.ShapeDtypeStruct((nrows, feats), F32),
            jax.ShapeDtypeStruct((120 // per, per, 8, 128), F32),
            jax.ShapeDtypeStruct((chans, feats), F32),
        ),
        in_specs=[vmem] * 3 + [pl.BlockSpec(memory_space=pl.ANY)] * 3 + [vmem],
        out_specs=[vmem] * 4,
        scratch_shapes=[
            pltpu.VMEM((full, nz), BF16),
            pltpu.VMEM((full, nz), BF16),
            pltpu.VMEM((27, chans, chans), BF16),
            dma((3,)),
            pltpu.VMEM((n, cap, feats), BF16),
            pltpu.VMEM((n, cap, feats), BF16),
            pltpu.VMEM((nrows, nslots), BF16),
            pltpu.VMEM((cy, chans, nslots), BF16),
            pltpu.VMEM((3, nz, nslots), BF16),
            pltpu.VMEM((full, full), BF16),
            pltpu.VMEM((full, full), BF16),
            pltpu.VMEM((3 * chans, N_TAPS * chans), BF16),
            pltpu.VMEM((N_TAPS * chans, 3 * chans), BF16),
            pltpu.VMEM(plane, BF16),
            pltpu.VMEM(plane, BF16),
            pltpu.VMEM(plane, BF16),
            pltpu.VMEM((cy + 2, 3, chans, nz), BF16),
            pltpu.VMEM((cy + 2, chans, nz), BF16),
            pltpu.VMEM((4, cy, chans, nz), BF16),
            pltpu.VMEM((2, 1, nslots), jnp.int32),
            pltpu.VMEM((2, chans, nslots), BF16),
            pltpu.VMEM((2, chans, nslots), BF16),
            pltpu.VMEM((3 * chans, 640), F32),
            pltpu.VMEM((2, n // 2, per, 8, 128), F32),
            pltpu.VMEM((n // 2, per, 8, 128), F32),
            pltpu.VMEM((n // 2, per, 8, 128), F32),
            pltpu.VMEM((2, n // 2, per, 8, 128), F32),
            pltpu.VMEM((pcount, chans // pcount, feats), F32),
            pltpu.VMEM((n, chans // pcount, feats), F32),
            pltpu.VMEM((pcount, chans // pcount, feats), F32),
            pltpu.VMEM((n, cap, feats), BF16),
            pltpu.VMEM((n, cap, feats), BF16),
            dma((2,)),
            dma((2,)),
            dma((2, 2)),
            dma((2, 2)),
            dma((2,)),
            dma((2,)),
            dma((2,)),
            dma((2,)),
            dma((2,)),
            dma((2,)),
            dma((5, 2)),
            dma((5, 2)),
            dma((2, 3)),
            dma((2, 3)),
            dma((2,)),
            dma((2,)),
        ],
        compiler_params=pltpu.CompilerParams(
            collective_id=0, has_side_effects=True, vmem_limit_bytes=60 * 1024 * 1024
        ),
        name="section",
    )(
        send_counts,
        cell_lists,
        particles,
        base_field.reshape(full, nz),
        cotangent.reshape(full, nz),
        conv_weight,
        weight_t,
    )
    out_field, row_grads, conv_grad, proj_t = pl.pallas_call(
        functools.partial(ending, 1.0 / math.sqrt(cy * nz * n), 1.0 / math.sqrt(nrows * n)),
        out_shape=(
            jax.ShapeDtypeStruct((full, nz), BF16),
            jax.ShapeDtypeStruct((nrows, feats), F32),
            jax.ShapeDtypeStruct((27, chans, chans), F32),
            jax.ShapeDtypeStruct((chans, feats), F32),
        ),
        in_specs=[vmem] * 4,
        out_specs=[vmem] * 4,
        compiler_params=pltpu.CompilerParams(vmem_limit_bytes=60 * 1024 * 1024),
        name="ending",
    )(rows, sums, psum, out)
    return out_field.reshape(base_field.shape), row_grads, conv_grad, proj_t.T


def solution(mesh):
    in_specs = (
        P(("gx", "gy"), None),
        P(("gx", "gy"), None),
        P(("gx", "gy"), None),
        P(None, "gx", "gy", None),
        P(),
        P(),
        P(None, "gx", "gy", None),
    )
    out_specs = (P(None, "gx", "gy", None), P(("gx", "gy"), None), P(), P())
    body = functools.partial(local, mesh.shape["gx"], mesh.shape["gy"])
    return jax.shard_map(body, mesh=mesh, in_specs=in_specs, out_specs=out_specs, check_vma=False)
```

```python
import functools
import math

import jax
import jax.numpy as jnp
from jax import lax
from jax.experimental import pallas as pl
from jax.experimental.pallas import tpu as pltpu
from jax.sharding import PartitionSpec as P

MESH = pl.DeviceIdType.MESH
FLAT = pl.DeviceIdType.LOGICAL
F32 = jnp.float32
BF16 = jnp.bfloat16

F_CHUNKS = ((0, 4), (12, 4), (4, 3), (7, 3), (10, 2))
F_ROWS = ((0, 3), (13, 3), (3, 3), (6, 3), (9, 4))
G_ROWS = ((), (), (1, 2, 3, 4, 14), (5, 6, 7, 0, 15), (8, 9, 10, 11, 12, 13))
EARLY = ((0, 4), (4, 4), (14, 2))
LATE = ((8, 3), (11, 3))
N_TAPS = 9


def nt_dot(a, b):
    return lax.dot_general(a, b, (((1,), (1,)), ((), ())), preferred_element_type=F32)


def roll_z(x, shift):
    return pltpu.roll(x, shift % x.shape[1], 1)


def kernel(
    ngx,
    ngy,
    counts_ref,
    cells_ref,
    rows_ref,
    base_hbm,
    cot_hbm,
    taps_hbm,
    wpt_ref,
    out_ref,
    rowg_ref,
    sums_ref,
    psum_ref,
    base_ref,
    cot_ref,
    taps_ref,
    load_sem,
    send,
    arr,
    onehot_t,
    paint_a,
    paint_b,
    perm,
    perm_back,
    wf,
    wb,
    base,
    cot,
    outs,
    fld,
    pgr,
    grads,
    near_cells,
    near_out,
    near_in,
    acc,
    tiles,
    pair_in,
    rs,
    ag,
    ptiles,
    prs,
    pag,
    sgs,
    sgr,
    a2a_sem,
    rev_sem,
    cell_sem,
    near_sem,
    pair_sem,
    rs_sem,
    ag_sem,
    prs_sem,
    pag_sem,
    share_sem,
    fx_send,
    fx_recv,
    fy_send,
    fy_recv,
    gy_send,
    gy_recv,
):
    n = ngx * ngy
    nrows, feats = rows_ref.shape
    cy, chans, nz = base.shape
    nslots = cells_ref.shape[1]
    cap = nslots // n
    per = tiles.shape[2]
    half = n // 2
    gi = lax.axis_index("gx")
    gj = lax.axis_index("gy")
    me = gi * ngy + gj

    low = 2 if ngx >= 8 else 1
    dims = (ngx // (4 * low), 4, ngy // 2 * low, 2)
    core = gj % 2
    chip = me // 2
    at = (gi // (4 * low), gi % 4, gj // 2 * low + gi // 4 % low, core)
    moved = [[(at[a] + d) % dims[a] for d in range(dims[a])] for a in range(4)]
    places = [
        [v * (4 * low * ngy) for v in moved[0]],
        [v * ngy for v in moved[1]],
        [v % low * (4 * ngy) + v // low * 2 for v in moved[2]],
        moved[3],
    ]
    steps = [
        (a, b, c, d)
        for a in range(dims[0])
        for b in range(dims[1])
        for c in range(dims[2])
        for d in range(dims[3])
        if (a, b, c, d) != (0, 0, 0, 0)
    ]

    def hops(step):
        return -sum(min(v, size - v) for v, size in zip(step[:3], dims)), -step[3]

    steps.sort(key=hops)
    chips = [
        [places[0][a] + places[1][b] for b in range(dims[1])] for a in range(dims[0])
    ]
    ends = [[places[2][c] + places[3][d] for d in range(2)] for c in range(dims[2])]
    peers = [(chips[a][b] + ends[c][d], d) for a, b, c, d in steps]

    def beside(b):
        return (lax.rem(gi + b + ngx, ngx), gj)

    barrier = pltpu.get_barrier_semaphore()

    for peer, _ in peers:
        pl.semaphore_signal(barrier, inc=1, device_id=peer, device_id_type=FLAT)

    loads = [
        pltpu.make_async_copy(src, dst, load_sem.at[j])
        for j, (src, dst) in enumerate(
            ((base_hbm, base_ref), (taps_hbm, taps_ref), (cot_hbm, cot_ref))
        )
    ]
    for load in loads:
        load.start()

    counts = counts_ref[...].astype(F32)
    lane = lax.broadcasted_iota(jnp.int32, (nslots, n), 1)
    slot = lax.broadcasted_iota(jnp.int32, (nslots, 1), 0)
    owner = slot // cap
    offs = jnp.sum(jnp.where(lane < owner, counts, 0.0), axis=1, keepdims=True)
    mine = jnp.sum(jnp.where(lane == owner, counts, 0.0), axis=1, keepdims=True)
    place = slot - owner * cap
    index = jnp.where(place < mine.astype(jnp.int32), offs.astype(jnp.int32) + place, -1)
    pick = lax.broadcasted_iota(jnp.int32, (nslots, nrows), 1) == index
    outgoing = jnp.dot(pick.astype(F32).astype(BF16), rows_ref[...], preferred_element_type=F32)
    send[...] = outgoing.astype(BF16).reshape(send.shape)

    pl.semaphore_wait(barrier, n - 1)

    def remote(src, dst, send_sem, recv_sem, device):
        return pltpu.make_async_remote_copy(
            src_ref=src,
            dst_ref=dst,
            send_sem=send_sem,
            recv_sem=recv_sem,
            device_id=device,
            device_id_type=MESH if isinstance(device, tuple) else FLAT,
        )

    def spread(src, dst, sems):
        for peer, _ in peers:
            remote(src.at[peer], dst.at[me], sems.at[0], sems.at[1], peer).start()
        dst[pl.ds(me, 1)] = src[pl.ds(me, 1)]

    def waits(src, dst, sems, count):
        part = pl.ds(0, count)
        return remote(src.at[part], dst.at[part], sems.at[0], sems.at[1], peers[0][0])

    spread(send, arr, a2a_sem)
    cell_copies = [
        remote(
            cells_ref,
            near_cells.at[(1 - b) // 2],
            cell_sem.at[0, (1 - b) // 2],
            cell_sem.at[1, (1 - b) // 2],
            beside(b),
        )
        for b in (-1, 1)
    ]
    for copy in cell_copies:
        copy.start()

    def at_depth(cells):
        hit = lax.broadcasted_iota(jnp.int32, (nz, nslots), 0) == cells % nz
        return hit.astype(F32).astype(BF16)

    cell_y = cells_ref[...] // nz
    paint_b[0] = at_depth(cells_ref[...])
    full = cy * chans
    row = lax.broadcasted_iota(jnp.int32, (full, 1), 0)
    col = lax.broadcasted_iota(jnp.int32, (full, full), 1)
    perm[...] = (col == (row % chans) * cy + row // chans).astype(F32).astype(BF16)
    for load in loads:
        load.wait()
    base[...] = (
        jnp.dot(perm[...], base_ref[...], preferred_element_type=F32).astype(BF16).reshape(base.shape)
    )
    cot[...] = (
        jnp.dot(perm[...], cot_ref[...], preferred_element_type=F32).astype(BF16).reshape(cot.shape)
    )
    for x in range(3):
        for y in range(3):
            for z in range(3):
                tap = taps_ref[x * 9 + y * 3 + z]
                at = (y * 3 + x) * chans
                wf[z * chans : (z + 1) * chans, at : at + chans] = tap
                at = (x * 3 + 2 - z) * chans
                side = (2 - y) * chans
                wb[at : at + chans, side : side + chans] = tap.astype(F32).T.astype(BF16)
    acc[...] = jnp.zeros_like(acc)
    upper = lax.broadcasted_iota(jnp.int32, (n, n), 0) <= lax.broadcasted_iota(jnp.int32, (n, n), 1)
    ends_at = jnp.dot(
        jnp.broadcast_to(counts, (8, n)).astype(BF16),
        upper.astype(F32).astype(BF16),
        preferred_element_type=F32,
    )[:1]
    order = lax.broadcasted_iota(jnp.int32, (nrows, 1), 0)
    below = ends_at <= order.astype(F32)
    owner_of = jnp.sum(jnp.where(below, 1.0, 0.0), axis=1, keepdims=True)
    start_of = jnp.max(jnp.where(below, ends_at, 0.0), axis=1, keepdims=True)
    slot_of = (owner_of * cap - start_of).astype(jnp.int32) + order
    hit = lax.broadcasted_iota(jnp.int32, (nrows, nslots), 1) == slot_of
    onehot_t[...] = hit.astype(F32).astype(BF16)
    perm_back[...] = (col == (row % cy) * chans + row // cy).astype(F32).astype(BF16)

    waits(send, arr, a2a_sem, n - 1).wait_recv()

    arrived = arr[...].reshape(nslots, feats)
    projected = nt_dot(wpt_ref[...], arrived).astype(BF16).astype(F32)
    def edge_copy(side, b):
        to = (lax.rem(gi + b + ngx, ngx), lax.rem(gj + (1 if side == 0 else ngy - 1), ngy))
        row = cy if side == 0 else 1
        dst = 0 if side == 0 else cy + 1
        sem = (side, 1 - b)
        return remote(fld.at[row, 1], fld.at[dst, 1 - b], fy_send.at[sem], fy_recv.at[sem], to)

    def grad_edge(side):
        to = (gi, lax.rem(gj + (1 if side == 0 else ngy - 1), ngy))
        row = cy if side == 0 else 1
        dst = 0 if side == 0 else cy + 1
        return remote(pgr.at[row], pgr.at[dst], gy_send.at[side], gy_recv.at[side], to)

    def plane_copy(c, first, count, b):
        rows = pl.ds(first + 1, count)
        sem = (c, (1 - b) // 2)
        return remote(
            fld.at[rows, 1], fld.at[rows, 1 - b], fx_send.at[sem], fx_recv.at[sem], beside(b)
        )

    f_planes = [
        [plane_copy(c, first, count, b) for b in (-1, 1)]
        for c, (first, count) in enumerate(F_CHUNKS)
    ]
    f_edges = [[edge_copy(side, b) for b in (-1, 0, 1)] for side in (0, 1)]
    g_edges = [grad_edge(side) for side in (0, 1)]

    for c, (first, count) in enumerate(F_CHUNKS):
        rows = slice(first, first + count)
        for y in range(first, first + count):
            paint_a[y] = jnp.where(cell_y == y, projected, 0.0).astype(BF16)
        painted = nt_dot(paint_a[rows].reshape(count * chans, nslots), paint_b[0])
        painted = painted.reshape(count, chans, nz)
        fld[first + 1 : first + count + 1, 1] = (base[rows].astype(F32) + painted).astype(BF16)
        if first == 0:
            for copy in f_edges[1]:
                copy.start()
        if first + count == cy:
            for copy in f_edges[0]:
                copy.start()
        for copy in f_planes[c]:
            copy.start()

    for copy in cell_copies:
        copy.wait()
    near_y = [near_cells[e] // nz for e in (0, 1)]
    for e in (0, 1):
        paint_b[1 + e] = at_depth(near_cells[e])

    def backward_row(y):
        slab = pgr[y : y + 3].reshape(3 * chans, nz)
        part = jnp.dot(wb[...], slab, preferred_element_type=F32)
        for x in range(3):
            p = part[3 * x * chans : 3 * (x + 1) * chans]
            got = roll_z(p[:chans], 1) + p[chans : 2 * chans] + roll_z(p[2 * chans :], -1)
            if x == 1:
                got = got + cot[y].astype(F32)
                high = got.astype(BF16)
                grads[3, y] = (got - high.astype(F32)).astype(BF16)
                grads[1, y] = high
            else:
                grads[x, y] = got.astype(BF16)

    def tap_terms(slabs, threes):
        acc[:, : N_TAPS * chans] = nt_dot(
            jnp.concatenate(threes, axis=1), jnp.concatenate(slabs, axis=1)
        )

    def at_slots(which, depth, ys, total, ranges):
        for first, count in ranges:
            rows = grads[which, first : first + count].reshape(count * chans, nz)
            got = jnp.dot(rows, paint_b[depth], preferred_element_type=F32)
            for y in range(count):
                part = got[y * chans : (y + 1) * chans]
                total = total + jnp.where(ys == first + y, part, 0.0)
        return total

    zero = jnp.zeros((chans, nslots), F32)
    late_slabs, late_threes = [], []
    for c, (first, count) in enumerate(F_ROWS):
        for copy in f_planes[c]:
            copy.wait_recv()
        if c < 2:
            for copy in f_edges[c]:
                copy.wait_recv()
        slabs, threes = [], []
        for y in range(first, first + count):
            slab = fld[y : y + 3].reshape(N_TAPS * chans, nz)
            part = jnp.dot(wf[...], slab, preferred_element_type=F32)
            pre = roll_z(part[:chans], 1) + part[chans : 2 * chans] + roll_z(part[2 * chans :], -1)
            sig = jax.nn.sigmoid(pre)
            outs[y] = (fld[y + 1, 1].astype(F32) + pre * sig).astype(BF16)
            grad = (cot[y].astype(F32) * sig * (1.0 + pre * (1.0 - sig))).astype(BF16)
            pgr[y + 1] = grad
            wide = grad.astype(F32)
            three = jnp.concatenate([roll_z(wide, -1), wide, roll_z(wide, 1)], axis=0)
            slabs.append(slab)
            threes.append(three.astype(BF16))
        if c < 2:
            g_edges[1 - c].start()
        late_slabs += slabs
        late_threes += threes
        if c == 3:
            for copy in g_edges:
                copy.wait_recv()
        for y in G_ROWS[c]:
            backward_row(y)
        if c == 3:
            sums = [at_slots(2 * e, 1 + e, near_y[e], zero, EARLY) for e in (0, 1)]

    near_copies = []
    for e, b in ((0, -1), (1, 1)):
        near_out[e] = at_slots(2 * e, 1 + e, near_y[e], sums[e], LATE).astype(BF16)
        copy = remote(
            near_out.at[e], near_in.at[1 - e], near_sem.at[0, e], near_sem.at[1, 1 - e], beside(b)
        )
        copy.start()
        near_copies.append(copy)

    tap_terms(late_slabs, late_threes)
    per_row = acc.shape[1] // 128
    proj_shares = 8 // per
    stride = n // proj_shares
    proj_at = [stride * m + 5 * (m % 4) for m in range(proj_shares)]
    conv_at = [d for d in range(n) if d not in proj_at]
    for t in range(120):
        r, q = divmod(t, per_row)
        d = conv_at[t // per]
        tiles[d % 2, d // 2, t % per] = acc[8 * r : 8 * r + 8, 128 * q : 128 * q + 128]
    for d in proj_at:
        tiles[d % 2, d // 2] = jnp.zeros((per, 8, 128), F32)
    pair_copy = remote(
        tiles.at[1 - core], pair_in, pair_sem.at[0], pair_sem.at[1], me + 1 - 2 * core
    )
    pair_copy.start()
    slot_grad = at_slots(3, 0, cell_y, zero, EARLY + LATE)
    slot_grad = at_slots(1, 0, cell_y, slot_grad, EARLY + LATE)
    pair_copy.wait()
    tiles[pl.ds(core, 1)] = tiles[pl.ds(core, 1)] + pair_in[...][None]
    for peer, d in peers:
        if d == 0:
            remote(
                tiles.at[core, peer // 2], rs.at[chip], rs_sem.at[0], rs_sem.at[1], peer
            ).start()

    for copy in near_copies:
        copy.wait()
    slot_grad = slot_grad + near_in[0].astype(F32) + near_in[1].astype(F32)

    slot_grad = slot_grad.astype(BF16)
    proj_part = jnp.dot(slot_grad, arrived, preferred_element_type=F32)
    for t in range(8):
        ptiles[t // per, t % per] = proj_part[8 * t : 8 * t + 8]
    group = me // stride
    proj_owner = me % stride == 5 * (group % 4)
    for m, d in enumerate(proj_at):

        @pl.when(me != d)
        def _(m=m, d=d):
            remote(ptiles.at[m], prs.at[me], prs_sem.at[0], prs_sem.at[1], d).start()

    wide = jnp.concatenate([slot_grad.astype(F32), jnp.zeros((feats - chans, nslots), F32)], axis=0)
    sgs[...] = wide.T.astype(BF16).reshape(sgs.shape)
    spread(sgs, sgr, rev_sem)

    waits(rs, rs, rs_sem, half - 1).wait_recv()
    rs[pl.ds(chip, 1)] = tiles[core, pl.ds(chip, 1)]
    ag[core, pl.ds(chip, 1)] = jnp.sum(rs[...], axis=0, keepdims=True)
    there = ag.at[core, chip]
    for peer, d in peers:
        if d == 0:
            remote(there, there, ag_sem.at[0], ag_sem.at[1], peer).start()

    @pl.when(proj_owner)
    def _():
        waits(prs, prs, prs_sem, n - 1).wait_recv()
        prs[pl.ds(me, 1)] = ptiles[pl.ds(group, 1)]
        pag[pl.ds(group, 1)] = jnp.sum(prs[...], axis=0, keepdims=True)
        for peer, _ in peers:
            remote(pag.at[group], pag.at[group], pag_sem.at[0], pag_sem.at[1], peer).start()

    out_ref[...] = jnp.dot(
        perm_back[...], outs[...].reshape(full, nz), preferred_element_type=F32
    ).astype(BF16)

    waits(rs, rs, ag_sem, half - 1).wait_recv()
    share_copy = remote(
        ag.at[core], ag.at[core], share_sem.at[0], share_sem.at[1], me + 1 - 2 * core
    )
    share_copy.start()
    waits(sgs, sgr, rev_sem, n - 1).wait_recv()
    back = sgr[...].reshape(nslots, feats)
    back = jnp.dot(onehot_t[...], back, preferred_element_type=F32)
    rowg_ref[...] = jnp.dot(
        back[:, :chans].astype(BF16), wpt_ref[...], preferred_element_type=F32
    )
    remote(
        ag.at[core], ag.at[1 - core], share_sem.at[0], share_sem.at[1], me + 1 - 2 * core
    ).wait()
    for t in range(120):
        d = conv_at[t // per]
        sums_ref[t // per, t % per] = ag[d % 2, d // 2, t % per]

    @pl.when(proj_owner)
    def _():
        waits(prs, prs, pag_sem, n - 1).wait_send()
        if proj_shares > 1:
            waits(ptiles, ptiles, prs_sem, proj_shares - 1).wait_send()
            waits(ptiles, ptiles, pag_sem, proj_shares - 1).wait_recv()

    @pl.when(jnp.logical_not(proj_owner))
    def _():
        waits(ptiles, ptiles, prs_sem, proj_shares).wait_send()
        waits(ptiles, ptiles, pag_sem, proj_shares).wait_recv()

    for t in range(8):
        psum_ref[8 * t : 8 * t + 8] = pag[t // per, t % per]

    waits(send, arr, a2a_sem, n - 1).wait_send()
    waits(sgs, sgr, rev_sem, n - 1).wait_send()
    waits(rs, rs, rs_sem, half - 1).wait_send()
    waits(rs, rs, ag_sem, half - 1).wait_send()
    for copies in f_edges + f_planes:
        for copy in copies:
            copy.wait_send()
    for copy in g_edges:
        copy.wait_send()


def ending(conv_scale, proj_scale, rows_ref, sums_ref, psum_ref, outf_ref, out_ref, rowg_ref, convg_ref, projg_ref):
    out_ref[...] = outf_ref[...]
    rowg_ref[...] = rows_ref[...]
    per = sums_ref.shape[1]
    chans = convg_ref.shape[1]
    rows = []
    for r in range(3 * chans // 8):
        tiles = [sums_ref[t // per, t % per] for t in range(5 * r, 5 * r + 5)]
        rows.append(jnp.concatenate(tiles, axis=1))
    sums = jnp.concatenate(rows, axis=0) * conv_scale
    for x in range(3):
        for y in range(3):
            for z in range(3):
                at = (y * 3 + x) * chans
                convg_ref[x * 9 + y * 3 + z] = sums[z * chans : (z + 1) * chans, at : at + chans]
    projg_ref[...] = psum_ref[...] * proj_scale


def local(ngx, ngy, particles, send_counts, cell_lists, base_field, proj_weight, conv_weight, cotangent):
    n = ngx * ngy
    nrows, feats = particles.shape
    chans, _, cy, nz = base_field.shape
    nslots = cell_lists.shape[1]
    full = chans * cy
    cap = nslots // n
    per = 128 // n
    weight_t = proj_weight.T
    dma = pltpu.SemaphoreType.DMA
    vmem = pl.BlockSpec(memory_space=pltpu.VMEM)
    plane = (cy, chans, nz)
    out, rows, sums, psum = pl.pallas_call(
        functools.partial(kernel, ngx, ngy),
        out_shape=(
            jax.ShapeDtypeStruct((full, nz), BF16),
            jax.ShapeDtypeStruct((nrows, feats), F32),
            jax.ShapeDtypeStruct((120 // per, per, 8, 128), F32),
            jax.ShapeDtypeStruct((chans, feats), F32),
        ),
        in_specs=[vmem] * 3 + [pl.BlockSpec(memory_space=pl.ANY)] * 3 + [vmem],
        out_specs=[vmem] * 4,
        scratch_shapes=[
            pltpu.VMEM((full, nz), BF16),
            pltpu.VMEM((full, nz), BF16),
            pltpu.VMEM((27, chans, chans), BF16),
            dma((3,)),
            pltpu.VMEM((n, cap, feats), BF16),
            pltpu.VMEM((n, cap, feats), BF16),
            pltpu.VMEM((nrows, nslots), BF16),
            pltpu.VMEM((cy, chans, nslots), BF16),
            pltpu.VMEM((3, nz, nslots), BF16),
            pltpu.VMEM((full, full), BF16),
            pltpu.VMEM((full, full), BF16),
            pltpu.VMEM((3 * chans, N_TAPS * chans), BF16),
            pltpu.VMEM((N_TAPS * chans, 3 * chans), BF16),
            pltpu.VMEM(plane, BF16),
            pltpu.VMEM(plane, BF16),
            pltpu.VMEM(plane, BF16),
            pltpu.VMEM((cy + 2, 3, chans, nz), BF16),
            pltpu.VMEM((cy + 2, chans, nz), BF16),
            pltpu.VMEM((4, cy, chans, nz), BF16),
            pltpu.VMEM((2, 1, nslots), jnp.int32),
            pltpu.VMEM((2, chans, nslots), BF16),
            pltpu.VMEM((2, chans, nslots), BF16),
            pltpu.VMEM((3 * chans, 640), F32),
            pltpu.VMEM((2, n // 2, per, 8, 128), F32),
            pltpu.VMEM((n // 2, per, 8, 128), F32),
            pltpu.VMEM((n // 2, per, 8, 128), F32),
            pltpu.VMEM((2, n // 2, per, 8, 128), F32),
            pltpu.VMEM((8 // per, per, 8, 128), F32),
            pltpu.VMEM((n, per, 8, 128), F32),
            pltpu.VMEM((8 // per, per, 8, 128), F32),
            pltpu.VMEM((n, cap, feats), BF16),
            pltpu.VMEM((n, cap, feats), BF16),
            dma((2,)),
            dma((2,)),
            dma((2, 2)),
            dma((2, 2)),
            dma((2,)),
            dma((2,)),
            dma((2,)),
            dma((2,)),
            dma((2,)),
            dma((2,)),
            dma((5, 2)),
            dma((5, 2)),
            dma((2, 3)),
            dma((2, 3)),
            dma((2,)),
            dma((2,)),
        ],
        compiler_params=pltpu.CompilerParams(
            collective_id=0, has_side_effects=True, vmem_limit_bytes=60 * 1024 * 1024
        ),
        name="section",
    )(
        send_counts,
        cell_lists,
        particles,
        base_field.reshape(full, nz),
        cotangent.reshape(full, nz),
        conv_weight,
        weight_t,
    )
    out_field, row_grads, conv_grad, proj_t = pl.pallas_call(
        functools.partial(ending, 1.0 / math.sqrt(cy * nz * n), 1.0 / math.sqrt(nrows * n)),
        out_shape=(
            jax.ShapeDtypeStruct((full, nz), BF16),
            jax.ShapeDtypeStruct((nrows, feats), F32),
            jax.ShapeDtypeStruct((27, chans, chans), F32),
            jax.ShapeDtypeStruct((chans, feats), F32),
        ),
        in_specs=[vmem] * 4,
        out_specs=[vmem] * 4,
        compiler_params=pltpu.CompilerParams(vmem_limit_bytes=60 * 1024 * 1024),
        name="ending",
    )(rows, sums, psum, out)
    return out_field.reshape(base_field.shape), row_grads, conv_grad, proj_t.T


def solution(mesh):
    in_specs = (
        P(("gx", "gy"), None),
        P(("gx", "gy"), None),
        P(("gx", "gy"), None),
        P(None, "gx", "gy", None),
        P(),
        P(),
        P(None, "gx", "gy", None),
    )
    out_specs = (P(None, "gx", "gy", None), P(("gx", "gy"), None), P(), P())
    body = functools.partial(local, mesh.shape["gx"], mesh.shape["gy"])
    return jax.shard_map(body, mesh=mesh, in_specs=in_specs, out_specs=out_specs, check_vma=False)
```

```python
import functools
import math

import jax
import jax.numpy as jnp
from jax import lax
from jax.experimental import pallas as pl
from jax.experimental.pallas import tpu as pltpu
from jax.sharding import PartitionSpec as P

MESH = pl.DeviceIdType.MESH
FLAT = pl.DeviceIdType.LOGICAL
F32 = jnp.float32
BF16 = jnp.bfloat16

F_CHUNKS = ((0, 4), (12, 4), (4, 3), (7, 3), (10, 2))
F_ROWS = ((0, 3), (13, 3), (3, 3), (6, 3), (9, 4))
G_ROWS = ((), (), (1, 2, 3, 4, 14), (5, 6, 7, 0, 15), (8, 9, 10, 11, 12, 13))
EARLY = ((0, 4), (4, 4), (14, 2))
LATE = ((8, 3), (11, 3))
N_TAPS = 9


def nt_dot(a, b):
    return lax.dot_general(a, b, (((1,), (1,)), ((), ())), preferred_element_type=F32)


def roll_z(x, shift):
    return pltpu.roll(x, shift % x.shape[1], 1)


def kernel(
    ngx,
    ngy,
    counts_ref,
    cells_ref,
    rows_ref,
    base_hbm,
    cot_hbm,
    taps_hbm,
    wpt_ref,
    out_ref,
    rowg_ref,
    sums_ref,
    psum_ref,
    base_ref,
    cot_ref,
    taps_ref,
    load_sem,
    send,
    arr,
    onehot_t,
    paint_a,
    paint_b,
    perm,
    perm_back,
    wf,
    wb,
    base,
    cot,
    outs,
    fld,
    pgr,
    grads,
    near_cells,
    near_out,
    near_in,
    acc,
    tiles,
    pair_in,
    rs,
    ag,
    ptiles,
    prs,
    pag,
    sgs,
    sgr,
    a2a_sem,
    rev_sem,
    cell_sem,
    near_sem,
    pair_sem,
    rs_sem,
    ag_sem,
    prs_sem,
    pag_sem,
    share_sem,
    fx_send,
    fx_recv,
    fy_send,
    fy_recv,
    gy_send,
    gy_recv,
):
    n = ngx * ngy
    nrows, feats = rows_ref.shape
    cy, chans, nz = base.shape
    nslots = cells_ref.shape[1]
    cap = nslots // n
    per = tiles.shape[2]
    half = n // 2
    gi = lax.axis_index("gx")
    gj = lax.axis_index("gy")
    me = gi * ngy + gj

    low = 2 if ngx >= 8 else 1
    dims = (ngx // (4 * low), 4, ngy // 2 * low, 2)
    core = gj % 2
    chip = me // 2
    at = (gi // (4 * low), gi % 4, gj // 2 * low + gi // 4 % low, core)
    moved = [[(at[a] + d) % dims[a] for d in range(dims[a])] for a in range(4)]
    places = [
        [v * (4 * low * ngy) for v in moved[0]],
        [v * ngy for v in moved[1]],
        [v % low * (4 * ngy) + v // low * 2 for v in moved[2]],
        moved[3],
    ]
    steps = [
        (a, b, c, d)
        for a in range(dims[0])
        for b in range(dims[1])
        for c in range(dims[2])
        for d in range(dims[3])
        if (a, b, c, d) != (0, 0, 0, 0)
    ]

    def hops(step):
        return -sum(min(v, size - v) for v, size in zip(step[:3], dims)), -step[3]

    steps.sort(key=hops)
    chips = [
        [places[0][a] + places[1][b] for b in range(dims[1])] for a in range(dims[0])
    ]
    ends = [[places[2][c] + places[3][d] for d in range(2)] for c in range(dims[2])]
    peers = [(chips[a][b] + ends[c][d], d) for a, b, c, d in steps]

    def beside(b):
        return (lax.rem(gi + b + ngx, ngx), gj)

    barrier = pltpu.get_barrier_semaphore()

    for peer, _ in peers:
        pl.semaphore_signal(barrier, inc=1, device_id=peer, device_id_type=FLAT)

    loads = [
        pltpu.make_async_copy(src, dst, load_sem.at[j])
        for j, (src, dst) in enumerate(
            ((base_hbm, base_ref), (taps_hbm, taps_ref), (cot_hbm, cot_ref))
        )
    ]
    for load in loads:
        load.start()

    counts = counts_ref[...].astype(F32)
    lane = lax.broadcasted_iota(jnp.int32, (nslots, n), 1)
    slot = lax.broadcasted_iota(jnp.int32, (nslots, 1), 0)
    owner = slot // cap
    offs = jnp.sum(jnp.where(lane < owner, counts, 0.0), axis=1, keepdims=True)
    mine = jnp.sum(jnp.where(lane == owner, counts, 0.0), axis=1, keepdims=True)
    place = slot - owner * cap
    index = jnp.where(place < mine.astype(jnp.int32), offs.astype(jnp.int32) + place, -1)
    pick = lax.broadcasted_iota(jnp.int32, (nslots, nrows), 1) == index
    outgoing = jnp.dot(pick.astype(F32).astype(BF16), rows_ref[...], preferred_element_type=F32)
    send[...] = outgoing.astype(BF16).reshape(send.shape)

    pl.semaphore_wait(barrier, n - 1)

    def remote(src, dst, send_sem, recv_sem, device):
        return pltpu.make_async_remote_copy(
            src_ref=src,
            dst_ref=dst,
            send_sem=send_sem,
            recv_sem=recv_sem,
            device_id=device,
            device_id_type=MESH if isinstance(device, tuple) else FLAT,
        )

    def spread(src, dst, sems):
        for peer, _ in peers:
            remote(src.at[peer], dst.at[me], sems.at[0], sems.at[1], peer).start()
        dst[pl.ds(me, 1)] = src[pl.ds(me, 1)]

    def waits(src, dst, sems, count):
        part = pl.ds(0, count)
        return remote(src.at[part], dst.at[part], sems.at[0], sems.at[1], peers[0][0])

    spread(send, arr, a2a_sem)
    cell_copies = [
        remote(
            cells_ref,
            near_cells.at[(1 - b) // 2],
            cell_sem.at[0, (1 - b) // 2],
            cell_sem.at[1, (1 - b) // 2],
            beside(b),
        )
        for b in (-1, 1)
    ]
    for copy in cell_copies:
        copy.start()

    def at_depth(cells):
        hit = lax.broadcasted_iota(jnp.int32, (nz, nslots), 0) == cells % nz
        return hit.astype(F32).astype(BF16)

    cell_y = cells_ref[...] // nz
    paint_b[0] = at_depth(cells_ref[...])
    full = cy * chans
    row = lax.broadcasted_iota(jnp.int32, (full, 1), 0)
    col = lax.broadcasted_iota(jnp.int32, (full, full), 1)
    perm[...] = (col == (row % chans) * cy + row // chans).astype(F32).astype(BF16)
    for load in loads:
        load.wait()
    base[...] = (
        jnp.dot(perm[...], base_ref[...], preferred_element_type=F32).astype(BF16).reshape(base.shape)
    )
    cot[...] = (
        jnp.dot(perm[...], cot_ref[...], preferred_element_type=F32).astype(BF16).reshape(cot.shape)
    )
    for x in range(3):
        for y in range(3):
            for z in range(3):
                tap = taps_ref[x * 9 + y * 3 + z]
                at = (y * 3 + x) * chans
                wf[z * chans : (z + 1) * chans, at : at + chans] = tap
                at = (x * 3 + 2 - z) * chans
                side = (2 - y) * chans
                wb[at : at + chans, side : side + chans] = tap.astype(F32).T.astype(BF16)
    acc[...] = jnp.zeros_like(acc)
    upper = lax.broadcasted_iota(jnp.int32, (n, n), 0) <= lax.broadcasted_iota(jnp.int32, (n, n), 1)
    ends_at = jnp.dot(
        jnp.broadcast_to(counts, (8, n)).astype(BF16),
        upper.astype(F32).astype(BF16),
        preferred_element_type=F32,
    )[:1]
    order = lax.broadcasted_iota(jnp.int32, (nrows, 1), 0)
    below = ends_at <= order.astype(F32)
    owner_of = jnp.sum(jnp.where(below, 1.0, 0.0), axis=1, keepdims=True)
    start_of = jnp.max(jnp.where(below, ends_at, 0.0), axis=1, keepdims=True)
    slot_of = (owner_of * cap - start_of).astype(jnp.int32) + order
    hit = lax.broadcasted_iota(jnp.int32, (nrows, nslots), 1) == slot_of
    onehot_t[...] = hit.astype(F32).astype(BF16)
    perm_back[...] = (col == (row % cy) * chans + row // cy).astype(F32).astype(BF16)

    waits(send, arr, a2a_sem, n - 1).wait_recv()

    arrived = arr[...].reshape(nslots, feats)
    projected = nt_dot(wpt_ref[...], arrived).astype(BF16).astype(F32)
    def edge_copy(side, b):
        to = (lax.rem(gi + b + ngx, ngx), lax.rem(gj + (1 if side == 0 else ngy - 1), ngy))
        row = cy if side == 0 else 1
        dst = 0 if side == 0 else cy + 1
        sem = (side, 1 - b)
        return remote(fld.at[row, 1], fld.at[dst, 1 - b], fy_send.at[sem], fy_recv.at[sem], to)

    def grad_edge(side):
        to = (gi, lax.rem(gj + (1 if side == 0 else ngy - 1), ngy))
        row = cy if side == 0 else 1
        dst = 0 if side == 0 else cy + 1
        return remote(pgr.at[row], pgr.at[dst], gy_send.at[side], gy_recv.at[side], to)

    def plane_copy(c, first, count, b):
        rows = pl.ds(first + 1, count)
        sem = (c, (1 - b) // 2)
        return remote(
            fld.at[rows, 1], fld.at[rows, 1 - b], fx_send.at[sem], fx_recv.at[sem], beside(b)
        )

    f_planes = [
        [plane_copy(c, first, count, b) for b in (-1, 1)]
        for c, (first, count) in enumerate(F_CHUNKS)
    ]
    f_edges = [[edge_copy(side, b) for b in (-1, 0, 1)] for side in (0, 1)]
    g_edges = [grad_edge(side) for side in (0, 1)]

    for c, (first, count) in enumerate(F_CHUNKS):
        rows = slice(first, first + count)
        for y in range(first, first + count):
            paint_a[y] = jnp.where(cell_y == y, projected, 0.0).astype(BF16)
        painted = nt_dot(paint_a[rows].reshape(count * chans, nslots), paint_b[0])
        painted = painted.reshape(count, chans, nz)
        fld[first + 1 : first + count + 1, 1] = (base[rows].astype(F32) + painted).astype(BF16)
        if first == 0:
            for copy in f_edges[1]:
                copy.start()
        if first + count == cy:
            for copy in f_edges[0]:
                copy.start()
        for copy in f_planes[c]:
            copy.start()

    for copy in cell_copies:
        copy.wait()
    near_y = [near_cells[e] // nz for e in (0, 1)]
    for e in (0, 1):
        paint_b[1 + e] = at_depth(near_cells[e])

    def backward_row(y):
        slab = pgr[y : y + 3].reshape(3 * chans, nz)
        part = jnp.dot(wb[...], slab, preferred_element_type=F32)
        for x in range(3):
            p = part[3 * x * chans : 3 * (x + 1) * chans]
            got = roll_z(p[:chans], 1) + p[chans : 2 * chans] + roll_z(p[2 * chans :], -1)
            if x == 1:
                got = got + cot[y].astype(F32)
                high = got.astype(BF16)
                grads[3, y] = (got - high.astype(F32)).astype(BF16)
                grads[1, y] = high
            else:
                grads[x, y] = got.astype(BF16)

    def tap_terms(slabs, threes):
        acc[:, : N_TAPS * chans] += nt_dot(
            jnp.concatenate(threes, axis=1), jnp.concatenate(slabs, axis=1)
        )

    def at_slots(which, depth, ys, total, ranges):
        for first, count in ranges:
            rows = grads[which, first : first + count].reshape(count * chans, nz)
            got = jnp.dot(rows, paint_b[depth], preferred_element_type=F32)
            for y in range(count):
                part = got[y * chans : (y + 1) * chans]
                total = total + jnp.where(ys == first + y, part, 0.0)
        return total

    zero = jnp.zeros((chans, nslots), F32)
    late_slabs, late_threes = [], []
    for c, (first, count) in enumerate(F_ROWS):
        for copy in f_planes[c]:
            copy.wait_recv()
        if c < 2:
            for copy in f_edges[c]:
                copy.wait_recv()
        slabs, threes = [], []
        for y in range(first, first + count):
            slab = fld[y : y + 3].reshape(N_TAPS * chans, nz)
            part = jnp.dot(wf[...], slab, preferred_element_type=F32)
            pre = roll_z(part[:chans], 1) + part[chans : 2 * chans] + roll_z(part[2 * chans :], -1)
            sig = jax.nn.sigmoid(pre)
            outs[y] = (fld[y + 1, 1].astype(F32) + pre * sig).astype(BF16)
            grad = (cot[y].astype(F32) * sig * (1.0 + pre * (1.0 - sig))).astype(BF16)
            pgr[y + 1] = grad
            wide = grad.astype(F32)
            three = jnp.concatenate([roll_z(wide, -1), wide, roll_z(wide, 1)], axis=0)
            slabs.append(slab)
            threes.append(three.astype(BF16))
        if c < 2:
            g_edges[1 - c].start()
        if c < 2:
            tap_terms(slabs, threes)
        else:
            late_slabs += slabs
            late_threes += threes
        if c == 3:
            for copy in g_edges:
                copy.wait_recv()
        for y in G_ROWS[c]:
            backward_row(y)
        if c == 3:
            sums = [at_slots(2 * e, 1 + e, near_y[e], zero, EARLY) for e in (0, 1)]

    near_copies = []
    for e, b in ((0, -1), (1, 1)):
        near_out[e] = at_slots(2 * e, 1 + e, near_y[e], sums[e], LATE).astype(BF16)
        copy = remote(
            near_out.at[e], near_in.at[1 - e], near_sem.at[0, e], near_sem.at[1, 1 - e], beside(b)
        )
        copy.start()
        near_copies.append(copy)

    tap_terms(late_slabs, late_threes)
    per_row = acc.shape[1] // 128
    proj_shares = 8 // per
    stride = n // proj_shares
    proj_at = [stride * m + 5 * (m % 4) for m in range(proj_shares)]
    conv_at = [d for d in range(n) if d not in proj_at]
    for t in range(120):
        r, q = divmod(t, per_row)
        d = conv_at[t // per]
        tiles[d % 2, d // 2, t % per] = acc[8 * r : 8 * r + 8, 128 * q : 128 * q + 128]
    for d in proj_at:
        tiles[d % 2, d // 2] = jnp.zeros((per, 8, 128), F32)
    pair_copy = remote(
        tiles.at[1 - core], pair_in, pair_sem.at[0], pair_sem.at[1], me + 1 - 2 * core
    )
    pair_copy.start()
    slot_grad = at_slots(3, 0, cell_y, zero, EARLY + LATE)
    slot_grad = at_slots(1, 0, cell_y, slot_grad, EARLY + LATE)
    pair_copy.wait()
    tiles[pl.ds(core, 1)] = tiles[pl.ds(core, 1)] + pair_in[...][None]
    for peer, d in peers:
        if d == 0:
            remote(
                tiles.at[core, peer // 2], rs.at[chip], rs_sem.at[0], rs_sem.at[1], peer
            ).start()

    for copy in near_copies:
        copy.wait()
    slot_grad = slot_grad + near_in[0].astype(F32) + near_in[1].astype(F32)

    slot_grad = slot_grad.astype(BF16)
    proj_part = jnp.dot(slot_grad, arrived, preferred_element_type=F32)
    for t in range(8):
        ptiles[t // per, t % per] = proj_part[8 * t : 8 * t + 8]
    group = me // stride
    proj_owner = me % stride == 5 * (group % 4)
    for m, d in enumerate(proj_at):

        @pl.when(me != d)
        def _(m=m, d=d):
            remote(ptiles.at[m], prs.at[me], prs_sem.at[0], prs_sem.at[1], d).start()

    wide = jnp.concatenate([slot_grad.astype(F32), jnp.zeros((feats - chans, nslots), F32)], axis=0)
    sgs[...] = wide.T.astype(BF16).reshape(sgs.shape)
    spread(sgs, sgr, rev_sem)

    waits(rs, rs, rs_sem, half - 1).wait_recv()
    rs[pl.ds(chip, 1)] = tiles[core, pl.ds(chip, 1)]
    ag[core, pl.ds(chip, 1)] = jnp.sum(rs[...], axis=0, keepdims=True)
    there = ag.at[core, chip]
    for peer, d in peers:
        if d == 0:
            remote(there, there, ag_sem.at[0], ag_sem.at[1], peer).start()

    @pl.when(proj_owner)
    def _():
        waits(prs, prs, prs_sem, n - 1).wait_recv()
        prs[pl.ds(me, 1)] = ptiles[pl.ds(group, 1)]
        pag[pl.ds(group, 1)] = jnp.sum(prs[...], axis=0, keepdims=True)
        for peer, _ in peers:
            remote(pag.at[group], pag.at[group], pag_sem.at[0], pag_sem.at[1], peer).start()

    out_ref[...] = jnp.dot(
        perm_back[...], outs[...].reshape(full, nz), preferred_element_type=F32
    ).astype(BF16)

    waits(rs, rs, ag_sem, half - 1).wait_recv()
    share_copy = remote(
        ag.at[core], ag.at[core], share_sem.at[0], share_sem.at[1], me + 1 - 2 * core
    )
    share_copy.start()
    waits(sgs, sgr, rev_sem, n - 1).wait_recv()
    back = sgr[...].reshape(nslots, feats)
    back = jnp.dot(onehot_t[...], back, preferred_element_type=F32)
    rowg_ref[...] = jnp.dot(
        back[:, :chans].astype(BF16), wpt_ref[...], preferred_element_type=F32
    )
    remote(
        ag.at[core], ag.at[1 - core], share_sem.at[0], share_sem.at[1], me + 1 - 2 * core
    ).wait()
    for t in range(120):
        d = conv_at[t // per]
        sums_ref[t // per, t % per] = ag[d % 2, d // 2, t % per]

    @pl.when(proj_owner)
    def _():
        waits(prs, prs, pag_sem, n - 1).wait_send()
        if proj_shares > 1:
            waits(ptiles, ptiles, prs_sem, proj_shares - 1).wait_send()
            waits(ptiles, ptiles, pag_sem, proj_shares - 1).wait_recv()

    @pl.when(jnp.logical_not(proj_owner))
    def _():
        waits(ptiles, ptiles, prs_sem, proj_shares).wait_send()
        waits(ptiles, ptiles, pag_sem, proj_shares).wait_recv()

    for t in range(8):
        psum_ref[8 * t : 8 * t + 8] = pag[t // per, t % per]

    waits(send, arr, a2a_sem, n - 1).wait_send()
    waits(sgs, sgr, rev_sem, n - 1).wait_send()
    waits(rs, rs, rs_sem, half - 1).wait_send()
    waits(rs, rs, ag_sem, half - 1).wait_send()
    for copies in f_edges + f_planes:
        for copy in copies:
            copy.wait_send()
    for copy in g_edges:
        copy.wait_send()


def ending(conv_scale, proj_scale, rows_ref, sums_ref, psum_ref, outf_ref, out_ref, rowg_ref, convg_ref, projg_ref):
    out_ref[...] = outf_ref[...]
    rowg_ref[...] = rows_ref[...]
    per = sums_ref.shape[1]
    chans = convg_ref.shape[1]
    rows = []
    for r in range(3 * chans // 8):
        tiles = [sums_ref[t // per, t % per] for t in range(5 * r, 5 * r + 5)]
        rows.append(jnp.concatenate(tiles, axis=1))
    sums = jnp.concatenate(rows, axis=0) * conv_scale
    for x in range(3):
        for y in range(3):
            for z in range(3):
                at = (y * 3 + x) * chans
                convg_ref[x * 9 + y * 3 + z] = sums[z * chans : (z + 1) * chans, at : at + chans]
    projg_ref[...] = psum_ref[...] * proj_scale


def local(ngx, ngy, particles, send_counts, cell_lists, base_field, proj_weight, conv_weight, cotangent):
    n = ngx * ngy
    nrows, feats = particles.shape
    chans, _, cy, nz = base_field.shape
    nslots = cell_lists.shape[1]
    full = chans * cy
    cap = nslots // n
    per = 128 // n
    weight_t = proj_weight.T
    dma = pltpu.SemaphoreType.DMA
    vmem = pl.BlockSpec(memory_space=pltpu.VMEM)
    plane = (cy, chans, nz)
    out, rows, sums, psum = pl.pallas_call(
        functools.partial(kernel, ngx, ngy),
        out_shape=(
            jax.ShapeDtypeStruct((full, nz), BF16),
            jax.ShapeDtypeStruct((nrows, feats), F32),
            jax.ShapeDtypeStruct((120 // per, per, 8, 128), F32),
            jax.ShapeDtypeStruct((chans, feats), F32),
        ),
        in_specs=[vmem] * 3 + [pl.BlockSpec(memory_space=pl.ANY)] * 3 + [vmem],
        out_specs=[vmem] * 4,
        scratch_shapes=[
            pltpu.VMEM((full, nz), BF16),
            pltpu.VMEM((full, nz), BF16),
            pltpu.VMEM((27, chans, chans), BF16),
            dma((3,)),
            pltpu.VMEM((n, cap, feats), BF16),
            pltpu.VMEM((n, cap, feats), BF16),
            pltpu.VMEM((nrows, nslots), BF16),
            pltpu.VMEM((cy, chans, nslots), BF16),
            pltpu.VMEM((3, nz, nslots), BF16),
            pltpu.VMEM((full, full), BF16),
            pltpu.VMEM((full, full), BF16),
            pltpu.VMEM((3 * chans, N_TAPS * chans), BF16),
            pltpu.VMEM((N_TAPS * chans, 3 * chans), BF16),
            pltpu.VMEM(plane, BF16),
            pltpu.VMEM(plane, BF16),
            pltpu.VMEM(plane, BF16),
            pltpu.VMEM((cy + 2, 3, chans, nz), BF16),
            pltpu.VMEM((cy + 2, chans, nz), BF16),
            pltpu.VMEM((4, cy, chans, nz), BF16),
            pltpu.VMEM((2, 1, nslots), jnp.int32),
            pltpu.VMEM((2, chans, nslots), BF16),
            pltpu.VMEM((2, chans, nslots), BF16),
            pltpu.VMEM((3 * chans, 640), F32),
            pltpu.VMEM((2, n // 2, per, 8, 128), F32),
            pltpu.VMEM((n // 2, per, 8, 128), F32),
            pltpu.VMEM((n // 2, per, 8, 128), F32),
            pltpu.VMEM((2, n // 2, per, 8, 128), F32),
            pltpu.VMEM((8 // per, per, 8, 128), F32),
            pltpu.VMEM((n, per, 8, 128), F32),
            pltpu.VMEM((8 // per, per, 8, 128), F32),
            pltpu.VMEM((n, cap, feats), BF16),
            pltpu.VMEM((n, cap, feats), BF16),
            dma((2,)),
            dma((2,)),
            dma((2, 2)),
            dma((2, 2)),
            dma((2,)),
            dma((2,)),
            dma((2,)),
            dma((2,)),
            dma((2,)),
            dma((2,)),
            dma((5, 2)),
            dma((5, 2)),
            dma((2, 3)),
            dma((2, 3)),
            dma((2,)),
            dma((2,)),
        ],
        compiler_params=pltpu.CompilerParams(
            collective_id=0, has_side_effects=True, vmem_limit_bytes=60 * 1024 * 1024
        ),
        name="section",
    )(
        send_counts,
        cell_lists,
        particles,
        base_field.reshape(full, nz),
        cotangent.reshape(full, nz),
        conv_weight,
        weight_t,
    )
    out_field, row_grads, conv_grad, proj_t = pl.pallas_call(
        functools.partial(ending, 1.0 / math.sqrt(cy * nz * n), 1.0 / math.sqrt(nrows * n)),
        out_shape=(
            jax.ShapeDtypeStruct((full, nz), BF16),
            jax.ShapeDtypeStruct((nrows, feats), F32),
            jax.ShapeDtypeStruct((27, chans, chans), F32),
            jax.ShapeDtypeStruct((chans, feats), F32),
        ),
        in_specs=[vmem] * 4,
        out_specs=[vmem] * 4,
        compiler_params=pltpu.CompilerParams(vmem_limit_bytes=60 * 1024 * 1024),
        name="ending",
    )(rows, sums, psum, out)
    return out_field.reshape(base_field.shape), row_grads, conv_grad, proj_t.T


def solution(mesh):
    in_specs = (
        P(("gx", "gy"), None),
        P(("gx", "gy"), None),
        P(("gx", "gy"), None),
        P(None, "gx", "gy", None),
        P(),
        P(),
        P(None, "gx", "gy", None),
    )
    out_specs = (P(None, "gx", "gy", None), P(("gx", "gy"), None), P(), P())
    body = functools.partial(local, mesh.shape["gx"], mesh.shape["gy"])
    return jax.shard_map(body, mesh=mesh, in_specs=in_specs, out_specs=out_specs, check_vma=False)
```
